128 devices in a mesh: tower: 8 (over y, x_lo), member: 16 (over z, x_hi, core).
Axes of the slice: x: 4 (x_hi: 2, x_lo: 2; x = x_hi * 2 + x_lo), y: 4, z: 4, core: 2. Of those that a mesh axis runs over, the one named last changes fastest.
Arguments:
- bag_ids: int32 [16, 16, 4, 2048], P('tower', 'member'), may hold values from 0 to 511
- touch_ids: int32 [16, 16, 128], P('tower', 'member'), may hold values from 0 to 511, as said below
- elapsed: int32 [16, 16, 128], P('tower', 'member'), may hold values from 0 to 39
- tables: float32 [16, 16, 512, 64], P('tower', 'member'), may hold values from -3 to 3
- accumulator: float32 [16, 16, 512], P('tower', 'member'), may hold values from 0.001 to 0.1
- first_weight: float32 [1024, 16, 1024], P(None, 'tower'), may hold values from -0.1875 to 0.1875
- second_weight: float32 [1024, 16, 256], P(None, 'tower'), may hold values from -0.1875 to 0.1875
- lift_weight: float32 [4096, 128], replicated, may hold values from -0.5 to 0.5
- press_weight: float32 [4096, 128], replicated, may hold values from -0.09375 to 0.09375
- head_weight: float32 [4096], replicated, may hold values from -0.09375 to 0.09375
- labels: int32 [16, 128], P('member'), may hold values 0 or 1
Outputs:
- new_tables: float32 [16, 16, 512, 64], P('tower', 'member')
- new_accumulator: float32 [16, 16, 512], P('tower', 'member')
- grad_first: float32 [1024, 16, 1024], P('member', 'tower')
- grad_second: float32 [1024, 16, 256], P('member', 'tower')
- grad_lift: float32 [4096, 128], P(('tower', 'member'))
- grad_press: float32 [4096, 128], P(('tower', 'member'))
- logits: float32 [16, 128], P('member', 'tower')
The draws below stay inside these ranges and needn't reach their ends.
Inputs may be any that keep to these rules, and one draw needn't show every extreme that they name: `touch_ids`: distinct within each table.
All inputs are finite; a program needn't handle non-finite values. No bound on the sum of `labels` on one device may be relied on, other than what follows from the above.
Results may differ from the reference program's by a relative error of at most 0.0003.
Values sent between devices are 32-bit elements; how exact they have to be, the bound alone decides.
No kernel may reach another device: no remote copies, remote signals or barrier semaphores. Data moves between devices by JAX's collectives and lax.ppermute only.
A program may use at most 128 MiB of HBM per device.

```python
import math
import jax
import jax.numpy as jnp
import numpy as np
from jax import lax

W = 64
HID = 1024
TOUT = 256
RANK = 128
BAG = 4
ROWS = 512
TOUCH = 128
TOWERS = 16
TTAB = 16
FIN = 1024
CROSS = 4096
SAMP = 128
SAMPLES = 2048
N_MEMBER = 16


def draw_touch_ids(key, part):
    keys = jax.random.split(jax.random.fold_in(key, 7), TOWERS * TTAB)

    def one_table(table_key):
        perm_key, shift_key = jax.random.split(table_key)
        others = (jax.random.permutation(perm_key, ROWS - 2)[:TOUCH - 2] + 1).astype(jnp.int32)
        listed = jnp.concatenate([jnp.full((1,), ROWS - 1, jnp.int32), jnp.zeros((1,), jnp.int32), others])
        shift = jax.random.randint(shift_key, (), 0, TOUCH)
        return jnp.roll(listed, shift)
    return jax.vmap(one_table)(keys).reshape(TOWERS, TTAB, TOUCH).astype(jnp.int32)


def place_ends(values, own_key, least, top_value):
    spot = [jax.random.randint(jax.random.fold_in(own_key, axis), (), 0, length) for axis, length in enumerate(values.shape)]
    longest = values.shape.index(max(values.shape))
    neighbour = spot[:longest] + [(spot[longest] + 1) % values.shape[longest]] + spot[longest + 1:]
    return values.at[tuple(spot)].set(least).at[tuple(neighbour)].set(top_value)


def level_of(key, extent, pieces, smallest, top_value):
    level = 1.0
    for dim, blocks in pieces:
        draws = jax.random.uniform(jax.random.fold_in(jax.random.fold_in(key, 6), dim), (blocks,), jnp.float32, smallest / len(pieces), top_value / len(pieces))
        level = level * jnp.repeat(jnp.exp(draws), extent[dim] // blocks).reshape((-1,) + (1,) * (len(extent) - 1 - dim))
    return level


def cumulative_ranks(count, slope):
    loads = [(1 << 20) // math.isqrt(standing ** slope) + 1 for standing in range(1, count + 1)]
    width = 1 + sum(loads) // (1 << 30)
    return np.cumsum(np.array([max(1, weight // width) for weight in loads]))


def ranked_ids(stream_key, shape, number_of, lean):
    table = cumulative_ranks(number_of, lean)
    pick = jax.random.randint(jax.random.fold_in(stream_key, 1), shape, 0, int(table[number_of - 1]))
    grade = jnp.searchsorted(jnp.asarray(table, jnp.int32), pick, side="right")
    return jax.random.permutation(jax.random.fold_in(stream_key, 2), number_of)[grade].astype(jnp.int32)


def normal_values(key, dims, deviation, most, cuts=(), kind=jnp.bfloat16):
    array = jax.random.normal(key, dims, jnp.float32) * deviation
    if len(cuts) > 0:
        array = level_of(key, dims, cuts, -0.22, 0.18) * array
    return jnp.clip(array, min=-most, max=most).astype(kind)


def setup_inputs(seed: int = 0) -> dict:
    key_of = jax.random.split(jax.random.key(seed), 12)
    bag_ids = place_ends(ranked_ids(key_of[0], (TOWERS, TTAB, BAG, SAMPLES), ROWS, 2), jax.random.fold_in(key_of[0], 3), 0, ROWS - 1).astype(jnp.int32)
    touch_ids = draw_touch_ids(jax.random.fold_in(key_of[11], 71), 0)
    elapsed = place_ends(jax.random.randint(key_of[2], (TOWERS, TTAB, TOUCH), 0, 40), jax.random.fold_in(key_of[2], 1), 0, 39).astype(jnp.int32)
    tables = normal_values(key_of[3], (TOWERS, TTAB, ROWS, W), 0.5, 3.0, ((0, 8), (1, 16)), jnp.float32)
    accumulator = jnp.clip(jnp.exp(math.log(0.1) - 4.6051702 * jax.random.uniform(key_of[4], (TOWERS, TTAB, ROWS), jnp.float32) ** level_of(key_of[4], (TOWERS, TTAB, ROWS), ((0, 8), (1, 16)), -0.2, 0.2)), 0.001, 0.1)
    first_weight = normal_values(key_of[5], (FIN, TOWERS, HID), FIN ** -0.5, 0.1875, ((1, 8),), jnp.float32)
    second_weight = normal_values(key_of[6], (HID, TOWERS, TOUT), HID ** -0.5, 0.1875, ((1, 8),), jnp.float32)
    lift_weight = normal_values(key_of[7], (CROSS, RANK), RANK ** -0.5, 0.5, (), jnp.float32)
    press_weight = normal_values(key_of[8], (CROSS, RANK), CROSS ** -0.5, 0.09375, (), jnp.float32)
    head_weight = normal_values(key_of[9], (CROSS,), CROSS ** -0.5, 0.09375, (), jnp.float32)
    labels = place_ends((jax.random.randint(key_of[10], (N_MEMBER, SAMP), 0, 2) < 1).astype(jnp.int32), jax.random.fold_in(key_of[10], 1), 0, 1)
    return dict(bag_ids=bag_ids, touch_ids=touch_ids, elapsed=elapsed, tables=tables, accumulator=accumulator, first_weight=first_weight, second_weight=second_weight, lift_weight=lift_weight, press_weight=press_weight, head_weight=head_weight, labels=labels)


PRECISE = lax.Precision.HIGHEST
DECAY_RATE = 0.98
LEARN_RATE = 1.0
EPSILON = 1e-08

def decay_factors(touch_ids, elapsed, table_rows):
    rates = jnp.exp(elapsed.astype(jnp.float32) * math.log(DECAY_RATE))
    matches = touch_ids[..., None] == jnp.arange(table_rows, dtype=jnp.int32)
    hits = lax.optimization_barrier(jnp.sum(matches.astype(jnp.float32), axis=-2))
    chosen = lax.optimization_barrier(jnp.sum(jnp.where(matches, rates[..., None], jnp.float32(0.0)), axis=-2))
    return jnp.where(hits > 0.0, chosen, jnp.float32(1.0))

def pool_table(decayed_table, bag_table):
    return lax.optimization_barrier(jnp.sum(decayed_table[bag_table], axis=0))

def reference(bag_ids, touch_ids, elapsed, tables, accumulator, first_weight, second_weight, lift_weight, press_weight, head_weight, labels):
    factors = lax.map(lambda inputs: decay_factors(inputs[0], inputs[1], ROWS), (touch_ids, elapsed))
    decayed = tables * factors[..., None]

    def forward(decayed_tables, weight_one, weight_two, lift, press):
        pooled = lax.map(lambda inputs: jax.vmap(pool_table)(inputs[0], inputs[1]), (decayed_tables, bag_ids))
        features = jnp.transpose(pooled, (2, 0, 1, 3)).reshape(SAMPLES, TOWERS, FIN)
        hidden = jnp.einsum('sti,ith->sth', features, weight_one, precision=PRECISE)
        tower_out = jnp.einsum('sth,hto->sto', jax.nn.silu(hidden), weight_two, precision=PRECISE)
        start_rows = tower_out.reshape(SAMPLES, CROSS)
        projected = jnp.dot(start_rows, press, precision=PRECISE)
        scaling = jnp.dot(projected, lift.T, precision=PRECISE)
        crossed = start_rows * scaling + start_rows
        return jnp.dot(crossed, head_weight, precision=PRECISE)
    logit_values, pullback = jax.vjp(forward, decayed, first_weight, second_weight, lift_weight, press_weight)
    errors = jax.nn.sigmoid(logit_values) - labels.reshape(SAMPLES).astype(jnp.float32)
    grad_tables, grad_one, grad_two, grad_lift, grad_press = pullback(errors)
    mean_square = lax.optimization_barrier(jnp.mean(grad_tables * grad_tables, axis=-1))
    new_accumulator = accumulator + mean_square
    new_tables = decayed - LEARN_RATE * grad_tables / (jnp.sqrt(new_accumulator)[..., None] + EPSILON)
    return (new_tables, new_accumulator, grad_one, grad_two, grad_lift, grad_press, logit_values.reshape(N_MEMBER, SAMP))
```

```python
import math

import jax
import jax.numpy as jnp
from jax import lax
from jax.experimental import pallas as pl
from jax.experimental.pallas import tpu as pltpu
from jax.sharding import Mesh, PartitionSpec as P

DECAY_RATE = 0.98
LEARN_RATE = 1.0
EPSILON = 1e-08
F32 = jnp.float32
BF16 = jnp.bfloat16
NN = (((1,), (0,)), ((), ()))
NT = (((1,), (1,)), ((), ()))
TOWER = ("y", "xl")
QUAD = ("xh", "core")
VMEM_LIMIT = 50 << 20


def halves(a):
    high = a.astype(BF16)
    return high, (a - high.astype(F32)).astype(BF16)


def dot1(a, b, dims):
    return lax.dot_general(a, b, dims, preferred_element_type=F32)


def dot3(a, b, dims=NN):
    return dot1(a[0], b[0], dims) + (dot1(a[0], b[1], dims) + dot1(a[1], b[0], dims))


def dot32(a, b, dims=NN):
    return dot3(halves(a), halves(b), dims)


def vmem(count):
    return [pl.BlockSpec(memory_space=pltpu.VMEM)] * count


def call(kernel, outs, spec_in, scratch=(), name=None):
    return pl.pallas_call(
        kernel,
        out_shape=outs,
        in_specs=spec_in,
        out_specs=vmem(len(outs)),
        scratch_shapes=list(scratch),
        compiler_params=pltpu.CompilerParams(vmem_limit_bytes=VMEM_LIMIT),
        name=name,
    )


SMEM_SPEC = pl.BlockSpec(memory_space=pltpu.SMEM)


def pool_kernel(bag, touch, elapsed, tables, pooled, decayed, counts):
    towers, width, rows = tables.shape
    touches = touch.shape[1]
    samples = bag.shape[2]
    chunk = samples // pooled.shape[0]
    for t in range(towers):
        ids = jnp.broadcast_to(touch[t : t + 1, :].astype(F32), (touches, touches)).T
        rates = jnp.exp(elapsed[t : t + 1, :].astype(F32) * math.log(DECAY_RATE))
        rates = jnp.broadcast_to(rates, (touches, touches)).T
        factor = []
        for block in range(rows // touches):
            row = lax.broadcasted_iota(jnp.int32, (touches, touches), 1).astype(F32) + float(block * touches)
            match = ids == row
            hits = jnp.sum(jnp.where(match, 1.0, 0.0), axis=0, keepdims=True)
            chosen = jnp.sum(jnp.where(match, rates, 0.0), axis=0, keepdims=True)
            factor.append(jnp.where(hits > 0.0, chosen, 1.0))
        table = tables[t] * jnp.concatenate(factor, axis=1)
        decayed[t] = table
        high, low = halves(table)
        both = jnp.concatenate([high, low], axis=0)
        step = 256

        def block_of(k, carry, t=t, both=both):
            at = pl.multiple_of(k * step, step)
            ids = bag[t, :, pl.ds(at, step)]
            row = lax.broadcasted_iota(jnp.int32, (rows, step), 0)
            count = jnp.zeros((rows, step), F32)
            for b in range(ids.shape[0]):
                count = count + jnp.where(row == ids[b : b + 1, :], 1.0, 0.0)
            count = count.astype(BF16)
            counts[t, :, pl.ds(at, step)] = count
            total = dot1(both, count, NN)
            total = total[:width] + total[width:]
            pooled[k // (chunk // step), t * width : (t + 1) * width, pl.ds(pl.multiple_of((k % (chunk // step)) * step, step), step)] = total
            return carry

        lax.fori_loop(0, samples // step, block_of, 0)


def forward_kernel(pay_rows, idx, x1, x2, y1, y2, w1h, w1l, w2h, w2l, press, lift, head, hidden, start, *rest):
    pay = rest[0] if pay_rows else None
    fh, fl = rest[-2:]
    sets = (x1, x2, y1, y2)
    zs, pair, samples = x1.shape
    width = pair // 2
    xh, core = idx[1], idx[2]
    hid = w1h.shape[-1]
    place = ((xh, core), (1 - xh, core), (xh, 1 - core), (1 - xh, 1 - core))
    depth = zs * width
    for t in range(2):
        for k, ref in enumerate(sets):
            block = jnp.concatenate([ref[z, t * width : (t + 1) * width, :] for z in range(zs)], axis=0)
            h, l = halves(block.T)
            fh[:, k * depth : (k + 1) * depth] = h
            fl[:, k * depth : (k + 1) * depth] = l

        def column(n, out, t=t):
            at = pl.multiple_of(n * 256, 256)
            wh, wl = [], []
            for k in range(4):
                for z in range(zs):
                    table = (z * 2 + place[k][0]) * 2 + place[k][1]
                    wh.append(w1h[t, table, :, pl.ds(at, 256)])
                    wl.append(w1l[t, table, :, pl.ds(at, 256)])
            wh = jnp.concatenate(wh, axis=0)
            wl = jnp.concatenate(wl, axis=0)
            value = dot3((fh[...], fl[...]), (wh, wl))
            hidden[t, :, pl.ds(at, 256)] = value
            act = halves(value * jax.nn.sigmoid(value))
            return out + dot3(act, (w2h[t, pl.ds(at, 256), :], w2l[t, pl.ds(at, 256), :]))

        width_out = w2h.shape[-1]
        out = lax.fori_loop(0, hid // 256, column, jnp.zeros((samples, width_out), F32))
        start[:, t * width_out : (t + 1) * width_out] = out
    if pay_rows:
        own = samples // 2
        x0 = start[pl.ds(pl.multiple_of(core * own, own), own), :]
        rank = press.shape[1]
        weighted = x0 * head[...]
        pay[0:rank, :] = dot32(x0, press[...]).T
        pay[rank : 2 * rank, :] = dot32(weighted, lift[...]).T
        direct = jnp.sum(weighted, axis=1, keepdims=True)
        pay[2 * rank : 2 * rank + 8, :] = jnp.broadcast_to(direct, (own, 128)).T[0:8, :]


def logit_kernel(mine, other, labels, pay, logits):
    total = mine[...] + other[...]
    rank = (total.shape[0] - 8) // 2
    value = jnp.sum(total[0:rank] * total[rank : 2 * rank], axis=0, keepdims=True) + total[2 * rank : 2 * rank + 1]
    logits[...] = value
    error = jax.nn.sigmoid(value) - labels[...].astype(F32)
    pay[0 : 2 * rank, :] = total[0 : 2 * rank]
    pay[2 * rank : 2 * rank + 8, :] = jnp.broadcast_to(error, (8, error.shape[1]))


def grads_kernel(idx, own, c1, xa, xb, hid_a, hid_b, w1h, w1l, w2h, w2l, press, lift, head, ghh, ghl, gout, pq, g0, g1, g2, g3, ps, qs, es):
    z, xh, core = idx[0], idx[1], idx[2]
    rank = press.shape[1]
    n = own.shape[1]
    half = 2 * n
    for base, ref, here in ((0, own, core), (0, c1, 1 - core), (half, xa, core), (half, xb, 1 - core)):
        at = pl.multiple_of(base + here * n, n)
        error = jnp.broadcast_to(ref[2 * rank : 2 * rank + 1, :], (n, n)).T
        p, q = ref[0:rank, :].T, ref[rank : 2 * rank, :].T
        ps[pl.ds(at, n), :] = p
        qs[pl.ds(at, n), :] = q
        es[pl.ds(at, n), :] = error
        pq[pl.ds(at, n), 0:rank] = error * p
        pq[pl.ds(at, n), rank : 2 * rank] = error * q
    width_out = w2h.shape[-1]
    hid = w1h.shape[-1]
    outs = (g0, g1, g2, g3)
    for g, hidden in enumerate((hid_a, hid_b)):
        rows = slice(g * half, (g + 1) * half)
        scaling = dot32(ps[rows, :], lift[...], NT)
        back = dot32(qs[rows, :], press[...], NT)
        go = es[rows, 0:1] * (head[...] * (scaling + 1.0) + back)
        gout[rows, :] = go
        for t in range(2):
            got = halves(go[:, t * width_out : (t + 1) * width_out])

            def column(k, carry, t=t, got=got, hidden=hidden, rows=rows):
                at = pl.multiple_of(k * 256, 256)
                ga = dot3(got, (w2h[t, pl.ds(at, 256), :], w2l[t, pl.ds(at, 256), :]), NT)
                value = hidden[t, :, pl.ds(at, 256)]
                s = jax.nn.sigmoid(value)
                h, l = halves(ga * (s * (1.0 + value * (1.0 - s))))
                ghh[t, rows, pl.ds(at, 256)] = h
                ghl[t, rows, pl.ds(at, 256)] = l
                return carry

            lax.fori_loop(0, hid // 256, column, 0)
    for t in range(2):
        wh, wl = [], []
        for k in range(4):
            table = (lax.rem(z + k, 4) * 2 + xh) * 2 + core
            wh.append(w1h[t, table])
            wl.append(w1l[t, table])
        w = (jnp.concatenate(wh, axis=0), jnp.concatenate(wl, axis=0))
        width = w1h.shape[2]
        for g in range(2):
            rows = slice(g * half, (g + 1) * half)
            grad = dot3(w, (ghh[t, rows, :], ghl[t, rows, :]), NT)
            lane = pl.multiple_of((xh if g == 0 else 1 - xh) * half, half)
            for k in range(4):
                outs[k][t * width : (t + 1) * width, pl.ds(lane, half)] = grad[k * width : (k + 1) * width]


def weights_kernel(idx, fq, ghh, ghl, gout, pq, hid_a, hid_b, x0a, x0b, head, w0, w1, w2, w3, act_t, cross):
    z, xh, core = idx[0], idx[1], idx[2]
    outs = (w0, w1, w2, w3)
    width = fq.shape[1] // 2
    half = hid_a.shape[1]
    quad = 2 * xh + core
    mine = pl.multiple_of(xh * half, half)
    theirs = pl.multiple_of((1 - xh) * half, half)
    width_out = gout.shape[1] // 2
    for t in range(2):
        f = []
        for k in range(4):
            at = lax.rem(z + k, 4)
            f.append(
                jnp.concatenate(
                    [
                        fq[at, t * width : (t + 1) * width, pl.ds(mine, half)],
                        fq[at, t * width : (t + 1) * width, pl.ds(theirs, half)],
                    ],
                    axis=1,
                )
            )
        f = halves(jnp.concatenate(f, axis=0))

        def column(n, carry, t=t, f=f):
            at = pl.multiple_of(n * 256, 256)
            grad = dot3(f, (ghh[t, :, pl.ds(at, 256)], ghl[t, :, pl.ds(at, 256)]))
            for k in range(4):
                outs[k][t * width : (t + 1) * width, pl.ds(at, 256)] = grad[k * width : (k + 1) * width]
            return carry

        lax.fori_loop(0, ghh.shape[-1] // 256, column, 0)
        picked = []
        for k in range(4):
            at = pl.multiple_of(lax.rem(z + k, 4) * 256, 256)
            for g, hidden in enumerate((hid_a, hid_b)):
                value = hidden[t, :, pl.ds(at, 256)]
                act_t[:, g * half : (g + 1) * half] = (value * jax.nn.sigmoid(value)).T
            picked.append(act_t[pl.ds(pl.multiple_of(quad * width, width), width), :])
        act = jnp.concatenate(picked, axis=0)
        grad = dot32(act, gout[:, t * width_out : (t + 1) * width_out])
        base = 2 * width + 16 * t
        for k in range(4):
            for b in range(4):
                outs[k][base : base + 16, b * 256 : (b + 1) * 256] = grad[k * width + 16 * b : k * width + 16 * b + 16]
    rank = pq.shape[1] // 2
    for t in range(2):
        lanes = slice(t * width_out, (t + 1) * width_out)
        x0 = jnp.concatenate([x0a[:, lanes], x0b[:, lanes]], axis=0)
        cross[lanes, 0:rank] = dot32((x0 * head[:, lanes]).T, pq[:, 0:rank])
        cross[lanes, rank : 2 * rank] = dot32(x0.T, pq[:, rank : 2 * rank])
    base = 2 * width + 32
    for k in range(4):
        block = cross[pl.ds(pl.multiple_of((lax.rem(z + k, 4) * 4 + quad) * 32, 32), 32), :]
        for b in range(4):
            outs[k][base : base + 8, b * 256 : (b + 1) * 256] = block[8 * b : 8 * b + 8]


def update_kernel(idx, p0, p1, p2, p3, counts, decayed, accumulator, new_tables, new_accumulator):
    z = idx[0]
    towers, width, rows = decayed.shape
    chunk = p0.shape[1]
    for t in range(towers):
        total = jnp.zeros((2 * width, rows), F32)
        for k, ref in enumerate((p0, p1, p2, p3)):
            at = pl.multiple_of(lax.rem(z + 4 - k, 4) * chunk, chunk)
            high, low = halves(ref[t * width : (t + 1) * width, :])
            total = total + dot1(jnp.concatenate([high, low], axis=0), counts[t, :, pl.ds(at, chunk)], NT)
        grad = total[:width] + total[width:]
        square = jnp.sum(grad * grad, axis=0, keepdims=True) * (1.0 / width)
        fresh = accumulator[t : t + 1, :] + square
        new_accumulator[t : t + 1, :] = fresh
        new_tables[t] = decayed[t] - LEARN_RATE * grad / (jnp.sqrt(fresh) + EPSILON)


def shift(x, axis, size, by):
    return lax.ppermute(x, axis, [(i, (i + by) % size) for i in range(size)])


def flip(x, axis, size, bit):
    return lax.ppermute(x, axis, [(i, i ^ bit) for i in range(size)])


def split_weight(w):
    high = lax.reduce_precision(w, 8, 7)
    return high.astype(BF16), (w - high).astype(BF16)


def per_device(bag_ids, touch_ids, elapsed, tables, accumulator, first_weight, second_weight, lift_weight, press_weight, head_weight, labels):
    f32 = lambda *shape: jax.ShapeDtypeStruct(shape, F32)
    bf16 = lambda *shape: jax.ShapeDtypeStruct(shape, BF16)
    z, xh, core = lax.axis_index("z"), lax.axis_index("xh"), lax.axis_index("core")
    idx = jnp.stack([z, xh, core]).astype(jnp.int32)
    tower = lax.axis_index(TOWER)
    rank = lift_weight.shape[1]
    local = lift_weight.shape[0] // 8
    lift = lax.dynamic_slice_in_dim(lift_weight, tower * local, local, 0)
    press = lax.dynamic_slice_in_dim(press_weight, tower * local, local, 0)
    head = lax.dynamic_slice_in_dim(head_weight, tower * local, local, 0)[None, :]

    tables_t = jnp.transpose(tables[:, 0], (0, 2, 1))
    pooled, decayed, counts = call(
        pool_kernel, [f32(4, 128, 512), f32(2, 64, 512), bf16(2, 512, 2048)], vmem(4), name="pool"
    )(bag_ids[:, 0], touch_ids[:, 0], elapsed[:, 0], tables_t)

    fq = lax.all_to_all(pooled, "z", 0, 0, tiled=True)
    x1 = lax.dynamic_slice_in_dim(fq, xh * 256, 256, 2)
    x1b = lax.dynamic_slice_in_dim(fq, (1 - xh) * 256, 256, 2)
    x2 = shift(x1b, "xh", 2, 1)
    y1 = shift(x1, "core", 2, 1)
    y1b = shift(x1b, "core", 2, 1)
    w1h, w1l = split_weight(jnp.transpose(first_weight, (1, 0, 2)).reshape(2, 16, 64, 1024))
    w2h, w2l = split_weight(jnp.transpose(second_weight, (1, 0, 2)))
    y2 = shift(x2, "core", 2, 1)
    x1_late, x2 = lax.optimization_barrier((x1, x2))
    x2b = shift(x1_late, "xh", 2, 1)
    y2b = shift(x2b, "core", 2, 1)

    scratch = [pltpu.VMEM((256, 1024), BF16)] * 2
    weights = (w1h, w1l, w2h, w2l, press, lift, head)
    hid_a, x0a, pay = call(
        lambda *refs: forward_kernel(True, *refs),
        [f32(2, 256, 1024), f32(256, 512), f32(2 * rank + 8, 128)],
        [SMEM_SPEC] + vmem(11),
        scratch,
        name="forward_a",
    )(idx, x1, x2, y1, y2, *weights)
    hid_b, x0b = call(
        lambda *refs: forward_kernel(False, *refs),
        [f32(2, 256, 1024), f32(256, 512)],
        [SMEM_SPEC] + vmem(11),
        scratch,
        name="forward_b",
    )(idx, x1b, x2b, y1b, y2b, *weights)

    pay = pay + flip(pay, TOWER, 8, 1)
    pay = pay + flip(pay, TOWER, 8, 2)
    pay, logits = call(logit_kernel, [f32(2 * rank + 8, 128), f32(1, 128)], vmem(3), name="logit")(
        pay, flip(pay, TOWER, 8, 4), labels
    )
    logits = lax.dynamic_slice_in_dim(logits, tower * 16, 16, 1)
    pays = [pay] + [flip(pay, QUAD, 4, k) for k in (1, 2, 3)]

    ghh, ghl, gout, pq, *g = call(
        grads_kernel,
        [bf16(2, 512, 1024), bf16(2, 512, 1024), f32(512, 512), f32(512, 2 * rank)] + [f32(128, 512)] * 4,
        [SMEM_SPEC] + vmem(13),
        [pltpu.VMEM((512, rank), F32)] * 3,
        name="grads",
    )(idx, *pays, hid_a, hid_b, *weights)
    got = [g[0]] + [shift(g[k], "z", 4, k) for k in (1, 2, 3)]
    w = call(
        weights_kernel,
        [f32(168, 1024)] * 4,
        [SMEM_SPEC] + vmem(10),
        [pltpu.VMEM((256, 512), F32), pltpu.VMEM((512, 2 * rank), F32)],
        name="weights",
    )(idx, fq, ghh, ghl, gout, pq, hid_a, hid_b, x0a, x0b, head)
    sent = [shift(w[k], "z", 4, k) for k in (1, 2, 3)]
    new_tables, new_accumulator = call(
        update_kernel, [f32(2, 64, 512), f32(2, 512)], [SMEM_SPEC] + vmem(7), name="update"
    )(idx, *got, counts, decayed, accumulator[:, 0])
    total = (w[0] + sent[0]) + (sent[1] + sent[2])
    grad_first = jnp.transpose(total[:128].reshape(2, 64, 1024), (1, 0, 2))
    grad_second = jnp.transpose(total[128:160].reshape(2, 16, 4, 256), (2, 1, 0, 3)).reshape(64, 2, 256)
    cross = jnp.transpose(total[160:168].reshape(8, 4, 256), (1, 0, 2)).reshape(32, 256)
    return (
        jnp.transpose(new_tables, (0, 2, 1))[:, None],
        new_accumulator[:, None],
        grad_first,
        grad_second,
        cross[:, :rank],
        cross[:, rank:],
        logits,
    )


def solution(mesh):
    split = Mesh(mesh.devices.reshape(4, 2, 4, 2, 2), ("y", "xl", "z", "xh", "core"))
    member = ("z", "xh", "core")
    placed = (
        P(TOWER, member, None, None),
        P(TOWER, member, None),
        P(TOWER, member, None),
        P(TOWER, member, None, None),
        P(TOWER, member, None),
        P(None, TOWER, None),
        P(None, TOWER, None),
        P(),
        P(),
        P(),
        P(member, None),
    )
    return jax.shard_map(
        per_device,
        mesh=split,
        in_specs=placed,
        out_specs=(
            P(TOWER, member, None, None),
            P(TOWER, member, None),
            P(member, TOWER, None),
            P(member, TOWER, None),
            P(TOWER + member, None),
            P(TOWER + member, None),
            P(member, TOWER),
        ),
        check_vma=False,
    )
```

```python
import math

import jax
import jax.numpy as jnp
from jax import lax
from jax.experimental import pallas as pl
from jax.experimental.pallas import tpu as pltpu
from jax.sharding import Mesh, PartitionSpec as P

DECAY_RATE = 0.98
LEARN_RATE = 1.0
EPSILON = 1e-08
F32 = jnp.float32
BF16 = jnp.bfloat16
NN = (((1,), (0,)), ((), ()))
NT = (((1,), (1,)), ((), ()))
TOWER = ("y", "xl")
QUAD = ("xh", "core")
VMEM_LIMIT = 16 << 20


def halves(a):
    high = a.astype(BF16)
    return high, (a - high.astype(F32)).astype(BF16)


def dot1(a, b, dims):
    return lax.dot_general(a, b, dims, preferred_element_type=F32)


def dot3(a, b, dims=NN):
    return dot1(a[0], b[0], dims) + (dot1(a[0], b[1], dims) + dot1(a[1], b[0], dims))


def dot32(a, b, dims=NN):
    return dot3(halves(a), halves(b), dims)


def vmem(count):
    return [pl.BlockSpec(memory_space=pltpu.VMEM)] * count


def call(kernel, outs, spec_in, scratch=(), name=None, flops=0):
    return pl.pallas_call(
        kernel,
        cost_estimate=pl.CostEstimate(flops=int(flops), transcendentals=0, bytes_accessed=1 << 20),
        out_shape=outs,
        in_specs=spec_in,
        out_specs=vmem(len(outs)),
        scratch_shapes=list(scratch),
        compiler_params=pltpu.CompilerParams(vmem_limit_bytes=VMEM_LIMIT),
        name=name,
    )


SMEM_SPEC = pl.BlockSpec(memory_space=pltpu.SMEM)


def decay(touch, elapsed, tables, decayed):
    towers, width, rows = tables.shape
    touches = touch.shape[1]
    for t in range(towers):
        ids = jnp.broadcast_to(touch[t : t + 1, :].astype(F32), (touches, touches)).T
        rates = jnp.exp(elapsed[t : t + 1, :].astype(F32) * math.log(DECAY_RATE))
        rates = jnp.broadcast_to(rates, (touches, touches)).T
        factor = []
        for block in range(rows // touches):
            row = lax.broadcasted_iota(jnp.int32, (touches, touches), 1).astype(F32) + float(block * touches)
            match = ids == row
            hits = jnp.sum(jnp.where(match, 1.0, 0.0), axis=0, keepdims=True)
            chosen = jnp.sum(jnp.where(match, rates, 0.0), axis=0, keepdims=True)
            factor.append(jnp.where(hits > 0.0, chosen, 1.0))
        decayed[t] = tables[t] * jnp.concatenate(factor, axis=1)


def pool_half(side, bag, decayed, pooled, counts):
    towers, width, rows = decayed.shape
    chunks, _, part = pooled.shape
    for t in range(towers):
        both = jnp.concatenate(halves(decayed[t]), axis=0)

        def block_of(k, carry, t=t, both=both):
            at = pl.multiple_of(k * 2 * part + side * part, part)
            ids = bag[t, :, pl.ds(at, part)]
            row = lax.broadcasted_iota(jnp.int32, (rows, part), 0)
            count = jnp.zeros((rows, part), F32)
            for b in range(ids.shape[0]):
                count = count + jnp.where(row == ids[b : b + 1, :], 1.0, 0.0)
            count = count.astype(BF16)
            counts[t, k] = count
            total = dot1(both, count, NN)
            pooled[k, t * width : (t + 1) * width, :] = total[:width] + total[width:]
            return carry

        lax.fori_loop(0, chunks, block_of, 0)


def pool_far_kernel(idx, bag_hbm, touch_hbm, elapsed_hbm, tables_hbm, pooled, counts, decayed, bag, touch, elapsed, tables, sems):
    pairs = ((bag_hbm, bag), (touch_hbm, touch), (elapsed_hbm, elapsed), (tables_hbm, tables))
    copies = [pltpu.make_async_copy(a, b, sems.at[n]) for n, (a, b) in enumerate(pairs)]
    for copy in copies:
        copy.start()
    for copy in copies:
        copy.wait()
    decay(touch, elapsed, tables, decayed)
    pool_half(1 - idx[1], bag, decayed, pooled, counts)


def pool_near_kernel(idx, bag, decayed, pooled, counts):
    pool_half(idx[1], bag, decayed, pooled, counts)


def turn_kernel(w, high, low):
    rows = w.shape[0]
    flat = w.reshape(rows * 16, 128)
    for t in range(2):
        for b in range(8):
            h, l = halves(flat[pl.ds(b * 2 + t, rows, stride=16), :].T)
            high[t, b * 128 : (b + 1) * 128, :] = h
            low[t, b * 128 : (b + 1) * 128, :] = l


def pick_kernel(idx, w, high, low):
    rows = w.shape[2]
    flat = w.reshape(rows * 16, 128)
    for t in range(2):
        for b in range(8):
            h, l = halves(flat[pl.ds(b * 2 + t, rows, stride=16), :])
            high[t, :, b * 128 : (b + 1) * 128] = h
            low[t, :, b * 128 : (b + 1) * 128] = l


def second_kernel(w, high, low, high_t, low_t):
    rows = w.shape[0]
    flat = w.reshape(rows * 4, 128)
    for t in range(2):
        for b in range(2):
            lanes = slice(b * 128, (b + 1) * 128)
            value = flat[pl.ds(b * 2 + t, rows, stride=4), :]
            h, l = halves(value)
            high[t, :, lanes] = h
            low[t, :, lanes] = l
            h, l = halves(value.T)
            high_t[t, lanes, :] = h
            low_t[t, lanes, :] = l


def forward_kernel(with_pay, idx, x1, x2, y1, y2, w1h, w1l, w2h, w2l, press, lift, head, hidden, start, *rest):
    fh, fl = rest[-2:]
    sets = (x1, x2, y1, y2)
    zs, pair, samples = x1.shape
    width = pair // 2
    xh, core = idx[1], idx[2]
    place = ((xh, core), (1 - xh, core), (xh, 1 - core), (1 - xh, 1 - core))
    width_out = w2h.shape[1]

    def one_tower(t, carry):
        for (a, b), ref in zip(place, sets):
            for z in range(zs):
                h, l = halves(ref[z, pl.ds(pl.multiple_of(t * width, width), width), :])
                at = pl.multiple_of(((z * 2 + a) * 2 + b) * width, width)
                fh[pl.ds(at, width), :] = h
                fl[pl.ds(at, width), :] = l
        value = dot3((w1h[t], w1l[t]), (fh[...], fl[...]))
        hidden[t] = value
        act = halves(value * jax.nn.sigmoid(value))
        start[pl.ds(pl.multiple_of(t * width_out, width_out), width_out), :] = dot3((w2h[t], w2l[t]), act)
        return carry

    lax.fori_loop(0, 2, one_tower, 0)
    if with_pay:
        pay = rest[0]
        own = samples // 2
        rank = press.shape[1]
        x0 = halves(start[:, pl.ds(pl.multiple_of(core * own, own), own)])
        p = dot3(halves(press[...].T), x0)
        q = dot3(halves(lift[...].T * head[...]), x0)
        d = dot3(halves(jnp.broadcast_to(head[...], (8, head.shape[1]))), x0)
        for j in range(pay.shape[0]):
            pay[j, 0:rank, :] = p
            pay[j, rank : 2 * rank, :] = q
            pay[j, 2 * rank : 2 * rank + 8, :] = d


def logit_kernel(parts, labels, pay, logits):
    total = parts[0]
    for j in range(1, parts.shape[0]):
        total = total + parts[j]
    rank = (total.shape[0] - 8) // 2
    value = jnp.sum(total[0:rank] * total[rank : 2 * rank], axis=0, keepdims=True) + total[2 * rank : 2 * rank + 1]
    logits[...] = value
    error = jax.nn.sigmoid(value) - labels[...].astype(F32)
    pay[0 : 2 * rank, :] = total[0 : 2 * rank]
    pay[2 * rank : 2 * rank + 8, :] = jnp.broadcast_to(error, (8, error.shape[1]))


def grads_kernel(idx, own, c1, xa, xb, hid_a, hid_b, w1h, w1l, w2h, w2l, press, lift, head, ghh, ghl, gout, pq, g0, g1, g2, g3):
    core = idx[2]
    rank = press.shape[1]
    n = own.shape[1]
    half = 2 * n
    outs = (g0, g1, g2, g3)
    width = w1h.shape[1] // 4
    width_out = w2h.shape[2]
    column = jnp.broadcast_to(head[...], (128, head.shape[1])).T[:, 0:1]
    first_core = core == 0
    for g, (mine, other, hidden) in enumerate(((own, c1, hid_a), (xa, xb, hid_b))):
        left = jnp.where(first_core, mine[...], other[...])
        right = jnp.where(first_core, other[...], mine[...])
        both = jnp.concatenate([left, right], axis=1)
        p, q, error = both[0:rank], both[rank : 2 * rank], both[2 * rank : 2 * rank + 1]
        lanes = slice(g * half, (g + 1) * half)
        pq[0:rank, lanes] = error * p
        pq[rank : 2 * rank, lanes] = error * q
        scaling = dot32(lift[...], p)
        back = dot32(press[...], q)
        gout[:, lanes] = error * (column * (scaling + 1.0) + back)

        def one_tower(t, carry, lanes=lanes, hidden=hidden):
            go = halves(gout[pl.ds(pl.multiple_of(t * width_out, width_out), width_out), lanes])
            ga = dot3((w2h[t], w2l[t]), go)
            value = hidden[t]
            s = jax.nn.sigmoid(value)
            gh = halves(ga * (s * (1.0 + value * (1.0 - s))))
            ghh[t, :, lanes] = gh[0]
            ghl[t, :, lanes] = gh[1]
            grad = dot3((w1h[t], w1l[t]), gh)
            for k in range(4):
                outs[k][pl.ds(pl.multiple_of(t * width, width), width), lanes] = grad[k * width : (k + 1) * width]
            return carry

        lax.fori_loop(0, 2, one_tower, 0)


def weights_kernel(idx, near, far, ghh, ghl, gout, hid_a, hid_b, x0a, x0b, pq, *blocks):
    z, quad = idx[0], 2 * idx[1] + idx[2]
    width = near.shape[1] // 2
    width_out = gout.shape[0] // 2
    for t in range(2):
        outs = blocks[4 * t : 4 * t + 4]
        rows = slice(t * width, (t + 1) * width)
        f, act = [], []
        for k in range(4):
            at = lax.rem(z + k, 4)
            f.append(jnp.concatenate([near[at, rows, :], far[at, rows, :]], axis=1))
            pick = pl.ds(pl.multiple_of((at * 4 + quad) * width, width), width)
            value = jnp.concatenate([hid_a[t, pick, :], hid_b[t, pick, :]], axis=1)
            act.append(value * jax.nn.sigmoid(value))
        grad = dot3(halves(jnp.concatenate(f, axis=0)), (ghh[t], ghl[t]), NT)
        for k in range(4):
            outs[k][0:width, :] = grad[k * width : (k + 1) * width]
        grad = dot32(jnp.concatenate(act, axis=0), gout[t * width_out : (t + 1) * width_out, :], NT)
        for k in range(4):
            for b in range(4):
                outs[k][width : width + 16, b * 256 : (b + 1) * 256] = grad[k * width + 16 * b : k * width + 16 * b + 16]
    rank = pq.shape[0] // 2
    x0 = []
    for k in range(4):
        pick = pl.ds(pl.multiple_of((lax.rem(z + k, 4) * 4 + quad) * 32, 32), 32)
        x0.append(jnp.concatenate([x0a[pick, :], x0b[pick, :]], axis=1))
    x0 = jnp.concatenate(x0, axis=0)
    both = dot32(x0, pq[...], NT)
    for k in range(4):
        for b in range(4):
            outs[k][width + 16 : width + 24, b * 256 : (b + 1) * 256] = both[32 * k + 8 * b : 32 * k + 8 * b + 8]


def update_kernel(idx, p0, p1, p2, p3, near, far, decayed, accumulator, new_tables, new_accumulator):
    z = idx[0]
    towers, width, rows = decayed.shape
    half = p0.shape[1] // 2
    for t in range(towers):
        total = jnp.zeros((2 * width, rows), F32)
        for k, ref in enumerate((p0, p1, p2, p3)):
            at = lax.rem(z + 4 - k, 4)
            both = jnp.concatenate(halves(ref[t * width : (t + 1) * width, :]), axis=0)
            total = total + dot1(both[:, :half], near[t, at], NT)
            total = total + dot1(both[:, half:], far[t, at], NT)
        grad = total[:width] + total[width:]
        square = jnp.sum(grad * grad, axis=0, keepdims=True) * (1.0 / width)
        fresh = accumulator[t : t + 1, :] + square
        new_accumulator[t : t + 1, :] = fresh
        new_tables[t] = decayed[t] - LEARN_RATE * grad / (jnp.sqrt(fresh) + EPSILON)


def sum_kernel(head, *refs):
    parts, (first, second, lift, press) = refs[:6], refs[6:]
    for t in range(2):
        a, b, c = parts[3 * t : 3 * t + 3]
        total = a[...] + (b[...] + c[...])
        for k in range(8):
            first[pl.ds(2 * k + t, 64, stride=16), :] = total[0:64, k * 128 : (k + 1) * 128]
        for b in range(4):
            for o in range(2):
                lanes = slice(b * 256 + o * 128, b * 256 + (o + 1) * 128)
                second[pl.ds(b * 64 + 2 * o + t, 16, stride=4), :] = total[64:80, lanes]
        if t == 1:
            column = jnp.broadcast_to(head[...], (128, 32)).T
            for b in range(4):
                at = slice(8 * b, 8 * b + 8)
                lift[at, :] = column[at] * total[80:88, b * 256 : b * 256 + 128]
                press[at, :] = total[80:88, b * 256 + 128 : (b + 1) * 256]


def shift(x, axis, size, by):
    return lax.ppermute(x, axis, [(i, (i + by) % size) for i in range(size)])


def flip(x, axis, size, bit):
    return lax.ppermute(x, axis, [(i, i ^ bit) for i in range(size)])


def per_device(bag_ids, touch_ids, elapsed, tables, accumulator, first_weight, second_weight, lift_weight, press_weight, head_weight, labels):
    f32 = lambda *shape: jax.ShapeDtypeStruct(shape, F32)
    bf16 = lambda *shape: jax.ShapeDtypeStruct(shape, BF16)
    z, xh, core = lax.axis_index("z"), lax.axis_index("xh"), lax.axis_index("core")
    idx = jnp.stack([z, xh, core]).astype(jnp.int32)
    tower = lax.axis_index(TOWER)
    rank = lift_weight.shape[1]
    local = lift_weight.shape[0] // 8
    any_spec = pl.BlockSpec(memory_space=pl.ANY)

    tables_t = jnp.transpose(tables[:, 0], (0, 2, 1))
    bag = bag_ids[:, 0]
    hbm = lambda x: pltpu.with_memory_space_constraint(x, pltpu.HBM)
    pooled_far, counts_far, decayed = call(
        pool_far_kernel,
        [f32(4, 128, 256), bf16(2, 4, 512, 256), f32(2, 64, 512)],
        [SMEM_SPEC] + [any_spec] * 4,
        [
            pltpu.VMEM((2, 4, 2048), jnp.int32),
            pltpu.VMEM((2, 128), jnp.int32),
            pltpu.VMEM((2, 128), jnp.int32),
            pltpu.VMEM((2, 64, 512), F32),
            pltpu.SemaphoreType.DMA((4,)),
        ],
        name="pool_far",
        flops=1e6,
    )(idx, hbm(bag), hbm(touch_ids[:, 0]), hbm(elapsed[:, 0]), hbm(tables_t))
    fq_far = lax.all_to_all(pooled_far, "z", 0, 0, tiled=True)
    pooled_near, counts_near = call(
        pool_near_kernel, [f32(4, 128, 256), bf16(2, 4, 512, 256)], [SMEM_SPEC] + vmem(2), name="pool_near", flops=1e6
    )(idx, bag, decayed)
    fq_near = lax.all_to_all(pooled_near, "z", 0, 0, tiled=True)

    _, first_weight, second_weight, lift_weight, press_weight, head_weight = lax.optimization_barrier(
        (decayed, first_weight, second_weight, lift_weight, press_weight, head_weight)
    )
    lift = lax.dynamic_slice_in_dim(lift_weight, tower * local, local, 0)
    press = lax.dynamic_slice_in_dim(press_weight, tower * local, local, 0)
    head = lax.dynamic_slice_in_dim(head_weight, tower * local, local, 0)[None, :]
    mine = lax.dynamic_slice_in_dim(head[0], ((z * 2 + xh) * 2 + core) * 32, 32, 0)[None, :]
    view = first_weight.reshape(1024, 2, 8, 128).transpose(0, 2, 1, 3).reshape(1024, 16, 128)
    w1th, w1tl = pl.pallas_call(
        turn_kernel,
        grid=(8,),
        in_specs=[pl.BlockSpec((128, 16, 128), lambda i: (i, 0, 0))],
        out_specs=[pl.BlockSpec((2, 1024, 128), lambda i: (0, 0, i))] * 2,
        out_shape=[bf16(2, 1024, 1024)] * 2,
        compiler_params=pltpu.CompilerParams(vmem_limit_bytes=VMEM_LIMIT),
        cost_estimate=pl.CostEstimate(flops=int(1e6), transcendentals=0, bytes_accessed=1 << 20),
        name="turn",
    )(hbm(view))
    w1qh, w1ql = pl.pallas_call(
        pick_kernel,
        grid_spec=pltpu.PrefetchScalarGridSpec(
            num_scalar_prefetch=1,
            grid=(4,),
            in_specs=[pl.BlockSpec((1, 1, 64, 16, 128), lambda k, i: (lax.rem(i[0] + k, 4), 2 * i[1] + i[2], 0, 0, 0))],
            out_specs=[pl.BlockSpec((2, 64, 1024), lambda k, i: (0, k, 0))] * 2,
        ),
        out_shape=[bf16(2, 256, 1024)] * 2,
        compiler_params=pltpu.CompilerParams(vmem_limit_bytes=VMEM_LIMIT),
        cost_estimate=pl.CostEstimate(flops=int(1e6), transcendentals=0, bytes_accessed=1 << 20),
        name="pick",
    )(idx, hbm(view.reshape(4, 4, 64, 16, 128)))
    w2h, w2l, w2th, w2tl = call(
        second_kernel, [bf16(2, 1024, 256)] * 2 + [bf16(2, 256, 1024)] * 2, vmem(1), name="second", flops=1e6
    )(second_weight.reshape(1024, 2, 2, 128).transpose(0, 2, 1, 3).reshape(1024, 4, 128))

    ready, _ = lax.optimization_barrier((fq_far, pooled_near))
    x2 = flip(ready, "xh", 2, 1)
    y1 = flip(fq_near, "core", 2, 1)
    y2 = flip(x2, "core", 2, 1)
    x2b = flip(fq_near, "xh", 2, 1)
    y1b = flip(fq_far, "core", 2, 1)
    y2b = flip(x2b, "core", 2, 1)

    scratch = [pltpu.VMEM((1024, 256), BF16)] * 2
    weights = (w1th, w1tl, w2th, w2tl, press, lift, head)
    hid_a, x0a, pay = call(
        lambda *refs: forward_kernel(True, *refs),
        [f32(2, 1024, 256), f32(512, 256), f32(8, 2 * rank + 8, 128)],
        [SMEM_SPEC] + vmem(11),
        scratch,
        name="forward_a",
        flops=1e6,
    )(idx, fq_near, x2, y1, y2, *weights)
    parts = lax.all_to_all(pay, TOWER, 0, 0, tiled=True)
    hid_b, x0b = call(
        lambda *refs: forward_kernel(False, *refs),
        [f32(2, 1024, 256), f32(512, 256)],
        [SMEM_SPEC] + vmem(11),
        scratch,
        name="forward_b",
        flops=1e6,
    )(idx, fq_far, x2b, y1b, y2b, *weights)
    pay, logits = call(logit_kernel, [f32(2 * rank + 8, 128), f32(1, 128)], vmem(2), name="logit", flops=1e6)(parts, labels)
    logits = lax.dynamic_slice_in_dim(logits, tower * 16, 16, 1)
    pays = [pay] + [flip(pay, QUAD, 4, k) for k in (1, 2, 3)]

    ghh, ghl, gout, pq, *g = call(
        grads_kernel,
        [bf16(2, 1024, 512), bf16(2, 1024, 512), f32(512, 512), f32(2 * rank, 512)] + [f32(128, 512)] * 4,
        [SMEM_SPEC] + vmem(13),
        name="grads",
        flops=9e9,
    )(idx, *pays, hid_a, hid_b, w1qh, w1ql, w2h, w2l, press, lift, head)
    got = [g[0]] + [shift(g[k], "z", 4, k) for k in (1, 2, 3)]
    w = call(
        weights_kernel,
        [f32(80, 1024)] * 4 + [f32(88, 1024)] * 4,
        [SMEM_SPEC] + vmem(10),
        name="weights",
        flops=5e9,
    )(idx, fq_near, fq_far, ghh, ghl, gout, hid_a, hid_b, x0a, x0b, pq)
    w, v = w[:4], w[4:]
    up = shift(w[2], "z", 4, 1)
    down = shift(v[2], "z", 4, 3)
    v1 = shift(v[1], "z", 4, 1)
    w3 = shift(w[3], "z", 4, 3)
    w1 = shift(w[1] + up, "z", 4, 1)
    v3 = shift(v[3] + down, "z", 4, 3)
    new_tables, new_accumulator = call(
        update_kernel, [f32(2, 64, 512), f32(2, 512)], [SMEM_SPEC] + vmem(8), name="update", flops=5e9
    )(idx, *got, counts_near, counts_far, decayed, accumulator[:, 0])
    first, second, lift_out, press_out = call(
        sum_kernel, [f32(1024, 128), f32(256, 128), f32(32, rank), f32(32, rank)], vmem(7), name="sum", flops=1e6
    )(mine, w[0], w1, w3, v[0], v1, v3)
    return (
        jnp.transpose(new_tables, (0, 2, 1))[:, None],
        new_accumulator[:, None],
        first.reshape(64, 8, 2, 128).transpose(0, 2, 1, 3).reshape(64, 2, 1024),
        second.reshape(64, 2, 2, 128).transpose(0, 2, 1, 3).reshape(64, 2, 256),
        lift_out,
        press_out,
        logits,
    )


def solution(mesh):
    split = Mesh(mesh.devices.reshape(4, 2, 4, 2, 2), ("y", "xl", "z", "xh", "core"))
    member = ("z", "xh", "core")
    placed = (
        P(TOWER, member, None, None),
        P(TOWER, member, None),
        P(TOWER, member, None),
        P(TOWER, member, None, None),
        P(TOWER, member, None),
        P(None, TOWER, None),
        P(None, TOWER, None),
        P(),
        P(),
        P(),
        P(member, None),
    )
    return jax.shard_map(
        per_device,
        mesh=split,
        in_specs=placed,
        out_specs=(
            P(TOWER, member, None, None),
            P(TOWER, member, None),
            P(member, TOWER, None),
            P(member, TOWER, None),
            P(TOWER + member, None),
            P(TOWER + member, None),
            P(member, TOWER),
        ),
        check_vma=False,
    )
```

```python
import math

import jax
import jax.numpy as jnp
from jax import lax
from jax.experimental import pallas as pl
from jax.experimental.pallas import tpu as pltpu
from jax.sharding import Mesh, PartitionSpec as P

DECAY_RATE = 0.98
LEARN_RATE = 1.0
EPSILON = 1e-08
F32 = jnp.float32
BF16 = jnp.bfloat16
NN = (((1,), (0,)), ((), ()))
NT = (((1,), (1,)), ((), ()))
TOWER = ("y", "xl")
QUAD = ("xh", "core")
VMEM_LIMIT = 16 << 20


def halves(a):
    high = a.astype(BF16)
    return high, (a - high.astype(F32)).astype(BF16)


def dot1(a, b, dims):
    return lax.dot_general(a, b, dims, preferred_element_type=F32)


def dot3(a, b, dims=NN):
    return dot1(a[0], b[0], dims) + (dot1(a[0], b[1], dims) + dot1(a[1], b[0], dims))


def dot32(a, b, dims=NN):
    return dot3(halves(a), halves(b), dims)


def vmem(count):
    return [pl.BlockSpec(memory_space=pltpu.VMEM)] * count


def call(kernel, outs, spec_in, scratch=(), name=None, flops=0):
    return pl.pallas_call(
        kernel,
        cost_estimate=pl.CostEstimate(flops=int(flops), transcendentals=0, bytes_accessed=1 << 20),
        out_shape=outs,
        in_specs=spec_in,
        out_specs=vmem(len(outs)),
        scratch_shapes=list(scratch),
        compiler_params=pltpu.CompilerParams(vmem_limit_bytes=VMEM_LIMIT),
        name=name,
    )


SMEM_SPEC = pl.BlockSpec(memory_space=pltpu.SMEM)


def decay(touch, elapsed, tables, decayed):
    towers, width, rows = tables.shape
    touches = touch.shape[1]
    for t in range(towers):
        ids = jnp.broadcast_to(touch[t : t + 1, :].astype(F32), (touches, touches)).T
        rates = jnp.exp(elapsed[t : t + 1, :].astype(F32) * math.log(DECAY_RATE))
        rates = jnp.broadcast_to(rates, (touches, touches)).T
        factor = []
        for block in range(rows // touches):
            row = lax.broadcasted_iota(jnp.int32, (touches, touches), 1).astype(F32) + float(block * touches)
            match = ids == row
            hits = jnp.sum(jnp.where(match, 1.0, 0.0), axis=0, keepdims=True)
            chosen = jnp.sum(jnp.where(match, rates, 0.0), axis=0, keepdims=True)
            factor.append(jnp.where(hits > 0.0, chosen, 1.0))
        decayed[t] = tables[t] * jnp.concatenate(factor, axis=1)


def pool_half(idx, side, bag, decayed, pooled, counts):
    towers, width, rows = decayed.shape
    part = pooled[0].shape[1]
    for t in range(towers):
        both = jnp.concatenate(halves(decayed[t]), axis=0)
        for k, out in enumerate(pooled):
            chunk = lax.rem(idx[0] + k, 4)
            at = pl.multiple_of(chunk * 2 * part + side * part, part)
            ids = bag[t, :, pl.ds(at, part)]
            row = lax.broadcasted_iota(jnp.int32, (rows, part), 0)
            count = jnp.zeros((rows, part), F32)
            for b in range(ids.shape[0]):
                count = count + jnp.where(row == ids[b : b + 1, :], 1.0, 0.0)
            count = count.astype(BF16)
            counts[t, chunk] = count
            total = dot1(both, count, NN)
            out[t * width : (t + 1) * width, :] = total[:width] + total[width:]


def pool_far_kernel(idx, bag_hbm, touch_hbm, elapsed_hbm, tables_hbm, p0, p1, p2, p3, counts, decayed, bag, touch, elapsed, tables, sems):
    pairs = ((bag_hbm, bag), (touch_hbm, touch), (elapsed_hbm, elapsed), (tables_hbm, tables))
    copies = [pltpu.make_async_copy(a, b, sems.at[n]) for n, (a, b) in enumerate(pairs)]
    for copy in copies:
        copy.start()
    for copy in copies:
        copy.wait()
    decay(touch, elapsed, tables, decayed)
    pool_half(idx, 1 - idx[1], bag, decayed, (p0, p1, p2, p3), counts)


def pool_near_kernel(idx, bag, decayed, p0, p1, p2, p3, counts):
    pool_half(idx, idx[1], bag, decayed, (p0, p1, p2, p3), counts)


def pack_kernel(idx, p0, p1, p2, p3, out):
    for k, ref in enumerate((p0, p1, p2, p3)):
        out[lax.rem(idx[0] + 4 - k, 4)] = ref[...]


def turn_kernel(w, high, low):
    rows = w.shape[0]
    flat = w.reshape(rows * 16, 128)
    for t in range(2):
        for b in range(8):
            h, l = halves(flat[pl.ds(b * 2 + t, rows, stride=16), :].T)
            high[t, b * 128 : (b + 1) * 128, :] = h
            low[t, b * 128 : (b + 1) * 128, :] = l


def pick_kernel(idx, w, high, low):
    rows = w.shape[2]
    flat = w.reshape(rows * 16, 128)
    for t in range(2):
        for b in range(8):
            h, l = halves(flat[pl.ds(b * 2 + t, rows, stride=16), :])
            high[t, :, b * 128 : (b + 1) * 128] = h
            low[t, :, b * 128 : (b + 1) * 128] = l


def prepare_kernel(idx, second_hbm, lift_hbm, press_hbm, heads, high_t, low_t, lift, press, head, second, sems):
    tower = idx[3]
    rows = pl.ds(pl.multiple_of(tower * lift.shape[0], lift.shape[0]), lift.shape[0])
    pairs = ((second_hbm, second), (lift_hbm.at[rows, :], lift), (press_hbm.at[rows, :], press))
    copies = [pltpu.make_async_copy(a, b, sems.at[n]) for n, (a, b) in enumerate(pairs)]
    for copy in copies:
        copy.start()
    head[...] = jnp.concatenate([heads[pl.ds(tower * 4 + b, 1), :] for b in range(4)], axis=1)
    for copy in copies:
        copy.wait()
    count = second.shape[0]
    flat = second.reshape(count * 4, 128)
    for t in range(2):
        for b in range(2):
            lanes = slice(b * 128, (b + 1) * 128)
            h, l = halves(flat[pl.ds(b * 2 + t, count, stride=4), :].T)
            high_t[t, lanes, :] = h
            low_t[t, lanes, :] = l


def natural_kernel(w, high, low):
    rows = w.shape[0]
    flat = w.reshape(rows * 4, 128)
    for t in range(2):
        for b in range(2):
            lanes = slice(b * 128, (b + 1) * 128)
            h, l = halves(flat[pl.ds(b * 2 + t, rows, stride=4), :])
            high[t, :, lanes] = h
            low[t, :, lanes] = l


def forward_kernel(towers, with_pay, idx, x1, x2, y1, y2, w1h, w1l, w2h, w2l, press, lift, head, hidden, start, *rest):
    fh, fl = rest[-2:]
    sets = (x1, x2, y1, y2)
    zs, pair, samples = x1.shape
    width = pair // 2
    xh, core = idx[1], idx[2]
    place = ((xh, core), (1 - xh, core), (xh, 1 - core), (1 - xh, 1 - core))
    width_out = w2h.shape[1]

    def one_tower(t, slot):
        for (a, b), ref in zip(place, sets):
            for z in range(zs):
                h, l = halves(ref[z, pl.ds(pl.multiple_of(t * width, width), width), :])
                at = pl.multiple_of(((z * 2 + a) * 2 + b) * width, width)
                fh[pl.ds(at, width), :] = h
                fl[pl.ds(at, width), :] = l
        value = dot3((w1h[t], w1l[t]), (fh[...], fl[...]))
        hidden[slot] = value
        act = halves(value * jax.nn.sigmoid(value))
        start[pl.ds(pl.multiple_of(slot * width_out, width_out), width_out), :] = dot3((w2h[t], w2l[t]), act)

    if len(towers) == 2:

        def step(t, carry):
            one_tower(t, t)
            return carry

        lax.fori_loop(0, 2, step, 0)
    else:
        one_tower(towers[0], 0)
    if with_pay:
        pay = rest[0]
        own = samples // 2
        rank = press.shape[1]
        x0 = halves(start[:, pl.ds(pl.multiple_of(core * own, own), own)])
        p = dot3(halves(press[...].T), x0)
        q = dot3(halves(lift[...].T * head[...]), x0)
        d = dot3(halves(jnp.broadcast_to(head[...], (8, head.shape[1]))), x0)
        pay[0:rank, :] = p
        pay[rank : 2 * rank, :] = q
        pay[2 * rank : 2 * rank + 8, :] = d


def logit_kernel(idx, mine, other, labels, pay, logits):
    total = mine[...] + other[...]
    rank = (total.shape[0] - 8) // 2
    value = jnp.sum(total[0:rank] * total[rank : 2 * rank], axis=0, keepdims=True) + total[2 * rank : 2 * rank + 1]
    turned = pltpu.roll(jnp.broadcast_to(value, (8, 128)), lax.rem(128 - 16 * idx[3], 128), 1)
    logits[...] = turned[0:1, 0:16]
    error = jax.nn.sigmoid(value) - labels[...].astype(F32)
    pay[0 : 2 * rank, :] = total[0 : 2 * rank]
    pay[2 * rank : 2 * rank + 8, :] = jnp.broadcast_to(error, (8, error.shape[1]))


def grads_kernel(idx, own, c1, xa, xb, hid_a, hid_b0, hid_b1, w1h, w1l, w2h, w2l, press, lift, head, ghh, ghl, gout, pq, g0, g1, g2, g3):
    core = idx[2]
    rank = press.shape[1]
    n = own.shape[1]
    half = 2 * n
    outs = (g0, g1, g2, g3)
    width = w1h.shape[1] // 4
    width_out = w2h.shape[2]
    column = jnp.broadcast_to(head[...], (128, head.shape[1])).T[:, 0:1]
    first_core = core == 0
    for g, (mine, other, hidden) in enumerate(((own, c1, (hid_a.at[0], hid_a.at[1])), (xa, xb, (hid_b0.at[0], hid_b1.at[0])))):
        left = jnp.where(first_core, mine[...], other[...])
        right = jnp.where(first_core, other[...], mine[...])
        both = jnp.concatenate([left, right], axis=1)
        p, q, error = both[0:rank], both[rank : 2 * rank], both[2 * rank : 2 * rank + 1]
        lanes = slice(g * half, (g + 1) * half)
        pq[0:rank, lanes] = error * p
        pq[rank : 2 * rank, lanes] = error * q
        scaling = dot32(lift[...], p)
        back = dot32(press[...], q)
        gout[:, lanes] = error * (column * (scaling + 1.0) + back)

        for t in range(2):
            go = halves(gout[t * width_out : (t + 1) * width_out, lanes])
            ga = dot3((w2h[t], w2l[t]), go)
            value = hidden[t][...]
            s = jax.nn.sigmoid(value)
            gh = halves(ga * (s * (1.0 + value * (1.0 - s))))
            ghh[t, :, lanes] = gh[0]
            ghl[t, :, lanes] = gh[1]
            grad = dot3((w1h[t], w1l[t]), gh)
            for k in range(4):
                outs[k][t * width : (t + 1) * width, lanes] = grad[k * width : (k + 1) * width]


def weights_kernel(idx, near, far, ghh, ghl, gout, hid_a, hid_b0, hid_b1, x0a, x0b0, x0b1, pq, g1, g3, *blocks):
    hid_b, x0b = (hid_b0, hid_b1), (x0b0, x0b1)
    z, quad = idx[0], 2 * idx[1] + idx[2]
    width = near.shape[1] // 2
    width_out = gout.shape[0] // 2
    for t in range(2):
        outs = blocks[4 * t : 4 * t + 4]
        rows = slice(t * width, (t + 1) * width)
        f, act = [], []
        for k in range(4):
            at = lax.rem(z + k, 4)
            f.append(jnp.concatenate([near[at, rows, :], far[at, rows, :]], axis=1))
            pick = pl.ds(pl.multiple_of((at * 4 + quad) * width, width), width)
            value = jnp.concatenate([hid_a[t, pick, :], hid_b[t][0, pick, :]], axis=1)
            act.append(value * jax.nn.sigmoid(value))
        grad = dot3(halves(jnp.concatenate(f, axis=0)), (ghh[t], ghl[t]), NT)
        for k in range(4):
            outs[k][0:width, :] = grad[k * width : (k + 1) * width]
        grad = dot32(jnp.concatenate(act, axis=0), gout[t * width_out : (t + 1) * width_out, :], NT)
        for k in range(4):
            for b in range(4):
                outs[k][width : width + 16, b * 256 : (b + 1) * 256] = grad[k * width + 16 * b : k * width + 16 * b + 16]
    for out, ref in ((blocks[5], g1), (blocks[3], g3)):
        base = out.shape[0] - width
        for t in range(2):
            out[base:, t * 512 : (t + 1) * 512] = ref[t * width : (t + 1) * width, :]
    rank = pq.shape[0] // 2
    x0 = []
    for k in range(4):
        block = lax.rem(z + k, 4) * 4 + quad
        pick = pl.ds(pl.multiple_of(block * 32, 32), 32)
        near_half = pl.ds(pl.multiple_of(lax.rem(block, 8) * 32, 32), 32)
        later = jnp.where(block < 8, x0b[0][near_half, :], x0b[1][near_half, :])
        x0.append(jnp.concatenate([x0a[pick, :], later], axis=1))
    x0 = jnp.concatenate(x0, axis=0)
    both = dot32(x0, pq[...], NT)
    for k in range(4):
        for b in range(4):
            outs[k][width + 16 : width + 24, b * 256 : (b + 1) * 256] = both[32 * k + 8 * b : 32 * k + 8 * b + 8]


def update_kernel(idx, p0, p1, p2, p3, near, far, decayed, accumulator, new_tables, new_accumulator):
    z = idx[0]
    towers, width, rows = decayed.shape
    half = p0.shape[1] // 2
    for t in range(towers):
        total = jnp.zeros((2 * width, rows), F32)
        for k, ref in enumerate((p0, p1, p2, p3)):
            at = lax.rem(z + 4 - k, 4)
            if ref.shape[0] == towers * width:
                value = ref[t * width : (t + 1) * width, :]
            else:
                value = ref[ref.shape[0] - width :, t * 2 * half : (t + 1) * 2 * half]
            both = jnp.concatenate(halves(value), axis=0)
            total = total + dot1(both[:, :half], near[t, at], NT)
            total = total + dot1(both[:, half:], far[t, at], NT)
        grad = total[:width] + total[width:]
        square = jnp.sum(grad * grad, axis=0, keepdims=True) * (1.0 / width)
        fresh = accumulator[t : t + 1, :] + square
        new_accumulator[t : t + 1, :] = fresh
        new_tables[t] = decayed[t] - LEARN_RATE * grad / (jnp.sqrt(fresh) + EPSILON)


def sum_kernel(idx, head, *refs):
    parts, (first, second, lift, press, wide) = refs[:6], refs[6:]
    for t in range(2):
        a, b, c = parts[3 * t : 3 * t + 3]
        total = a[...] + (b[0 : a.shape[0]] + c[0 : a.shape[0]])
        for k in range(8):
            first[pl.ds(2 * k + t, 64, stride=16), :] = total[0:64, k * 128 : (k + 1) * 128]
        for b in range(4):
            for o in range(2):
                lanes = slice(b * 256 + o * 128, b * 256 + (o + 1) * 128)
                second[pl.ds(b * 64 + 2 * o + t, 16, stride=4), :] = total[64:80, lanes]
        if t == 1:
            wide[...] = jnp.broadcast_to(head[...], (128, head.shape[1])).T
            device = (idx[0] * 2 + idx[1]) * 2 + idx[2]
            column = wide[pl.ds(pl.multiple_of(device * 32, 32), 32), :]
            for b in range(4):
                at = slice(8 * b, 8 * b + 8)
                lift[at, :] = column[at] * total[80:88, b * 256 : b * 256 + 128]
                press[at, :] = total[80:88, b * 256 + 128 : (b + 1) * 256]


def shift(x, axis, size, by):
    return lax.ppermute(x, axis, [(i, (i + by) % size) for i in range(size)])


def flip(x, axis, size, bit):
    return lax.ppermute(x, axis, [(i, i ^ bit) for i in range(size)])


def per_device(bag_ids, touch_ids, elapsed, tables, accumulator, first_weight, second_weight, lift_weight, press_weight, head_weight, labels):
    f32 = lambda *shape: jax.ShapeDtypeStruct(shape, F32)
    bf16 = lambda *shape: jax.ShapeDtypeStruct(shape, BF16)
    axes = [lax.axis_index(name) for name in ("z", "xh", "core", TOWER)]
    idx = jnp.stack(axes).astype(jnp.int32)
    rank = lift_weight.shape[1]
    local = lift_weight.shape[0] // 8
    any_spec = pl.BlockSpec(memory_space=pl.ANY)

    tables_t = jnp.transpose(tables[:, 0], (0, 2, 1))
    bag = bag_ids[:, 0]
    hbm = lambda x: pltpu.with_memory_space_constraint(x, pltpu.HBM)
    *far, counts_far, decayed = call(
        pool_far_kernel,
        [f32(128, 256)] * 4 + [bf16(2, 4, 512, 256), f32(2, 64, 512)],
        [SMEM_SPEC] + [any_spec] * 4,
        [
            pltpu.VMEM((2, 4, 2048), jnp.int32),
            pltpu.VMEM((2, 128), jnp.int32),
            pltpu.VMEM((2, 128), jnp.int32),
            pltpu.VMEM((2, 64, 512), F32),
            pltpu.SemaphoreType.DMA((4,)),
        ],
        name="pool_far",
        flops=1e6,
    )(idx, hbm(bag), hbm(touch_ids[:, 0]), hbm(elapsed[:, 0]), hbm(tables_t))
    pack = call(pack_kernel, [f32(4, 128, 256)], [SMEM_SPEC] + vmem(4), name="pack", flops=1e6)
    far = [far[0]] + [shift(far[k], "z", 4, k) for k in (1, 2, 3)]
    *near, counts_near = call(
        pool_near_kernel, [f32(128, 256)] * 4 + [bf16(2, 4, 512, 256)], [SMEM_SPEC] + vmem(2), name="pool_near", flops=1e6
    )(idx, bag, decayed)
    *far, _ = lax.optimization_barrier((*far, near[0]))
    (fq_far,) = pack(idx, *far)
    x2 = flip(fq_far, "xh", 2, 1)
    near = [near[0]] + [shift(near[k], "z", 4, k) for k in (1, 2, 3)]

    _, first_weight = lax.optimization_barrier((fq_far, first_weight))
    view = first_weight.reshape(1024, 2, 8, 128).transpose(0, 2, 1, 3).reshape(1024, 16, 128)
    w1th, w1tl = pl.pallas_call(
        turn_kernel,
        grid=(8,),
        in_specs=[pl.BlockSpec((128, 16, 128), lambda i: (i, 0, 0))],
        out_specs=[pl.BlockSpec((2, 1024, 128), lambda i: (0, 0, i))] * 2,
        out_shape=[bf16(2, 1024, 1024)] * 2,
        compiler_params=pltpu.CompilerParams(vmem_limit_bytes=VMEM_LIMIT),
        cost_estimate=pl.CostEstimate(flops=int(1e6), transcendentals=0, bytes_accessed=1 << 20),
        name="turn",
    )(hbm(view))
    *near, _ = lax.optimization_barrier((*near, w1th))
    (fq_near,) = pack(idx, *near)
    y1 = flip(fq_near, "core", 2, 1)
    y2 = flip(x2, "core", 2, 1)
    x2b = flip(fq_near, "xh", 2, 1)
    y1b = flip(fq_far, "core", 2, 1)
    y2b = flip(x2b, "core", 2, 1)

    _, second_weight, lift_weight, press_weight, head_weight = lax.optimization_barrier(
        (w1th, second_weight, lift_weight, press_weight, head_weight)
    )
    second_view = second_weight.reshape(1024, 2, 2, 128).transpose(0, 2, 1, 3).reshape(1024, 4, 128)
    w2th, w2tl, lift, press, head = call(
        prepare_kernel,
        [bf16(2, 256, 1024)] * 2 + [f32(local, rank), f32(local, rank), f32(1, local)],
        [SMEM_SPEC] + [any_spec] * 3 + vmem(1),
        [pltpu.VMEM((1024, 4, 128), F32), pltpu.SemaphoreType.DMA((3,))],
        name="prepare",
        flops=1e6,
    )(idx, hbm(second_view), hbm(lift_weight), hbm(press_weight), head_weight.reshape(32, 128))

    scratch = [pltpu.VMEM((1024, 256), BF16)] * 2
    weights = (w1th, w1tl, w2th, w2tl, press, lift, head)
    hid_a, x0a, pay = call(
        lambda *refs: forward_kernel((0, 1), True, *refs),
        [f32(2, 1024, 256), f32(512, 256), f32(2 * rank + 8, 128)],
        [SMEM_SPEC] + vmem(11),
        scratch,
        name="forward_a",
        flops=1e6,
    )(idx, fq_near, x2, y1, y2, *weights)
    pay, x2b = lax.optimization_barrier((pay, x2b))
    y2b = flip(x2b, "core", 2, 1)

    def later_half(at, t):
        return call(
            lambda *refs: forward_kernel((t,), False, *refs),
            [f32(1, 1024, 256), f32(256, 256)],
            [SMEM_SPEC] + vmem(11),
            scratch,
            name="forward_b%d" % t,
            flops=4e9,
        )(at, fq_far, x2b, y1b, y2b, *weights)

    view, second_view, pay = lax.optimization_barrier((view, second_view, pay))
    other = flip(pay, TOWER, 8, 1)
    w1qh, w1ql = pl.pallas_call(
        pick_kernel,
        grid_spec=pltpu.PrefetchScalarGridSpec(
            num_scalar_prefetch=1,
            grid=(4,),
            in_specs=[pl.BlockSpec((1, 1, 64, 16, 128), lambda k, i: (lax.rem(i[0] + k, 4), 2 * i[1] + i[2], 0, 0, 0))],
            out_specs=[pl.BlockSpec((2, 64, 1024), lambda k, i: (0, k, 0))] * 2,
        ),
        out_shape=[bf16(2, 256, 1024)] * 2,
        compiler_params=pltpu.CompilerParams(vmem_limit_bytes=VMEM_LIMIT),
        cost_estimate=pl.CostEstimate(flops=int(4e9), transcendentals=0, bytes_accessed=1 << 20),
        name="pick",
    )(idx, hbm(view.reshape(4, 4, 64, 16, 128)))
    w2h, w2l = call(natural_kernel, [bf16(2, 1024, 256)] * 2, vmem(1), name="natural", flops=1e9)(second_view)
    other, w1qh, w2h = lax.optimization_barrier((other, w1qh, w2h))
    pay = pay + other
    after, pay = lax.optimization_barrier((idx, pay))
    other = flip(pay, TOWER, 8, 2)
    hid_b0, x0b0 = later_half(after, 0)
    other, x0b0 = lax.optimization_barrier((other, x0b0))
    pay = pay + other
    after, pay = lax.optimization_barrier((idx, pay))
    other = flip(pay, TOWER, 8, 4)
    hid_b1, x0b1 = later_half(after, 1)
    other, x0b1 = lax.optimization_barrier((other, x0b1))
    pay, logits = call(logit_kernel, [f32(2 * rank + 8, 128), f32(1, 16)], [SMEM_SPEC] + vmem(3), name="logit", flops=1e6)(
        idx, pay, other, labels
    )
    pays = [pay] + [flip(pay, QUAD, 4, k) for k in (1, 2, 3)]

    ghh, ghl, gout, pq, *g = call(
        grads_kernel,
        [bf16(2, 1024, 512), bf16(2, 1024, 512), f32(512, 512), f32(2 * rank, 512)] + [f32(128, 512)] * 4,
        [SMEM_SPEC] + vmem(14),
        name="grads",
        flops=9e9,
    )(idx, *pays, hid_a, hid_b0, hid_b1, w1qh, w1ql, w2h, w2l, press, lift, head)
    w = call(
        weights_kernel,
        [f32(rows, 1024) for rows in (80, 80, 80, 144, 88, 152, 88, 88)],
        [SMEM_SPEC] + vmem(14),
        name="weights",
        flops=5e9,
    )(idx, fq_near, fq_far, ghh, ghl, gout, hid_a, hid_b0, hid_b1, x0a, x0b0, x0b1, pq, g[1], g[3])
    w, v = w[:4], w[4:]
    up = shift(w[2], "z", 4, 1)
    down = shift(v[2], "z", 4, 3)
    v1 = shift(v[1], "z", 4, 1)
    w3 = shift(w[3], "z", 4, 3)
    g2 = shift(g[2], "z", 4, 2)
    w1 = shift(w[1] + up, "z", 4, 1)
    v3 = shift(v[3] + down, "z", 4, 3)
    new_tables, new_accumulator = call(
        update_kernel, [f32(2, 64, 512), f32(2, 512)], [SMEM_SPEC] + vmem(8), name="update", flops=5e9
    )(idx, g[0], v1, g2, w3, counts_near, counts_far, decayed, accumulator[:, 0])
    first, second, lift_out, press_out = call(
        sum_kernel,
        [f32(1024, 128), f32(256, 128), f32(32, rank), f32(32, rank)],
        [SMEM_SPEC] + vmem(7),
        [pltpu.VMEM((local, 128), F32)],
        name="sum",
        flops=1e6,
    )(idx, head, w[0], w1, w3, v[0], v1, v3)
    return (
        jnp.transpose(new_tables, (0, 2, 1))[:, None],
        new_accumulator[:, None],
        first.reshape(64, 8, 2, 128).transpose(0, 2, 1, 3).reshape(64, 2, 1024),
        second.reshape(64, 2, 2, 128).transpose(0, 2, 1, 3).reshape(64, 2, 256),
        lift_out,
        press_out,
        logits,
    )


def solution(mesh):
    split = Mesh(mesh.devices.reshape(4, 2, 4, 2, 2), ("y", "xl", "z", "xh", "core"))
    member = ("z", "xh", "core")
    placed = (
        P(TOWER, member, None, None),
        P(TOWER, member, None),
        P(TOWER, member, None),
        P(TOWER, member, None, None),
        P(TOWER, member, None),
        P(None, TOWER, None),
        P(None, TOWER, None),
        P(),
        P(),
        P(),
        P(member, None),
    )
    return jax.shard_map(
        per_device,
        mesh=split,
        in_specs=placed,
        out_specs=(
            P(TOWER, member, None, None),
            P(TOWER, member, None),
            P(member, TOWER, None),
            P(member, TOWER, None),
            P(TOWER + member, None),
            P(TOWER + member, None),
            P(member, TOWER),
        ),
        check_vma=False,
    )
```

```python
import math

import jax
import jax.numpy as jnp
from jax import lax
from jax.experimental import pallas as pl
from jax.experimental.pallas import tpu as pltpu
from jax.sharding import Mesh, PartitionSpec as P

DECAY_RATE = 0.98
LEARN_RATE = 1.0
EPSILON = 1e-08
F32 = jnp.float32
BF16 = jnp.bfloat16
NN = (((1,), (0,)), ((), ()))
NT = (((1,), (1,)), ((), ()))
TOWER = ("y", "xl")
QUAD = ("xh", "core")
VMEM_LIMIT = 16 << 20


def halves(a):
    high = a.astype(BF16)
    return high, (a - high.astype(F32)).astype(BF16)


def dot1(a, b, dims):
    return lax.dot_general(a, b, dims, preferred_element_type=F32)


def dot3(a, b, dims=NN):
    return dot1(a[0], b[0], dims) + (dot1(a[0], b[1], dims) + dot1(a[1], b[0], dims))


def dot32(a, b, dims=NN):
    return dot3(halves(a), halves(b), dims)


def vmem(count):
    return [pl.BlockSpec(memory_space=pltpu.VMEM)] * count


def call(kernel, outs, spec_in, scratch=(), name=None, flops=0):
    return pl.pallas_call(
        kernel,
        cost_estimate=pl.CostEstimate(flops=int(flops), transcendentals=0, bytes_accessed=1 << 20),
        out_shape=outs,
        in_specs=spec_in,
        out_specs=vmem(len(outs)),
        scratch_shapes=list(scratch),
        compiler_params=pltpu.CompilerParams(vmem_limit_bytes=VMEM_LIMIT),
        name=name,
    )


SMEM_SPEC = pl.BlockSpec(memory_space=pltpu.SMEM)


def decay(touch, elapsed, tables, decayed):
    towers, width, rows = tables.shape
    touches = touch.shape[1]
    for t in range(towers):
        ids = jnp.broadcast_to(touch[t : t + 1, :].astype(F32), (touches, touches)).T
        rates = jnp.exp(elapsed[t : t + 1, :].astype(F32) * math.log(DECAY_RATE))
        rates = jnp.broadcast_to(rates, (touches, touches)).T
        factor = []
        for block in range(rows // touches):
            row = lax.broadcasted_iota(jnp.int32, (touches, touches), 1).astype(F32) + float(block * touches)
            match = ids == row
            hits = jnp.sum(jnp.where(match, 1.0, 0.0), axis=0, keepdims=True)
            chosen = jnp.sum(jnp.where(match, rates, 0.0), axis=0, keepdims=True)
            factor.append(jnp.where(hits > 0.0, chosen, 1.0))
        decayed[t] = tables[t] * jnp.concatenate(factor, axis=1)


def pool_half(idx, side, bag, decayed, pooled, counts):
    towers, width, rows = decayed.shape
    part = pooled[0].shape[1]
    for t in range(towers):
        both = jnp.concatenate(halves(decayed[t]), axis=0)
        for k, out in enumerate(pooled):
            chunk = lax.rem(idx[0] + k, 4)
            at = pl.multiple_of(chunk * 2 * part + side * part, part)
            ids = bag[t, :, pl.ds(at, part)]
            row = lax.broadcasted_iota(jnp.int32, (rows, part), 0)
            count = jnp.zeros((rows, part), F32)
            for b in range(ids.shape[0]):
                count = count + jnp.where(row == ids[b : b + 1, :], 1.0, 0.0)
            count = count.astype(BF16)
            counts[t, chunk] = count
            total = dot1(both, count, NN)
            out[t * width : (t + 1) * width, :] = total[:width] + total[width:]


def pool_far_kernel(idx, bag_hbm, touch_hbm, elapsed_hbm, tables_hbm, p0, p1, p2, p3, counts, decayed, bag, touch, elapsed, tables, sems):
    pairs = ((bag_hbm, bag), (touch_hbm, touch), (elapsed_hbm, elapsed), (tables_hbm, tables))
    copies = [pltpu.make_async_copy(a, b, sems.at[n]) for n, (a, b) in enumerate(pairs)]
    for copy in copies:
        copy.start()
    for copy in copies:
        copy.wait()
    decay(touch, elapsed, tables, decayed)
    pool_half(idx, 1 - idx[1], bag, decayed, (p0, p1, p2, p3), counts)


def pool_near_kernel(idx, bag, decayed, p0, p1, p2, p3, counts):
    pool_half(idx, idx[1], bag, decayed, (p0, p1, p2, p3), counts)


def pack_kernel(idx, p0, p1, p2, p3, out):
    for k, ref in enumerate((p0, p1, p2, p3)):
        out[lax.rem(idx[0] + 4 - k, 4)] = ref[...]


def turn_kernel(at, w_hbm, high, low, w, sems):
    pieces, rows = w.shape[:2]
    copies = [pltpu.make_async_copy(w_hbm.at[pl.ds((at * pieces + n) * rows, rows)], w.at[n], sems.at[n]) for n in range(pieces)]
    for copy in copies:
        copy.start()
    for n, copy in enumerate(copies):
        copy.wait()
        flat = w.at[n].reshape(rows * 16, 128)
        for t in range(2):
            for b in range(8):
                h, l = halves(flat[pl.ds(b * 2 + t, rows, stride=16), :].T)
                high[t, b * 128 : (b + 1) * 128, n * rows : (n + 1) * rows] = h
                low[t, b * 128 : (b + 1) * 128, n * rows : (n + 1) * rows] = l


def pick_kernel(idx, w_hbm, high, low, w, sems):
    rows = w.shape[1]
    quad = 2 * idx[1] + idx[2]
    copies = []
    for k in range(4):
        table = lax.rem(idx[0] + k, 4) * 4 + quad
        copies.append(pltpu.make_async_copy(w_hbm.at[pl.ds(pl.multiple_of(table * rows, rows), rows)], w.at[k], sems.at[k]))
    for copy in copies:
        copy.start()
    for k, copy in enumerate(copies):
        copy.wait()
        flat = w.at[k].reshape(rows * 16, 128)
        for t in range(2):
            for b in range(8):
                h, l = halves(flat[pl.ds(b * 2 + t, rows, stride=16), :])
                high[t, k * rows : (k + 1) * rows, b * 128 : (b + 1) * 128] = h
                low[t, k * rows : (k + 1) * rows, b * 128 : (b + 1) * 128] = l


def prepare_kernel(idx, second_hbm, lift_hbm, press_hbm, heads, high_t, low_t, lift, press, head, second, sems):
    tower = idx[3]
    rows = pl.ds(pl.multiple_of(tower * lift.shape[0], lift.shape[0]), lift.shape[0])
    pairs = ((second_hbm, second), (lift_hbm.at[rows, :], lift), (press_hbm.at[rows, :], press))
    copies = [pltpu.make_async_copy(a, b, sems.at[n]) for n, (a, b) in enumerate(pairs)]
    for copy in copies:
        copy.start()
    head[...] = jnp.concatenate([heads[pl.ds(tower * 4 + b, 1), :] for b in range(4)], axis=1)
    for copy in copies:
        copy.wait()
    count = second.shape[0]
    flat = second.reshape(count * 4, 128)
    for t in range(2):
        for b in range(2):
            lanes = slice(b * 128, (b + 1) * 128)
            h, l = halves(flat[pl.ds(b * 2 + t, count, stride=4), :].T)
            high_t[t, lanes, :] = h
            low_t[t, lanes, :] = l


def natural_kernel(w, high, low):
    rows = w.shape[0]
    flat = w.reshape(rows * 4, 128)
    for t in range(2):
        for b in range(2):
            lanes = slice(b * 128, (b + 1) * 128)
            h, l = halves(flat[pl.ds(b * 2 + t, rows, stride=4), :])
            high[t, :, lanes] = h
            low[t, :, lanes] = l


def forward_kernel(towers, with_pay, idx, x1, x2, y1, y2, w1ha, w1la, w1hb, w1lb, w2h, w2l, press, lift, head, hidden, start, *rest):
    fh, fl = rest[-2:]
    sets = (x1, x2, y1, y2)
    zs, pair, samples = x1.shape
    width = pair // 2
    xh, core = idx[1], idx[2]
    place = ((xh, core), (1 - xh, core), (xh, 1 - core), (1 - xh, 1 - core))
    width_out = w2h.shape[1]

    def one_tower(t, slot):
        for (a, b), ref in zip(place, sets):
            for z in range(zs):
                h, l = halves(ref[z, pl.ds(pl.multiple_of(t * width, width), width), :])
                at = pl.multiple_of(((z * 2 + a) * 2 + b) * width, width)
                fh[pl.ds(at, width), :] = h
                fl[pl.ds(at, width), :] = l
        deep = w1ha.shape[2]
        value = dot3((w1ha[t], w1la[t]), (fh[0:deep, :], fl[0:deep, :]))
        value = value + dot3((w1hb[t], w1lb[t]), (fh[deep:, :], fl[deep:, :]))
        hidden[slot] = value
        act = halves(value * jax.nn.sigmoid(value))
        start[pl.ds(pl.multiple_of(slot * width_out, width_out), width_out), :] = dot3((w2h[t], w2l[t]), act)

    if len(towers) == 2:

        def step(t, carry):
            one_tower(t, t)
            return carry

        lax.fori_loop(0, 2, step, 0)
    else:
        one_tower(towers[0], 0)
    if with_pay:
        pay = rest[0]
        own = samples // 2
        rank = press.shape[1]
        x0 = halves(start[:, pl.ds(pl.multiple_of(core * own, own), own)])
        p = dot3(halves(press[...].T), x0)
        q = dot3(halves(lift[...].T * head[...]), x0)
        d = dot3(halves(jnp.broadcast_to(head[...], (8, head.shape[1]))), x0)
        pay[0:rank, :] = p
        pay[rank : 2 * rank, :] = q
        pay[2 * rank : 2 * rank + 8, :] = d


def logit_kernel(idx, mine, other, labels, pay, logits):
    total = mine[...] + other[...]
    rank = (total.shape[0] - 8) // 2
    value = jnp.sum(total[0:rank] * total[rank : 2 * rank], axis=0, keepdims=True) + total[2 * rank : 2 * rank + 1]
    turned = pltpu.roll(jnp.broadcast_to(value, (8, 128)), lax.rem(128 - 16 * idx[3], 128), 1)
    logits[...] = turned[0:1, 0:16]
    error = jax.nn.sigmoid(value) - labels[...].astype(F32)
    pay[0 : 2 * rank, :] = total[0 : 2 * rank]
    pay[2 * rank : 2 * rank + 8, :] = jnp.broadcast_to(error, (8, error.shape[1]))


def grads_kernel(towers, with_pq, idx, mine, other, hidden, w1h, w1l, w2h, w2l, press, lift, head, ghh, ghl, gout, g0, g1, g2, g3, *pq):
    rank = press.shape[1]
    width = w1h.shape[1] // 4
    width_out = w2h.shape[2]
    first_core = idx[2] == 0
    left = jnp.where(first_core, mine[...], other[...])
    right = jnp.where(first_core, other[...], mine[...])
    both = jnp.concatenate([left, right], axis=1)
    error = both[2 * rank : 2 * rank + 1]
    if with_pq:
        pq[0][...] = error * both[0 : 2 * rank]
    p, q = halves(both[0:rank]), halves(both[rank : 2 * rank])
    column = jnp.broadcast_to(head[...], (128, head.shape[1])).T[:, 0:1]
    for slot, t in enumerate(towers):
        rows = slice(t * width_out, (t + 1) * width_out)
        scaling = dot3(halves(lift[rows, :]), p)
        back = dot3(halves(press[rows, :]), q)
        go = error * (column[rows] * (scaling + 1.0) + back)
        gout[slot] = go
        ga = dot3((w2h[t], w2l[t]), halves(go))
        value = hidden[slot]
        s = jax.nn.sigmoid(value)
        gh = halves(ga * (s * (1.0 + value * (1.0 - s))))
        ghh[slot] = gh[0]
        ghl[slot] = gh[1]
        grad = dot3((w1h[t], w1l[t]), gh)
        for k, out in enumerate((g0, g1, g2, g3)):
            out[slot] = grad[k * width : (k + 1) * width]


def weights_kernel(t, riders, idx, near, far, ghha, ghla, ghhb, ghlb, gouta, goutb, hid_a, hid_b, *rest):
    if t == 1:
        rest, far_block = rest[:-1], rest[-1]
    blocks, rest = rest[-4:], rest[:-4]
    z, quad = idx[0], 2 * idx[1] + idx[2]
    width = near.shape[1] // 2
    rows = slice(t * width, (t + 1) * width)
    fa, fb, acta, actb = [], [], [], []
    for k in range(4):
        at = lax.rem(z + k, 4)
        fa.append(near[at, rows, :])
        fb.append(far[at, rows, :])
        pick = pl.ds(pl.multiple_of((at * 4 + quad) * width, width), width)
        value = hid_a[t, pick, :]
        acta.append(value * jax.nn.sigmoid(value))
        value = hid_b[0, pick, :]
        actb.append(value * jax.nn.sigmoid(value))
    join = lambda parts: halves(jnp.concatenate(parts, axis=0))
    grad = dot3(join(fa), (ghha[t], ghla[t]), NT) + dot3(join(fb), (ghhb[0], ghlb[0]), NT)
    for k in range(4):
        blocks[k][0:width, :] = grad[k * width : (k + 1) * width]
    grad = dot3(join(acta), halves(gouta[t]), NT) + dot3(join(actb), halves(goutb[0]), NT)
    for k in range(4):
        for b in range(4):
            blocks[k][width : width + 16, b * 256 : (b + 1) * 256] = grad[k * width + 16 * b : k * width + 16 * b + 16]
    low = width // 2
    for n, k in enumerate(riders):
        ga, gb = rest[2 * n], rest[2 * n + 1]
        base = blocks[k].shape[0] - low
        blocks[k][base:, 0:256] = ga[t, 0:low, :]
        blocks[k][base:, 256:512] = gb[0, 0:low, :]
        blocks[k][base:, 512:768] = ga[t, low:, :]
        blocks[k][base:, 768:1024] = gb[0, low:, :]
    if t == 1:
        x0a, x0b0, x0b1, pqa, pqb, ga, gb0, gb1 = rest[4:]
        for n, gb in enumerate((gb0, gb1)):
            for b in range(2):
                part = slice(b * low, (b + 1) * low)
                far_block[n * low : (n + 1) * low, b * 512 : b * 512 + 256] = ga[n, part, :]
                far_block[n * low : (n + 1) * low, b * 512 + 256 : (b + 1) * 512] = gb[0, part, :]
        parts_a, parts_b = [], []
        for k in range(4):
            block = lax.rem(z + k, 4) * 4 + quad
            parts_a.append(x0a[pl.ds(pl.multiple_of(block * 32, 32), 32), :])
            inner = pl.ds(pl.multiple_of(lax.rem(block, 8) * 32, 32), 32)
            parts_b.append(jnp.where(block < 8, x0b0[inner, :], x0b1[inner, :]))
        both = dot3(join(parts_a), halves(pqa[...]), NT) + dot3(join(parts_b), halves(pqb[...]), NT)
        for k in range(4):
            for b in range(4):
                blocks[k][width + 16 : width + 24, b * 256 : (b + 1) * 256] = both[32 * k + 8 * b : 32 * k + 8 * b + 8]


def update_kernel(idx, ga, gb0, gb1, w_up, w_down, v_up, v_down, opposite, near, far, decayed, accumulator, new_tables, new_accumulator):
    z = idx[0]
    towers, width, rows = decayed.shape
    low = width // 2

    def rider(ref, start=None):
        start = ref.shape[0] - low if start is None else start
        block = ref[start : start + low, :]
        return (
            jnp.concatenate([block[:, 0:256], block[:, 512:768]], axis=0),
            jnp.concatenate([block[:, 256:512], block[:, 768:1024]], axis=0),
        )

    for t in range(towers):
        gb = (gb0, gb1)[t]
        pieces = (
            (ga[t], gb[0]),
            rider((w_up, v_up)[t]),
            rider(opposite, low * t),
            rider((w_down, v_down)[t]),
        )
        total = jnp.zeros((2 * width, rows), F32)
        for k, (a, b) in enumerate(pieces):
            at = lax.rem(z + 4 - k, 4)
            total = total + dot1(jnp.concatenate(halves(a), axis=0), near[t, at], NT)
            total = total + dot1(jnp.concatenate(halves(b), axis=0), far[t, at], NT)
        grad = total[:width] + total[width:]
        square = jnp.sum(grad * grad, axis=0, keepdims=True) * (1.0 / width)
        fresh = accumulator[t : t + 1, :] + square
        new_accumulator[t : t + 1, :] = fresh
        new_tables[t] = decayed[t] - LEARN_RATE * grad / (jnp.sqrt(fresh) + EPSILON)


def sum_kernel(idx, head, *refs):
    parts, (first, second, lift, press, wide) = refs[:6], refs[6:]
    for t in range(2):
        a, b, c = parts[3 * t : 3 * t + 3]
        total = a[...] + (b[0 : a.shape[0]] + c[0 : a.shape[0]])
        for k in range(8):
            first[pl.ds(2 * k + t, 64, stride=16), :] = total[0:64, k * 128 : (k + 1) * 128]
        for b in range(4):
            for o in range(2):
                lanes = slice(b * 256 + o * 128, b * 256 + (o + 1) * 128)
                second[pl.ds(b * 64 + 2 * o + t, 16, stride=4), :] = total[64:80, lanes]
        if t == 1:
            wide[...] = jnp.broadcast_to(head[...], (128, head.shape[1])).T
            device = (idx[0] * 2 + idx[1]) * 2 + idx[2]
            column = wide[pl.ds(pl.multiple_of(device * 32, 32), 32), :]
            for b in range(4):
                at = slice(8 * b, 8 * b + 8)
                lift[at, :] = column[at] * total[80:88, b * 256 : b * 256 + 128]
                press[at, :] = total[80:88, b * 256 + 128 : (b + 1) * 256]


def shift(x, axis, size, by):
    return lax.ppermute(x, axis, [(i, (i + by) % size) for i in range(size)])


def flip(x, axis, size, bit):
    return lax.ppermute(x, axis, [(i, i ^ bit) for i in range(size)])


def per_device(bag_ids, touch_ids, elapsed, tables, accumulator, first_weight, second_weight, lift_weight, press_weight, head_weight, labels):
    f32 = lambda *shape: jax.ShapeDtypeStruct(shape, F32)
    bf16 = lambda *shape: jax.ShapeDtypeStruct(shape, BF16)
    axes = [lax.axis_index(name) for name in ("z", "xh", "core", TOWER)]
    idx = jnp.stack(axes).astype(jnp.int32)
    rank = lift_weight.shape[1]
    local = lift_weight.shape[0] // 8
    any_spec = pl.BlockSpec(memory_space=pl.ANY)

    tables_t = jnp.transpose(tables[:, 0], (0, 2, 1))
    bag = bag_ids[:, 0]
    hbm = lambda x: pltpu.with_memory_space_constraint(x, pltpu.HBM)
    *far, counts_far, decayed = call(
        pool_far_kernel,
        [f32(128, 256)] * 4 + [bf16(2, 4, 512, 256), f32(2, 64, 512)],
        [SMEM_SPEC] + [any_spec] * 4,
        [
            pltpu.VMEM((2, 4, 2048), jnp.int32),
            pltpu.VMEM((2, 128), jnp.int32),
            pltpu.VMEM((2, 128), jnp.int32),
            pltpu.VMEM((2, 64, 512), F32),
            pltpu.SemaphoreType.DMA((4,)),
        ],
        name="pool_far",
        flops=1e6,
    )(idx, hbm(bag), hbm(touch_ids[:, 0]), hbm(elapsed[:, 0]), hbm(tables_t))
    pack = call(pack_kernel, [f32(4, 128, 256)], [SMEM_SPEC] + vmem(4), name="pack", flops=1e6)
    far = [far[0]] + [shift(far[k], "z", 4, k) for k in (1, 2, 3)]
    *near, counts_near = call(
        pool_near_kernel, [f32(128, 256)] * 4 + [bf16(2, 4, 512, 256)], [SMEM_SPEC] + vmem(2), name="pool_near", flops=1e6
    )(idx, bag, decayed)
    view = first_weight.reshape(1024, 2, 8, 128).transpose(0, 2, 1, 3).reshape(1024, 16, 128)

    def turn(view, at):
        return pl.pallas_call(
            lambda *refs: turn_kernel(at, *refs),
            in_specs=[any_spec],
            out_specs=vmem(2),
            out_shape=[bf16(2, 1024, 512)] * 2,
            scratch_shapes=[pltpu.VMEM((4, 128, 16, 128), F32), pltpu.SemaphoreType.DMA((4,))],
            compiler_params=pltpu.CompilerParams(vmem_limit_bytes=VMEM_LIMIT),
            cost_estimate=pl.CostEstimate(flops=int(1e6), transcendentals=0, bytes_accessed=1 << 20),
            name="turn_%d" % at,
        )(hbm(view))

    view, _ = lax.optimization_barrier((view, decayed))
    w1ha, w1la = turn(view, 0)
    *far, _, _ = lax.optimization_barrier((*far, near[0], w1ha))
    (fq_far,) = pack(idx, *far)
    x2 = flip(fq_far, "xh", 2, 1)
    near = [near[0]] + [shift(near[k], "z", 4, k) for k in (1, 2, 3)]
    view, _ = lax.optimization_barrier((view, fq_far))
    w1hb, w1lb = turn(view, 1)
    *near, _ = lax.optimization_barrier((*near, w1hb))
    (fq_near,) = pack(idx, *near)
    y1 = flip(fq_near, "core", 2, 1)
    y2 = flip(x2, "core", 2, 1)
    x2b = flip(fq_near, "xh", 2, 1)
    y1b = flip(fq_far, "core", 2, 1)
    y2b = flip(x2b, "core", 2, 1)

    _, second_weight, lift_weight, press_weight, head_weight = lax.optimization_barrier(
        (w1hb, second_weight, lift_weight, press_weight, head_weight)
    )
    second_view = second_weight.reshape(1024, 2, 2, 128).transpose(0, 2, 1, 3).reshape(1024, 4, 128)
    w2th, w2tl, lift, press, head = call(
        prepare_kernel,
        [bf16(2, 256, 1024)] * 2 + [f32(local, rank), f32(local, rank), f32(1, local)],
        [SMEM_SPEC] + [any_spec] * 3 + vmem(1),
        [pltpu.VMEM((1024, 4, 128), F32), pltpu.SemaphoreType.DMA((3,))],
        name="prepare",
        flops=1e6,
    )(idx, hbm(second_view), hbm(lift_weight), hbm(press_weight), head_weight.reshape(32, 128))

    scratch = [pltpu.VMEM((1024, 256), BF16)] * 2
    weights = (w1ha, w1la, w1hb, w1lb, w2th, w2tl, press, lift, head)
    hid_a, x0a, pay = call(
        lambda *refs: forward_kernel((0, 1), True, *refs),
        [f32(2, 1024, 256), f32(512, 256), f32(2 * rank + 8, 128)],
        [SMEM_SPEC] + vmem(13),
        scratch,
        name="forward_a",
        flops=1e6,
    )(idx, fq_near, x2, y1, y2, *weights)

    def later_half(at, t, y2b):
        return call(
            lambda *refs: forward_kernel((t,), False, *refs),
            [f32(1, 1024, 256), f32(256, 256)],
            [SMEM_SPEC] + vmem(13),
            scratch,
            name="forward_b%d" % t,
            flops=4e9,
        )(at, fq_far, x2b, y1b, y2b, *weights)

    view, second_view, pay = lax.optimization_barrier((view, second_view, pay))
    other = flip(pay, TOWER, 8, 1)
    w1qh, w1ql = call(
        pick_kernel,
        [bf16(2, 256, 1024)] * 2,
        [SMEM_SPEC, any_spec],
        [pltpu.VMEM((4, 64, 16, 128), F32), pltpu.SemaphoreType.DMA((4,))],
        name="pick",
        flops=1e6,
    )(idx, hbm(view))
    w2h, w2l = call(natural_kernel, [bf16(2, 1024, 256)] * 2, vmem(1), name="natural", flops=1e6)(second_view)
    other, w1qh, w2h, x2b = lax.optimization_barrier((other, w1qh, w2h, x2b))
    pay = pay + other
    after, pay = lax.optimization_barrier((idx, pay))
    other = flip(pay, TOWER, 8, 2)
    y2b = flip(x2b, "core", 2, 1)
    hid_b0, x0b0 = later_half(after, 0, y2b)
    other, x0b0 = lax.optimization_barrier((other, x0b0))
    pay = pay + other
    after, pay = lax.optimization_barrier((idx, pay))
    other = flip(pay, TOWER, 8, 4)
    hid_b1, x0b1 = later_half(after, 1, y2b)
    other, x0b1 = lax.optimization_barrier((other, x0b1))
    pay, logits = call(logit_kernel, [f32(2 * rank + 8, 128), f32(1, 16)], [SMEM_SPEC] + vmem(3), name="logit", flops=1e6)(
        idx, pay, other, labels
    )
    c1 = flip(pay, "core", 2, 1)
    xa = flip(pay, "xh", 2, 1)

    def grads(towers, with_pq, mine, other, hidden, name):
        n = len(towers)
        return call(
            lambda *refs: grads_kernel(towers, with_pq, *refs),
            [bf16(n, 1024, 256)] * 2 + [f32(n, 256, 256)] + [f32(n, 64, 256)] * 4 + [f32(2 * rank, 256)] * with_pq,
            [SMEM_SPEC] + vmem(10),
            name=name,
            flops=4e9,
        )(idx, mine, other, hidden, w1qh, w1ql, w2h, w2l, press, lift, head)

    ghha, ghla, gouta, *ga, pqa = grads((0, 1), True, pay, c1, hid_a, "grads_a")

    xa, pqa = lax.optimization_barrier((xa, pqa))
    xb = flip(xa, "core", 2, 1)

    def weights_of(t, riders, rows, ghhb, ghlb, goutb, hid_b, extra):
        return call(
            lambda *refs: weights_kernel(t, riders, *refs),
            [f32(n, 1024) for n in rows],
            [SMEM_SPEC] + vmem(10 + len(extra)),
            name="weights_%d" % t,
            flops=3e9,
        )(idx, fq_near, fq_far, ghha, ghla, ghhb, ghlb, gouta, goutb, hid_a, hid_b, *extra)

    ghh0, ghl0, gout0, *gb0, pqb = grads((0,), True, xa, xb, hid_b0, "grads_b0")
    w = weights_of(0, (2, 3), (80, 80, 112, 112), ghh0, ghl0, gout0, hid_b0, (ga[1], gb0[1], ga[3], gb0[3]))
    up = shift(w[2], "z", 4, 1)
    w3 = shift(w[3], "z", 4, 3)
    ghh1, ghl1, gout1, *gb1 = grads((1,), False, xa, xb, hid_b1, "grads_b1")
    v = weights_of(
        1,
        (1, 2),
        (88, 120, 120, 88, 64),
        ghh1,
        ghl1,
        gout1,
        hid_b1,
        (ga[1], gb1[1], ga[3], gb1[3], x0a, x0b0, x0b1, pqa, pqb, ga[2], gb0[2], gb1[2]),
    )
    down = shift(v[2], "z", 4, 3)
    v1 = shift(v[1], "z", 4, 1)
    g2 = shift(v[4], "z", 4, 2)
    up, w3 = lax.optimization_barrier((up, w3))
    down, v1 = lax.optimization_barrier((down, v1))
    w1 = shift(w[1] + up[0:80], "z", 4, 1)
    v3 = shift(v[3] + down[0:88], "z", 4, 3)
    new_tables, new_accumulator = call(
        update_kernel, [f32(2, 64, 512), f32(2, 512)], [SMEM_SPEC] + vmem(12), name="update", flops=5e9
    )(idx, ga[0], gb0[0], gb1[0], up, w3, v1, down, g2, counts_near, counts_far, decayed, accumulator[:, 0])
    first, second, lift_out, press_out = call(
        sum_kernel,
        [f32(1024, 128), f32(256, 128), f32(32, rank), f32(32, rank)],
        [SMEM_SPEC] + vmem(7),
        [pltpu.VMEM((local, 128), F32)],
        name="sum",
        flops=1e6,
    )(idx, head, w[0], w1, w3, v[0], v1, v3)
    return (
        jnp.transpose(new_tables, (0, 2, 1))[:, None],
        new_accumulator[:, None],
        first.reshape(64, 8, 2, 128).transpose(0, 2, 1, 3).reshape(64, 2, 1024),
        second.reshape(64, 2, 2, 128).transpose(0, 2, 1, 3).reshape(64, 2, 256),
        lift_out,
        press_out,
        logits,
    )


def solution(mesh):
    split = Mesh(mesh.devices.reshape(4, 2, 4, 2, 2), ("y", "xl", "z", "xh", "core"))
    member = ("z", "xh", "core")
    placed = (
        P(TOWER, member, None, None),
        P(TOWER, member, None),
        P(TOWER, member, None),
        P(TOWER, member, None, None),
        P(TOWER, member, None),
        P(None, TOWER, None),
        P(None, TOWER, None),
        P(),
        P(),
        P(),
        P(member, None),
    )
    return jax.shard_map(
        per_device,
        mesh=split,
        in_specs=placed,
        out_specs=(
            P(TOWER, member, None, None),
            P(TOWER, member, None),
            P(member, TOWER, None),
            P(member, TOWER, None),
            P(TOWER + member, None),
            P(TOWER + member, None),
            P(member, TOWER),
        ),
        check_vma=False,
    )
```

```python
import math

import jax
import jax.numpy as jnp
from jax import lax
from jax.experimental import pallas as pl
from jax.experimental.pallas import tpu as pltpu
from jax.sharding import Mesh, PartitionSpec as P

DECAY_RATE = 0.98
LEARN_RATE = 1.0
EPSILON = 1e-08
F32 = jnp.float32
BF16 = jnp.bfloat16
NN = (((1,), (0,)), ((), ()))
NT = (((1,), (1,)), ((), ()))
TOWER = ("y", "xl")
QUAD = ("xh", "core")
VMEM_LIMIT = 16 << 20


def halves(a):
    high = a.astype(BF16)
    return high, (a - high.astype(F32)).astype(BF16)


def dot1(a, b, dims):
    return lax.dot_general(a, b, dims, preferred_element_type=F32)


def dot3(a, b, dims=NN):
    return dot1(a[0], b[0], dims) + (dot1(a[0], b[1], dims) + dot1(a[1], b[0], dims))


def dot32(a, b, dims=NN):
    return dot3(halves(a), halves(b), dims)


def vmem(count):
    return [pl.BlockSpec(memory_space=pltpu.VMEM)] * count


def call(kernel, outs, spec_in, scratch=(), name=None, flops=0):
    return pl.pallas_call(
        kernel,
        cost_estimate=pl.CostEstimate(flops=int(flops), transcendentals=0, bytes_accessed=1 << 20),
        out_shape=outs,
        in_specs=spec_in,
        out_specs=vmem(len(outs)),
        scratch_shapes=list(scratch),
        compiler_params=pltpu.CompilerParams(vmem_limit_bytes=VMEM_LIMIT),
        name=name,
    )


SMEM_SPEC = pl.BlockSpec(memory_space=pltpu.SMEM)


def decay(touch, elapsed, tables, decayed):
    towers, width, rows = tables.shape
    touches = touch.shape[1]
    for t in range(towers):
        ids = jnp.broadcast_to(touch[t : t + 1, :].astype(F32), (touches, touches)).T
        rates = jnp.exp(elapsed[t : t + 1, :].astype(F32) * math.log(DECAY_RATE))
        rates = jnp.broadcast_to(rates, (touches, touches)).T
        factor = []
        for block in range(rows // touches):
            row = lax.broadcasted_iota(jnp.int32, (touches, touches), 1).astype(F32) + float(block * touches)
            match = ids == row
            hits = jnp.sum(jnp.where(match, 1.0, 0.0), axis=0, keepdims=True)
            chosen = jnp.sum(jnp.where(match, rates, 0.0), axis=0, keepdims=True)
            factor.append(jnp.where(hits > 0.0, chosen, 1.0))
        decayed[t] = tables[t] * jnp.concatenate(factor, axis=1)


def pool_half(idx, side, bag, decayed, pooled, counts):
    towers, width, rows = decayed.shape
    part = pooled[0].shape[1]
    for t in range(towers):
        both = jnp.concatenate(halves(decayed[t]), axis=0)
        for k, out in enumerate(pooled):
            chunk = lax.rem(idx[0] + k, 4)
            at = pl.multiple_of(chunk * 2 * part + side * part, part)
            ids = bag[t, :, pl.ds(at, part)]
            row = lax.broadcasted_iota(jnp.int32, (rows, part), 0)
            count = jnp.zeros((rows, part), F32)
            for b in range(ids.shape[0]):
                count = count + jnp.where(row == ids[b : b + 1, :], 1.0, 0.0)
            count = count.astype(BF16)
            counts[t, chunk] = count
            total = dot1(both, count, NN)
            out[t * width : (t + 1) * width, :] = total[:width] + total[width:]


def pool_far_kernel(idx, bag_hbm, touch_hbm, elapsed_hbm, tables_hbm, p0, p1, p2, p3, counts, decayed, bag, touch, elapsed, tables, sems):
    pairs = ((bag_hbm, bag), (touch_hbm, touch), (elapsed_hbm, elapsed), (tables_hbm, tables))
    copies = [pltpu.make_async_copy(a, b, sems.at[n]) for n, (a, b) in enumerate(pairs)]
    for copy in copies:
        copy.start()
    for copy in copies:
        copy.wait()
    decay(touch, elapsed, tables, decayed)
    pool_half(idx, 1 - idx[1], bag, decayed, (p0, p1, p2, p3), counts)


def pool_near_kernel(idx, bag, decayed, p0, p1, p2, p3, counts):
    pool_half(idx, idx[1], bag, decayed, (p0, p1, p2, p3), counts)


def pack_kernel(idx, p0, p1, p2, p3, out):
    for k, ref in enumerate((p0, p1, p2, p3)):
        out[lax.rem(idx[0] + 4 - k, 4)] = ref[...]


def turn_kernel(at, w_hbm, high, low, w, sems):
    pieces, rows = w.shape[:2]
    copies = [pltpu.make_async_copy(w_hbm.at[pl.ds((at * pieces + n) * rows, rows)], w.at[n], sems.at[n]) for n in range(pieces)]
    for copy in copies:
        copy.start()
    for n, copy in enumerate(copies):
        copy.wait()
        flat = w.at[n].reshape(rows * 16, 128)
        for t in range(2):
            for b in range(8):
                h, l = halves(flat[pl.ds(b * 2 + t, rows, stride=16), :].T)
                high[t, b * 128 : (b + 1) * 128, n * rows : (n + 1) * rows] = h
                low[t, b * 128 : (b + 1) * 128, n * rows : (n + 1) * rows] = l


def pick_kernel(idx, w_hbm, high, low, w, sems):
    rows = w.shape[1]
    quad = 2 * idx[1] + idx[2]
    copies = []
    for k in range(4):
        table = lax.rem(idx[0] + k, 4) * 4 + quad
        copies.append(pltpu.make_async_copy(w_hbm.at[pl.ds(pl.multiple_of(table * rows, rows), rows)], w.at[k], sems.at[k]))
    for copy in copies:
        copy.start()
    for k, copy in enumerate(copies):
        copy.wait()
        flat = w.at[k].reshape(rows * 16, 128)
        for t in range(2):
            for b in range(8):
                h, l = halves(flat[pl.ds(b * 2 + t, rows, stride=16), :])
                high[t, k * rows : (k + 1) * rows, b * 128 : (b + 1) * 128] = h
                low[t, k * rows : (k + 1) * rows, b * 128 : (b + 1) * 128] = l


def prepare_kernel(idx, second, lift_hbm, press_hbm, heads, high_t, low_t, lift, press, head, sems):
    tower = idx[3]
    rows = pl.ds(pl.multiple_of(tower * lift.shape[0], lift.shape[0]), lift.shape[0])
    pairs = ((lift_hbm.at[rows, :], lift), (press_hbm.at[rows, :], press))
    copies = [pltpu.make_async_copy(a, b, sems.at[n]) for n, (a, b) in enumerate(pairs)]
    for copy in copies:
        copy.start()
    head[...] = jnp.concatenate([heads[pl.ds(tower * 4 + b, 1), :] for b in range(4)], axis=1)
    count = second.shape[0]
    flat = second.reshape(count * 4, 128)
    for t in range(2):
        for b in range(2):
            lanes = slice(b * 128, (b + 1) * 128)
            h, l = halves(flat[pl.ds(b * 2 + t, count, stride=4), :].T)
            high_t[t, lanes, :] = h
            low_t[t, lanes, :] = l
    for copy in copies:
        copy.wait()


def natural_kernel(w, high, low):
    rows = w.shape[0]
    flat = w.reshape(rows * 4, 128)
    for t in range(2):
        for b in range(2):
            lanes = slice(b * 128, (b + 1) * 128)
            h, l = halves(flat[pl.ds(b * 2 + t, rows, stride=4), :])
            high[t, :, lanes] = h
            low[t, :, lanes] = l


def forward_kernel(towers, with_pay, idx, x1, x2, y1, y2, w1ha, w1la, w1hb, w1lb, w2h, w2l, press, lift, head, hidden, start, *rest):
    fh, fl = rest[-2:]
    sets = (x1, x2, y1, y2)
    zs, pair, samples = x1.shape
    width = pair // 2
    xh, core = idx[1], idx[2]
    place = ((xh, core), (1 - xh, core), (xh, 1 - core), (1 - xh, 1 - core))
    width_out = w2h.shape[1]

    def one_tower(t, slot):
        for (a, b), ref in zip(place, sets):
            for z in range(zs):
                h, l = halves(ref[z, pl.ds(pl.multiple_of(t * width, width), width), :])
                at = pl.multiple_of(((z * 2 + a) * 2 + b) * width, width)
                fh[pl.ds(at, width), :] = h
                fl[pl.ds(at, width), :] = l
        deep = w1ha.shape[2]
        value = dot3((w1ha[t], w1la[t]), (fh[0:deep, :], fl[0:deep, :]))
        value = value + dot3((w1hb[t], w1lb[t]), (fh[deep:, :], fl[deep:, :]))
        hidden[slot] = value
        act = halves(value * jax.nn.sigmoid(value))
        start[pl.ds(pl.multiple_of(slot * width_out, width_out), width_out), :] = dot3((w2h[t], w2l[t]), act)

    if len(towers) == 2:

        def step(t, carry):
            one_tower(t, t)
            return carry

        lax.fori_loop(0, 2, step, 0)
    else:
        one_tower(towers[0], 0)
    if with_pay:
        pay = rest[0]
        own = samples // 2
        rank = press.shape[1]
        x0 = halves(start[:, pl.ds(pl.multiple_of(core * own, own), own)])
        p = dot3(halves(press[...].T), x0)
        q = dot3(halves(lift[...].T * head[...]), x0)
        d = dot3(halves(jnp.broadcast_to(head[...], (8, head.shape[1]))), x0)
        pay[0:rank, :] = p
        pay[rank : 2 * rank, :] = q
        pay[2 * rank : 2 * rank + 8, :] = d


def logit_kernel(idx, mine, other, labels, pay, logits):
    total = mine[...] + other[...]
    rank = (total.shape[0] - 8) // 2
    value = jnp.sum(total[0:rank] * total[rank : 2 * rank], axis=0, keepdims=True) + total[2 * rank : 2 * rank + 1]
    turned = pltpu.roll(jnp.broadcast_to(value, (8, 128)), lax.rem(128 - 16 * idx[3], 128), 1)
    logits[...] = turned[0:1, 0:16]
    error = jax.nn.sigmoid(value) - labels[...].astype(F32)
    pay[0 : 2 * rank, :] = total[0 : 2 * rank]
    pay[2 * rank : 2 * rank + 8, :] = jnp.broadcast_to(error, (8, error.shape[1]))


def grads_kernel(towers, with_pq, idx, mine, other, hidden, w1h, w1l, w2h, w2l, press, lift, head, ghh, ghl, gout, g0, g1, g2, g3, *pq):
    rank = press.shape[1]
    width = w1h.shape[1] // 4
    width_out = w2h.shape[2]
    first_core = idx[2] == 0
    left = jnp.where(first_core, mine[...], other[...])
    right = jnp.where(first_core, other[...], mine[...])
    both = jnp.concatenate([left, right], axis=1)
    error = both[2 * rank : 2 * rank + 1]
    if with_pq:
        pq[0][...] = error * both[0 : 2 * rank]
    p, q = halves(both[0:rank]), halves(both[rank : 2 * rank])
    column = jnp.broadcast_to(head[...], (128, head.shape[1])).T[:, 0:1]
    for slot, t in enumerate(towers):
        rows = slice(t * width_out, (t + 1) * width_out)
        scaling = dot3(halves(lift[rows, :]), p)
        back = dot3(halves(press[rows, :]), q)
        go = error * (column[rows] * (scaling + 1.0) + back)
        gout[slot] = go
        ga = dot3((w2h[t], w2l[t]), halves(go))
        value = hidden[slot]
        s = jax.nn.sigmoid(value)
        gh = halves(ga * (s * (1.0 + value * (1.0 - s))))
        ghh[slot] = gh[0]
        ghl[slot] = gh[1]
        grad = dot3((w1h[t], w1l[t]), gh)
        for k, out in enumerate((g0, g1, g2, g3)):
            out[slot] = grad[k * width : (k + 1) * width]


def weights_kernel(t, riders, idx, near, far, ghha, ghla, ghhb, ghlb, gouta, goutb, hid_a, hid_b, *rest):
    if t == 1:
        rest, far_block = rest[:-1], rest[-1]
    blocks, rest = rest[-4:], rest[:-4]
    z, quad = idx[0], 2 * idx[1] + idx[2]
    width = near.shape[1] // 2
    rows = slice(t * width, (t + 1) * width)
    fa, fb, acta, actb = [], [], [], []
    for k in range(4):
        at = lax.rem(z + k, 4)
        fa.append(near[at, rows, :])
        fb.append(far[at, rows, :])
        pick = pl.ds(pl.multiple_of((at * 4 + quad) * width, width), width)
        value = hid_a[t, pick, :]
        acta.append(value * jax.nn.sigmoid(value))
        value = hid_b[0, pick, :]
        actb.append(value * jax.nn.sigmoid(value))
    join = lambda parts: halves(jnp.concatenate(parts, axis=0))
    grad = dot3(join(fa), (ghha[t], ghla[t]), NT) + dot3(join(fb), (ghhb[0], ghlb[0]), NT)
    for k in range(4):
        blocks[k][0:width, :] = grad[k * width : (k + 1) * width]
    grad = dot3(join(acta), halves(gouta[t]), NT) + dot3(join(actb), halves(goutb[0]), NT)
    for k in range(4):
        for b in range(4):
            blocks[k][width : width + 16, b * 256 : (b + 1) * 256] = grad[k * width + 16 * b : k * width + 16 * b + 16]
    low = width // 2
    for n, k in enumerate(riders):
        ga, gb = rest[2 * n], rest[2 * n + 1]
        base = blocks[k].shape[0] - low
        blocks[k][base:, 0:256] = ga[t, 0:low, :]
        blocks[k][base:, 256:512] = gb[0, 0:low, :]
        blocks[k][base:, 512:768] = ga[t, low:, :]
        blocks[k][base:, 768:1024] = gb[0, low:, :]
    if t == 1:
        x0a, x0b0, x0b1, pqa, pqb, ga, gb0, gb1 = rest[4:]
        for n, gb in enumerate((gb0, gb1)):
            for b in range(2):
                part = slice(b * low, (b + 1) * low)
                far_block[n * low : (n + 1) * low, b * 512 : b * 512 + 256] = ga[n, part, :]
                far_block[n * low : (n + 1) * low, b * 512 + 256 : (b + 1) * 512] = gb[0, part, :]
        parts_a, parts_b = [], []
        for k in range(4):
            block = lax.rem(z + k, 4) * 4 + quad
            parts_a.append(x0a[pl.ds(pl.multiple_of(block * 32, 32), 32), :])
            inner = pl.ds(pl.multiple_of(lax.rem(block, 8) * 32, 32), 32)
            parts_b.append(jnp.where(block < 8, x0b0[inner, :], x0b1[inner, :]))
        both = dot3(join(parts_a), halves(pqa[...]), NT) + dot3(join(parts_b), halves(pqb[...]), NT)
        for k in range(4):
            for b in range(4):
                blocks[k][width + 16 : width + 24, b * 256 : (b + 1) * 256] = both[32 * k + 8 * b : 32 * k + 8 * b + 8]


def update_kernel(idx, ga, gb0, gb1, w_up, w_down, v_up, v_down, opposite, near, far, decayed, accumulator, new_tables, new_accumulator):
    z = idx[0]
    towers, width, rows = decayed.shape
    low = width // 2

    def rider(ref, start=None):
        start = ref.shape[0] - low if start is None else start
        block = ref[start : start + low, :]
        return (
            jnp.concatenate([block[:, 0:256], block[:, 512:768]], axis=0),
            jnp.concatenate([block[:, 256:512], block[:, 768:1024]], axis=0),
        )

    for t in range(towers):
        gb = (gb0, gb1)[t]
        pieces = (
            (ga[t], gb[0]),
            rider((w_up, v_up)[t]),
            rider(opposite, low * t),
            rider((w_down, v_down)[t]),
        )
        total = jnp.zeros((2 * width, rows), F32)
        for k, (a, b) in enumerate(pieces):
            at = lax.rem(z + 4 - k, 4)
            total = total + dot1(jnp.concatenate(halves(a), axis=0), near[t, at], NT)
            total = total + dot1(jnp.concatenate(halves(b), axis=0), far[t, at], NT)
        grad = total[:width] + total[width:]
        square = jnp.sum(grad * grad, axis=0, keepdims=True) * (1.0 / width)
        fresh = accumulator[t : t + 1, :] + square
        new_accumulator[t : t + 1, :] = fresh
        new_tables[t] = decayed[t] - LEARN_RATE * grad / (jnp.sqrt(fresh) + EPSILON)


def sum_kernel(idx, head, *refs):
    parts, (first, second, lift, press, wide) = refs[:6], refs[6:]
    for t in range(2):
        a, b, c = parts[3 * t : 3 * t + 3]
        total = a[...] + (b[0 : a.shape[0]] + c[0 : a.shape[0]])
        for k in range(8):
            first[pl.ds(2 * k + t, 64, stride=16), :] = total[0:64, k * 128 : (k + 1) * 128]
        for b in range(4):
            for o in range(2):
                lanes = slice(b * 256 + o * 128, b * 256 + (o + 1) * 128)
                second[pl.ds(b * 64 + 2 * o + t, 16, stride=4), :] = total[64:80, lanes]
        if t == 1:
            wide[...] = jnp.broadcast_to(head[...], (128, head.shape[1])).T
            device = (idx[0] * 2 + idx[1]) * 2 + idx[2]
            column = wide[pl.ds(pl.multiple_of(device * 32, 32), 32), :]
            for b in range(4):
                at = slice(8 * b, 8 * b + 8)
                lift[at, :] = column[at] * total[80:88, b * 256 : b * 256 + 128]
                press[at, :] = total[80:88, b * 256 + 128 : (b + 1) * 256]


def shift(x, axis, size, by):
    return lax.ppermute(x, axis, [(i, (i + by) % size) for i in range(size)])


def flip(x, axis, size, bit):
    return lax.ppermute(x, axis, [(i, i ^ bit) for i in range(size)])


def per_device(bag_ids, touch_ids, elapsed, tables, accumulator, first_weight, second_weight, lift_weight, press_weight, head_weight, labels):
    f32 = lambda *shape: jax.ShapeDtypeStruct(shape, F32)
    bf16 = lambda *shape: jax.ShapeDtypeStruct(shape, BF16)
    axes = [lax.axis_index(name) for name in ("z", "xh", "core", TOWER)]
    idx = jnp.stack(axes).astype(jnp.int32)
    rank = lift_weight.shape[1]
    local = lift_weight.shape[0] // 8
    any_spec = pl.BlockSpec(memory_space=pl.ANY)

    tables_t = jnp.transpose(tables[:, 0], (0, 2, 1))
    bag = bag_ids[:, 0]
    hbm = lambda x: pltpu.with_memory_space_constraint(x, pltpu.HBM)
    *far, counts_far, decayed, bag_here = call(
        pool_far_kernel,
        [f32(128, 256)] * 4 + [bf16(2, 4, 512, 256), f32(2, 64, 512), jax.ShapeDtypeStruct((2, 4, 2048), jnp.int32)],
        [SMEM_SPEC] + [any_spec] * 4,
        [
            pltpu.VMEM((2, 128), jnp.int32),
            pltpu.VMEM((2, 128), jnp.int32),
            pltpu.VMEM((2, 64, 512), F32),
            pltpu.SemaphoreType.DMA((4,)),
        ],
        name="pool_far",
        flops=1e6,
    )(idx, hbm(bag), hbm(touch_ids[:, 0]), hbm(elapsed[:, 0]), hbm(tables_t))
    pack = call(pack_kernel, [f32(4, 128, 256)], [SMEM_SPEC] + vmem(4), name="pack", flops=1e6)
    far = [far[0]] + [shift(far[k], "z", 4, k) for k in (1, 2, 3)]
    *near, counts_near = call(
        pool_near_kernel, [f32(128, 256)] * 4 + [bf16(2, 4, 512, 256)], [SMEM_SPEC] + vmem(2), name="pool_near", flops=1e6
    )(idx, bag_here, decayed)
    view = first_weight.reshape(1024, 2, 8, 128).transpose(0, 2, 1, 3).reshape(1024, 16, 128)

    def turn(view, at):
        return pl.pallas_call(
            lambda *refs: turn_kernel(at, *refs),
            in_specs=[any_spec],
            out_specs=vmem(2),
            out_shape=[bf16(2, 1024, 512)] * 2,
            scratch_shapes=[pltpu.VMEM((4, 128, 16, 128), F32), pltpu.SemaphoreType.DMA((4,))],
            compiler_params=pltpu.CompilerParams(vmem_limit_bytes=VMEM_LIMIT),
            cost_estimate=pl.CostEstimate(flops=int(1e6), transcendentals=0, bytes_accessed=1 << 20),
            name="turn_%d" % at,
        )(hbm(view))

    view, _ = lax.optimization_barrier((view, decayed))
    w1ha, w1la = turn(view, 0)
    *far, _, _ = lax.optimization_barrier((*far, near[0], w1ha))
    (fq_far,) = pack(idx, *far)
    x2 = flip(fq_far, "xh", 2, 1)
    near = [near[0]] + [shift(near[k], "z", 4, k) for k in (1, 2, 3)]
    view, _ = lax.optimization_barrier((view, fq_far))
    w1hb, w1lb = turn(view, 1)
    *near, _ = lax.optimization_barrier((*near, w1hb))
    (fq_near,) = pack(idx, *near)
    y1 = flip(fq_near, "core", 2, 1)
    y2 = flip(x2, "core", 2, 1)
    x2b = flip(fq_near, "xh", 2, 1)
    y1b = flip(fq_far, "core", 2, 1)
    y2b = flip(x2b, "core", 2, 1)

    _, lift_weight, press_weight = lax.optimization_barrier((w1hb, lift_weight, press_weight))
    second_view = second_weight.reshape(1024, 2, 2, 128).transpose(0, 2, 1, 3).reshape(1024, 4, 128)
    w2th, w2tl, lift, press, head = call(
        prepare_kernel,
        [bf16(2, 256, 1024)] * 2 + [f32(local, rank), f32(local, rank), f32(1, local)],
        [SMEM_SPEC] + vmem(1) + [any_spec] * 2 + vmem(1),
        [pltpu.SemaphoreType.DMA((2,))],
        name="prepare",
        flops=1e6,
    )(idx, second_view, hbm(lift_weight), hbm(press_weight), head_weight.reshape(32, 128))

    scratch = [pltpu.VMEM((1024, 256), BF16)] * 2
    weights = (w1ha, w1la, w1hb, w1lb, w2th, w2tl, press, lift, head)
    hid_a, x0a, pay = call(
        lambda *refs: forward_kernel((0, 1), True, *refs),
        [f32(2, 1024, 256), f32(512, 256), f32(2 * rank + 8, 128)],
        [SMEM_SPEC] + vmem(13),
        scratch,
        name="forward_a",
        flops=1e6,
    )(idx, fq_near, x2, y1, y2, *weights)

    def later_half(at, t, y2b):
        return call(
            lambda *refs: forward_kernel((t,), False, *refs),
            [f32(1, 1024, 256), f32(256, 256)],
            [SMEM_SPEC] + vmem(13),
            scratch,
            name="forward_b%d" % t,
            flops=4e9,
        )(at, fq_far, x2b, y1b, y2b, *weights)

    view, second_view, pay = lax.optimization_barrier((view, second_view, pay))
    other = flip(pay, TOWER, 8, 1)
    w1qh, w1ql = call(
        pick_kernel,
        [bf16(2, 256, 1024)] * 2,
        [SMEM_SPEC, any_spec],
        [pltpu.VMEM((4, 64, 16, 128), F32), pltpu.SemaphoreType.DMA((4,))],
        name="pick",
        flops=1e6,
    )(idx, hbm(view))
    w2h, w2l = call(natural_kernel, [bf16(2, 1024, 256)] * 2, vmem(1), name="natural", flops=1e6)(second_view)
    other, w1qh, w2h, x2b = lax.optimization_barrier((other, w1qh, w2h, x2b))
    pay = pay + other
    after, pay = lax.optimization_barrier((idx, pay))
    other = flip(pay, TOWER, 8, 2)
    y2b = flip(x2b, "core", 2, 1)
    hid_b0, x0b0 = later_half(after, 0, y2b)
    other, x0b0 = lax.optimization_barrier((other, x0b0))
    pay = pay + other
    after, pay = lax.optimization_barrier((idx, pay))
    other = flip(pay, TOWER, 8, 6)
    hid_b1, x0b1 = later_half(after, 1, y2b)
    other, x0b1 = lax.optimization_barrier((other, x0b1))
    pay, logits = call(logit_kernel, [f32(2 * rank + 8, 128), f32(1, 16)], [SMEM_SPEC] + vmem(3), name="logit", flops=1e6)(
        idx, pay, other, labels
    )
    c1 = flip(pay, "core", 2, 1)
    xa = flip(pay, "xh", 2, 1)

    def grads(towers, with_pq, mine, other, hidden, name):
        n = len(towers)
        return call(
            lambda *refs: grads_kernel(towers, with_pq, *refs),
            [bf16(n, 1024, 256)] * 2 + [f32(n, 256, 256)] + [f32(n, 64, 256)] * 4 + [f32(2 * rank, 256)] * with_pq,
            [SMEM_SPEC] + vmem(10),
            name=name,
            flops=4e9,
        )(idx, mine, other, hidden, w1qh, w1ql, w2h, w2l, press, lift, head)

    ghha, ghla, gouta, *ga, pqa = grads((0, 1), True, pay, c1, hid_a, "grads_a")

    xa, pqa = lax.optimization_barrier((xa, pqa))
    xb = flip(xa, "core", 2, 1)

    def weights_of(t, riders, rows, ghhb, ghlb, goutb, hid_b, extra):
        return call(
            lambda *refs: weights_kernel(t, riders, *refs),
            [f32(n, 1024) for n in rows],
            [SMEM_SPEC] + vmem(10 + len(extra)),
            name="weights_%d" % t,
            flops=3e9,
        )(idx, fq_near, fq_far, ghha, ghla, ghhb, ghlb, gouta, goutb, hid_a, hid_b, *extra)

    ghh0, ghl0, gout0, *gb0, pqb = grads((0,), True, xa, xb, hid_b0, "grads_b0")
    w = weights_of(0, (2, 3), (80, 80, 112, 112), ghh0, ghl0, gout0, hid_b0, (ga[1], gb0[1], ga[3], gb0[3]))
    up = shift(w[2], "z", 4, 1)
    w3 = shift(w[3], "z", 4, 3)
    ghh1, ghl1, gout1, *gb1 = grads((1,), False, xa, xb, hid_b1, "grads_b1")
    v = weights_of(
        1,
        (1, 2),
        (88, 120, 120, 88, 64),
        ghh1,
        ghl1,
        gout1,
        hid_b1,
        (ga[1], gb1[1], ga[3], gb1[3], x0a, x0b0, x0b1, pqa, pqb, ga[2], gb0[2], gb1[2]),
    )
    down = shift(v[2], "z", 4, 3)
    v1 = shift(v[1], "z", 4, 1)
    g2 = shift(v[4], "z", 4, 2)
    up, w3 = lax.optimization_barrier((up, w3))
    down, v1 = lax.optimization_barrier((down, v1))
    w1 = shift(w[1] + up[0:80], "z", 4, 1)
    v3 = shift(v[3] + down[0:88], "z", 4, 3)
    new_tables, new_accumulator = call(
        update_kernel, [f32(2, 64, 512), f32(2, 512)], [SMEM_SPEC] + vmem(12), name="update", flops=5e9
    )(idx, ga[0], gb0[0], gb1[0], up, w3, v1, down, g2, counts_near, counts_far, decayed, accumulator[:, 0])
    first, second, lift_out, press_out = call(
        sum_kernel,
        [f32(1024, 128), f32(256, 128), f32(32, rank), f32(32, rank)],
        [SMEM_SPEC] + vmem(7),
        [pltpu.VMEM((local, 128), F32)],
        name="sum",
        flops=1e6,
    )(idx, head, w[0], w1, w3, v[0], v1, v3)
    return (
        jnp.transpose(new_tables, (0, 2, 1))[:, None],
        new_accumulator[:, None],
        first.reshape(64, 8, 2, 128).transpose(0, 2, 1, 3).reshape(64, 2, 1024),
        second.reshape(64, 2, 2, 128).transpose(0, 2, 1, 3).reshape(64, 2, 256),
        lift_out,
        press_out,
        logits,
    )


def solution(mesh):
    split = Mesh(mesh.devices.reshape(4, 2, 4, 2, 2), ("y", "xl", "z", "xh", "core"))
    member = ("z", "xh", "core")
    placed = (
        P(TOWER, member, None, None),
        P(TOWER, member, None),
        P(TOWER, member, None),
        P(TOWER, member, None, None),
        P(TOWER, member, None),
        P(None, TOWER, None),
        P(None, TOWER, None),
        P(),
        P(),
        P(),
        P(member, None),
    )
    return jax.shard_map(
        per_device,
        mesh=split,
        in_specs=placed,
        out_specs=(
            P(TOWER, member, None, None),
            P(TOWER, member, None),
            P(member, TOWER, None),
            P(member, TOWER, None),
            P(TOWER + member, None),
            P(TOWER + member, None),
            P(member, TOWER),
        ),
        check_vma=False,
    )
```

```python
import math

import jax
import jax.numpy as jnp
from jax import lax
from jax.experimental import pallas as pl
from jax.experimental.pallas import tpu as pltpu
from jax.sharding import Mesh, PartitionSpec as P

DECAY_RATE = 0.98
LEARN_RATE = 1.0
EPSILON = 1e-08
F32 = jnp.float32
BF16 = jnp.bfloat16
NN = (((1,), (0,)), ((), ()))
NT = (((1,), (1,)), ((), ()))
TOWER = ("y", "xl")
QUAD = ("xh", "core")
VMEM_LIMIT = 16 << 20


def halves(a):
    high = a.astype(BF16)
    return high, (a - high.astype(F32)).astype(BF16)


def dot1(a, b, dims):
    return lax.dot_general(a, b, dims, preferred_element_type=F32)


def dot3(a, b, dims=NN):
    return dot1(a[0], b[0], dims) + (dot1(a[0], b[1], dims) + dot1(a[1], b[0], dims))


def dot32(a, b, dims=NN):
    return dot3(halves(a), halves(b), dims)


def vmem(count):
    return [pl.BlockSpec(memory_space=pltpu.VMEM)] * count


def call(kernel, outs, spec_in, scratch=(), name=None, flops=0):
    return pl.pallas_call(
        kernel,
        cost_estimate=pl.CostEstimate(flops=int(flops), transcendentals=0, bytes_accessed=1 << 20),
        out_shape=outs,
        in_specs=spec_in,
        out_specs=vmem(len(outs)),
        scratch_shapes=list(scratch),
        compiler_params=pltpu.CompilerParams(vmem_limit_bytes=VMEM_LIMIT),
        name=name,
    )


SMEM_SPEC = pl.BlockSpec(memory_space=pltpu.SMEM)


def decay(touch, elapsed, tables, decayed):
    towers, width, rows = tables.shape
    touches = touch.shape[1]
    for t in range(towers):
        ids = jnp.broadcast_to(touch[t : t + 1, :].astype(F32), (touches, touches)).T
        rates = jnp.exp(elapsed[t : t + 1, :].astype(F32) * math.log(DECAY_RATE))
        rates = jnp.broadcast_to(rates, (touches, touches)).T
        factor = []
        for block in range(rows // touches):
            row = lax.broadcasted_iota(jnp.int32, (touches, touches), 1).astype(F32) + float(block * touches)
            match = ids == row
            hits = jnp.sum(jnp.where(match, 1.0, 0.0), axis=0, keepdims=True)
            chosen = jnp.sum(jnp.where(match, rates, 0.0), axis=0, keepdims=True)
            factor.append(jnp.where(hits > 0.0, chosen, 1.0))
        decayed[t] = tables[t] * jnp.concatenate(factor, axis=1)


def pool_half(idx, side, bag, decayed, pooled, counts):
    towers, width, rows = decayed.shape
    part = pooled[0].shape[1]
    for t in range(towers):
        both = jnp.concatenate(halves(decayed[t]), axis=0)
        for k, out in enumerate(pooled):
            chunk = lax.rem(idx[0] + k, 4)
            at = pl.multiple_of(chunk * 2 * part + side * part, part)
            ids = bag[t, :, pl.ds(at, part)]
            row = lax.broadcasted_iota(jnp.int32, (rows, part), 0)
            count = jnp.zeros((rows, part), F32)
            for b in range(ids.shape[0]):
                count = count + jnp.where(row == ids[b : b + 1, :], 1.0, 0.0)
            count = count.astype(BF16)
            counts[t, chunk] = count
            total = dot1(both, count, NN)
            out[t * width : (t + 1) * width, :] = total[:width] + total[width:]


def pool_far_kernel(idx, bag_hbm, touch_hbm, elapsed_hbm, tables_hbm, p0, p1, p2, p3, counts, decayed, bag, touch, elapsed, tables, sems):
    pairs = ((bag_hbm, bag), (touch_hbm, touch), (elapsed_hbm, elapsed), (tables_hbm, tables))
    copies = [pltpu.make_async_copy(a, b, sems.at[n]) for n, (a, b) in enumerate(pairs)]
    for copy in copies:
        copy.start()
    for copy in copies:
        copy.wait()
    decay(touch, elapsed, tables, decayed)
    pool_half(idx, 1 - idx[1], bag, decayed, (p0, p1, p2, p3), counts)


def pool_near_kernel(idx, bag, decayed, p0, p1, p2, p3, counts):
    pool_half(idx, idx[1], bag, decayed, (p0, p1, p2, p3), counts)


def pack_kernel(idx, p0, p1, p2, p3, out):
    for k, ref in enumerate((p0, p1, p2, p3)):
        out[lax.rem(idx[0] + 4 - k, 4)] = ref[...]


def turn_kernel(at, w_hbm, high, low, w, sems):
    pieces, rows = w.shape[:2]
    copies = [pltpu.make_async_copy(w_hbm.at[pl.ds((at * pieces + n) * rows, rows)], w.at[n], sems.at[n]) for n in range(pieces)]
    for copy in copies:
        copy.start()
    for n, copy in enumerate(copies):
        copy.wait()
        flat = w.at[n].reshape(rows * 16, 128)
        for t in range(2):
            for b in range(8):
                h, l = halves(flat[pl.ds(b * 2 + t, rows, stride=16), :].T)
                high[t, b * 128 : (b + 1) * 128, n * rows : (n + 1) * rows] = h
                low[t, b * 128 : (b + 1) * 128, n * rows : (n + 1) * rows] = l


def pick_kernel(idx, w_hbm, high, low, w, sems):
    rows = w.shape[1]
    quad = 2 * idx[1] + idx[2]
    copies = []
    for k in range(4):
        table = lax.rem(idx[0] + k, 4) * 4 + quad
        copies.append(pltpu.make_async_copy(w_hbm.at[pl.ds(pl.multiple_of(table * rows, rows), rows)], w.at[k], sems.at[k]))
    for copy in copies:
        copy.start()
    for k, copy in enumerate(copies):
        copy.wait()
        flat = w.at[k].reshape(rows * 16, 128)
        for t in range(2):
            for b in range(8):
                h, l = halves(flat[pl.ds(b * 2 + t, rows, stride=16), :])
                high[t, k * rows : (k + 1) * rows, b * 128 : (b + 1) * 128] = h
                low[t, k * rows : (k + 1) * rows, b * 128 : (b + 1) * 128] = l


def prepare_kernel(idx, second, lift_hbm, press_hbm, heads, high_t, low_t, lift, press, head, sems):
    tower = idx[3]
    rows = pl.ds(pl.multiple_of(tower * lift.shape[0], lift.shape[0]), lift.shape[0])
    pairs = ((lift_hbm.at[rows, :], lift), (press_hbm.at[rows, :], press))
    copies = [pltpu.make_async_copy(a, b, sems.at[n]) for n, (a, b) in enumerate(pairs)]
    for copy in copies:
        copy.start()
    head[...] = jnp.concatenate([heads[pl.ds(tower * 4 + b, 1), :] for b in range(4)], axis=1)
    count = second.shape[0]
    flat = second.reshape(count * 4, 128)
    for t in range(2):
        for b in range(2):
            lanes = slice(b * 128, (b + 1) * 128)
            h, l = halves(flat[pl.ds(b * 2 + t, count, stride=4), :].T)
            high_t[t, lanes, :] = h
            low_t[t, lanes, :] = l
    for copy in copies:
        copy.wait()


def natural_kernel(w, high, low):
    rows = w.shape[0]
    flat = w.reshape(rows * 4, 128)
    for t in range(2):
        for b in range(2):
            lanes = slice(b * 128, (b + 1) * 128)
            h, l = halves(flat[pl.ds(b * 2 + t, rows, stride=4), :])
            high[t, :, lanes] = h
            low[t, :, lanes] = l


def forward_kernel(towers, with_pay, idx, x1, x2, y1, y2, w1ha, w1la, w1hb, w1lb, w2h, w2l, press, lift, head, hidden, start, *rest):
    fh, fl = rest[-2:]
    sets = (x1, x2, y1, y2)
    zs, pair, samples = x1.shape
    width = pair // 2
    xh, core = idx[1], idx[2]
    place = ((xh, core), (1 - xh, core), (xh, 1 - core), (1 - xh, 1 - core))
    width_out = w2h.shape[1]

    def one_tower(t, slot):
        for (a, b), ref in zip(place, sets):
            for z in range(zs):
                h, l = halves(ref[z, pl.ds(pl.multiple_of(t * width, width), width), :])
                at = pl.multiple_of(((z * 2 + a) * 2 + b) * width, width)
                fh[pl.ds(at, width), :] = h
                fl[pl.ds(at, width), :] = l
        deep = w1ha.shape[2]
        value = dot3((w1ha[t], w1la[t]), (fh[0:deep, :], fl[0:deep, :]))
        value = value + dot3((w1hb[t], w1lb[t]), (fh[deep:, :], fl[deep:, :]))
        hidden[slot] = value
        act = halves(value * jax.nn.sigmoid(value))
        start[pl.ds(pl.multiple_of(slot * width_out, width_out), width_out), :] = dot3((w2h[t], w2l[t]), act)

    if len(towers) == 2:

        def step(t, carry):
            one_tower(t, t)
            return carry

        lax.fori_loop(0, 2, step, 0)
    else:
        one_tower(towers[0], 0)
    if with_pay:
        pay = rest[0]
        own = samples // 2
        rank = press.shape[1]
        x0 = halves(start[:, pl.ds(pl.multiple_of(core * own, own), own)])
        p = dot3(halves(press[...].T), x0)
        q = dot3(halves(lift[...].T * head[...]), x0)
        d = dot3(halves(jnp.broadcast_to(head[...], (8, head.shape[1]))), x0)
        pay[0:rank, :] = p
        pay[rank : 2 * rank, :] = q
        pay[2 * rank : 2 * rank + 8, :] = d


def logit_kernel(idx, mine, other, labels, pay, logits):
    total = mine[...] + other[...]
    rank = (total.shape[0] - 8) // 2
    value = jnp.sum(total[0:rank] * total[rank : 2 * rank], axis=0, keepdims=True) + total[2 * rank : 2 * rank + 1]
    turned = pltpu.roll(jnp.broadcast_to(value, (8, 128)), lax.rem(128 - 16 * idx[3], 128), 1)
    logits[...] = turned[0:1, 0:16]
    error = jax.nn.sigmoid(value) - labels[...].astype(F32)
    pay[0 : 2 * rank, :] = total[0 : 2 * rank]
    pay[2 * rank : 2 * rank + 8, :] = jnp.broadcast_to(error, (8, error.shape[1]))


def grads_kernel(towers, with_pq, extra, idx, mine, other, hidden, w1h, w1l, w2h, w2l, press, lift, head, *refs):
    ghh, ghl, gout, g0, g1, g2, g3, *pq = refs[extra:]
    rank = press.shape[1]
    width = w1h.shape[1] // 4
    width_out = w2h.shape[2]
    first_core = idx[2] == 0
    left = jnp.where(first_core, mine[...], other[...])
    right = jnp.where(first_core, other[...], mine[...])
    both = jnp.concatenate([left, right], axis=1)
    error = both[2 * rank : 2 * rank + 1]
    if with_pq:
        pq[0][...] = error * both[0 : 2 * rank]
    p, q = halves(both[0:rank]), halves(both[rank : 2 * rank])
    column = jnp.broadcast_to(head[...], (128, head.shape[1])).T[:, 0:1]
    for slot, t in enumerate(towers):
        rows = slice(t * width_out, (t + 1) * width_out)
        scaling = dot3(halves(lift[rows, :]), p)
        back = dot3(halves(press[rows, :]), q)
        go = error * (column[rows] * (scaling + 1.0) + back)
        gout[slot] = go
        ga = dot3((w2h[t], w2l[t]), halves(go))
        value = hidden[slot]
        s = jax.nn.sigmoid(value)
        gh = halves(ga * (s * (1.0 + value * (1.0 - s))))
        ghh[slot] = gh[0]
        ghl[slot] = gh[1]
        grad = dot3((w1h[t], w1l[t]), gh)
        for k, out in enumerate((g0, g1, g2, g3)):
            out[slot] = grad[k * width : (k + 1) * width]


def weights_kernel(t, riders, idx, near, far, ghha, ghla, ghhb, ghlb, gouta, goutb, hid_a, hid_b, *rest):
    if t == 1:
        rest, far_block = rest[:-1], rest[-1]
    blocks, rest = rest[-4:], rest[:-4]
    z, quad = idx[0], 2 * idx[1] + idx[2]
    width = near.shape[1] // 2
    rows = slice(t * width, (t + 1) * width)
    fa, fb, acta, actb = [], [], [], []
    for k in range(4):
        at = lax.rem(z + k, 4)
        fa.append(near[at, rows, :])
        fb.append(far[at, rows, :])
        pick = pl.ds(pl.multiple_of((at * 4 + quad) * width, width), width)
        value = hid_a[t, pick, :]
        acta.append(value * jax.nn.sigmoid(value))
        value = hid_b[0, pick, :]
        actb.append(value * jax.nn.sigmoid(value))
    join = lambda parts: halves(jnp.concatenate(parts, axis=0))
    grad = dot3(join(fa), (ghha[t], ghla[t]), NT) + dot3(join(fb), (ghhb[0], ghlb[0]), NT)
    for k in range(4):
        blocks[k][0:width, :] = grad[k * width : (k + 1) * width]
    grad = dot3(join(acta), halves(gouta[t]), NT) + dot3(join(actb), halves(goutb[0]), NT)
    for k in range(4):
        for b in range(4):
            blocks[k][width : width + 16, b * 256 : (b + 1) * 256] = grad[k * width + 16 * b : k * width + 16 * b + 16]
    low = width // 4
    for n, k in enumerate(riders):
        base = blocks[k].shape[0] - low
        for b in range(4):
            blocks[k][base:, b * 256 : (b + 1) * 256] = rest[n][0, b * low : (b + 1) * low, :]
    if t == 1:
        x0a, x0b0, x0b1, pqa, pqb, gb0, gb1 = rest[2:]
        for n, gb in enumerate((gb0, gb1)):
            for b in range(4):
                far_block[n * low : (n + 1) * low, b * 256 : (b + 1) * 256] = gb[0, b * low : (b + 1) * low, :]
        parts_a, parts_b = [], []
        for k in range(4):
            block = lax.rem(z + k, 4) * 4 + quad
            parts_a.append(x0a[pl.ds(pl.multiple_of(block * 32, 32), 32), :])
            inner = pl.ds(pl.multiple_of(lax.rem(block, 8) * 32, 32), 32)
            parts_b.append(jnp.where(block < 8, x0b0[inner, :], x0b1[inner, :]))
        both = dot3(join(parts_a), halves(pqa[...]), NT) + dot3(join(parts_b), halves(pqb[...]), NT)
        for k in range(4):
            for b in range(4):
                blocks[k][width + 16 : width + 24, b * 256 : (b + 1) * 256] = both[32 * k + 8 * b : 32 * k + 8 * b + 8]


def update_kernel(idx, ga0, ga1, ga2, ga3, gb0, gb1, w_up, w_down, v_up, v_down, opposite, near, far, decayed, accumulator, new_tables, new_accumulator):
    z = idx[0]
    towers, width, rows = decayed.shape
    low = width // 4

    def rider(ref, start=None):
        start = ref.shape[0] - low if start is None else start
        block = ref[start : start + low, :]
        return jnp.concatenate([block[:, b * 256 : (b + 1) * 256] for b in range(4)], axis=0)

    for t in range(towers):
        pieces = (
            (ga0[t], (gb0, gb1)[t][0]),
            (ga1[t], rider((w_up, v_up)[t])),
            (ga2[t], rider(opposite, low * t)),
            (ga3[t], rider((w_down, v_down)[t])),
        )
        total = jnp.zeros((2 * width, rows), F32)
        for k, (a, b) in enumerate(pieces):
            at = lax.rem(z + 4 - k, 4)
            total = total + dot1(jnp.concatenate(halves(a), axis=0), near[t, at], NT)
            total = total + dot1(jnp.concatenate(halves(b), axis=0), far[t, at], NT)
        grad = total[:width] + total[width:]
        square = jnp.sum(grad * grad, axis=0, keepdims=True) * (1.0 / width)
        fresh = accumulator[t : t + 1, :] + square
        new_accumulator[t : t + 1, :] = fresh
        new_tables[t] = decayed[t] - LEARN_RATE * grad / (jnp.sqrt(fresh) + EPSILON)


def sum_kernel(idx, head, *refs):
    parts, (first, second, lift, press, wide) = refs[:6], refs[6:]
    for t in range(2):
        a, b, c = parts[3 * t : 3 * t + 3]
        total = a[...] + (b[0 : a.shape[0]] + c[0 : a.shape[0]])
        for k in range(8):
            first[pl.ds(2 * k + t, 64, stride=16), :] = total[0:64, k * 128 : (k + 1) * 128]
        for b in range(4):
            for o in range(2):
                lanes = slice(b * 256 + o * 128, b * 256 + (o + 1) * 128)
                second[pl.ds(b * 64 + 2 * o + t, 16, stride=4), :] = total[64:80, lanes]
        if t == 1:
            wide[...] = jnp.broadcast_to(head[...], (128, head.shape[1])).T
            device = (idx[0] * 2 + idx[1]) * 2 + idx[2]
            column = wide[pl.ds(pl.multiple_of(device * 32, 32), 32), :]
            for b in range(4):
                at = slice(8 * b, 8 * b + 8)
                lift[at, :] = column[at] * total[80:88, b * 256 : b * 256 + 128]
                press[at, :] = total[80:88, b * 256 + 128 : (b + 1) * 256]


def shift(x, axis, size, by):
    return lax.ppermute(x, axis, [(i, (i + by) % size) for i in range(size)])


def flip(x, axis, size, bit):
    return lax.ppermute(x, axis, [(i, i ^ bit) for i in range(size)])


def per_device(bag_ids, touch_ids, elapsed, tables, accumulator, first_weight, second_weight, lift_weight, press_weight, head_weight, labels):
    f32 = lambda *shape: jax.ShapeDtypeStruct(shape, F32)
    bf16 = lambda *shape: jax.ShapeDtypeStruct(shape, BF16)
    axes = [lax.axis_index(name) for name in ("z", "xh", "core", TOWER)]
    idx = jnp.stack(axes).astype(jnp.int32)
    rank = lift_weight.shape[1]
    local = lift_weight.shape[0] // 8
    any_spec = pl.BlockSpec(memory_space=pl.ANY)

    tables_t = jnp.transpose(tables[:, 0], (0, 2, 1))
    bag = bag_ids[:, 0]
    hbm = lambda x: pltpu.with_memory_space_constraint(x, pltpu.HBM)
    *far, counts_far, decayed, bag_here = call(
        pool_far_kernel,
        [f32(128, 256)] * 4 + [bf16(2, 4, 512, 256), f32(2, 64, 512), jax.ShapeDtypeStruct((2, 4, 2048), jnp.int32)],
        [SMEM_SPEC] + [any_spec] * 4,
        [
            pltpu.VMEM((2, 128), jnp.int32),
            pltpu.VMEM((2, 128), jnp.int32),
            pltpu.VMEM((2, 64, 512), F32),
            pltpu.SemaphoreType.DMA((4,)),
        ],
        name="pool_far",
        flops=1e6,
    )(idx, hbm(bag), hbm(touch_ids[:, 0]), hbm(elapsed[:, 0]), hbm(tables_t))
    pack = call(pack_kernel, [f32(4, 128, 256)], [SMEM_SPEC] + vmem(4), name="pack", flops=1e6)
    far = [far[0]] + [shift(far[k], "z", 4, k) for k in (1, 2, 3)]
    *near, counts_near = call(
        pool_near_kernel, [f32(128, 256)] * 4 + [bf16(2, 4, 512, 256)], [SMEM_SPEC] + vmem(2), name="pool_near", flops=1e6
    )(idx, bag_here, decayed)
    view = first_weight.reshape(1024, 2, 8, 128).transpose(0, 2, 1, 3).reshape(1024, 16, 128)

    def turn(view, at):
        return pl.pallas_call(
            lambda *refs: turn_kernel(at, *refs),
            in_specs=[any_spec],
            out_specs=vmem(2),
            out_shape=[bf16(2, 1024, 512)] * 2,
            scratch_shapes=[pltpu.VMEM((4, 128, 16, 128), F32), pltpu.SemaphoreType.DMA((4,))],
            compiler_params=pltpu.CompilerParams(vmem_limit_bytes=VMEM_LIMIT),
            cost_estimate=pl.CostEstimate(flops=int(1e6), transcendentals=0, bytes_accessed=1 << 20),
            name="turn_%d" % at,
        )(hbm(view))

    view, _ = lax.optimization_barrier((view, decayed))
    w1ha, w1la = turn(view, 0)
    *far, _, _ = lax.optimization_barrier((*far, near[0], w1ha))
    (fq_far,) = pack(idx, *far)
    x2 = flip(fq_far, "xh", 2, 1)
    near = [near[0]] + [shift(near[k], "z", 4, k) for k in (1, 2, 3)]
    view, _ = lax.optimization_barrier((view, fq_far))
    w1hb, w1lb = turn(view, 1)
    *near, _ = lax.optimization_barrier((*near, w1hb))
    (fq_near,) = pack(idx, *near)
    y1 = flip(fq_near, "core", 2, 1)
    y2 = flip(x2, "core", 2, 1)
    x2b = flip(fq_near, "xh", 2, 1)
    y1b = flip(fq_far, "core", 2, 1)
    y2b = flip(x2b, "core", 2, 1)

    _, lift_weight, press_weight = lax.optimization_barrier((w1hb, lift_weight, press_weight))
    second_view = second_weight.reshape(1024, 2, 2, 128).transpose(0, 2, 1, 3).reshape(1024, 4, 128)
    w2th, w2tl, lift, press, head = call(
        prepare_kernel,
        [bf16(2, 256, 1024)] * 2 + [f32(local, rank), f32(local, rank), f32(1, local)],
        [SMEM_SPEC] + vmem(1) + [any_spec] * 2 + vmem(1),
        [pltpu.SemaphoreType.DMA((2,))],
        name="prepare",
        flops=1e6,
    )(idx, second_view, hbm(lift_weight), hbm(press_weight), head_weight.reshape(32, 128))

    scratch = [pltpu.VMEM((1024, 256), BF16)] * 2
    weights = (w1ha, w1la, w1hb, w1lb, w2th, w2tl, press, lift, head)
    hid_a, x0a, pay = call(
        lambda *refs: forward_kernel((0, 1), True, *refs),
        [f32(2, 1024, 256), f32(512, 256), f32(2 * rank + 8, 128)],
        [SMEM_SPEC] + vmem(13),
        scratch,
        name="forward_a",
        flops=1e6,
    )(idx, fq_near, x2, y1, y2, *weights)

    def later_half(at, t, y2b):
        return call(
            lambda *refs: forward_kernel((t,), False, *refs),
            [f32(1, 1024, 256), f32(256, 256)],
            [SMEM_SPEC] + vmem(13),
            scratch,
            name="forward_b%d" % t,
            flops=4e9,
        )(at, fq_far, x2b, y1b, y2b, *weights)

    view, second_view, pay = lax.optimization_barrier((view, second_view, pay))
    other = flip(pay, TOWER, 8, 1)
    w1qh, w1ql = call(
        pick_kernel,
        [bf16(2, 256, 1024)] * 2,
        [SMEM_SPEC, any_spec],
        [pltpu.VMEM((4, 64, 16, 128), F32), pltpu.SemaphoreType.DMA((4,))],
        name="pick",
        flops=1e6,
    )(idx, hbm(view))
    w2h, w2l = call(natural_kernel, [bf16(2, 1024, 256)] * 2, vmem(1), name="natural", flops=1e6)(second_view)
    other, w1qh, w2h, x2b = lax.optimization_barrier((other, w1qh, w2h, x2b))
    pay = pay + other
    after, pay = lax.optimization_barrier((idx, pay))
    other = flip(pay, TOWER, 8, 2)
    y2b = flip(x2b, "core", 2, 1)
    hid_b0, x0b0 = later_half(after, 0, y2b)
    other, x0b0 = lax.optimization_barrier((other, x0b0))
    pay = pay + other
    after, pay = lax.optimization_barrier((idx, pay))
    other = flip(pay, TOWER, 8, 6)
    hid_b1, x0b1 = later_half(after, 1, y2b)
    other, x0b1 = lax.optimization_barrier((other, x0b1))
    pay, logits = call(logit_kernel, [f32(2 * rank + 8, 128), f32(1, 16)], [SMEM_SPEC] + vmem(3), name="logit", flops=1e6)(
        idx, pay, other, labels
    )
    c1 = flip(pay, "core", 2, 1)
    xa = flip(pay, "xh", 2, 1)

    def grads(towers, with_pq, mine, other, hidden, name, flops, extra=()):
        n = len(towers)
        return call(
            lambda *refs: grads_kernel(towers, with_pq, len(extra), *refs),
            [bf16(n, 1024, 256)] * 2 + [f32(n, 256, 256)] + [f32(n, 64, 256)] * 4 + [f32(2 * rank, 256)] * with_pq,
            [SMEM_SPEC] + vmem(10 + len(extra)),
            name=name,
            flops=flops,
        )(idx, mine, other, hidden, w1qh, w1ql, w2h, w2l, press, lift, head, *extra)

    ghha, ghla, gouta, *ga, pqa = grads((0, 1), True, pay, c1, hid_a, "grads_a", 4e9)

    gone = [shift(ga[k], "z", 4, k) for k in (1, 2, 3)]
    xa, pqa = lax.optimization_barrier((xa, pqa))
    xb = flip(xa, "core", 2, 1)

    def weights_of(t, riders, rows, ghhb, ghlb, goutb, hid_b, extra):
        return call(
            lambda *refs: weights_kernel(t, riders, *refs),
            [f32(n, 1024) for n in rows],
            [SMEM_SPEC] + vmem(10 + len(extra)),
            name="weights_%d" % t,
            flops=3e9,
        )(idx, fq_near, fq_far, ghha, ghla, ghhb, ghlb, gouta, goutb, hid_a, hid_b, *extra)

    ghh0, ghl0, gout0, *gb0, pqb = grads((0,), True, xa, xb, hid_b0, "grads_b0", 4e9)
    w = weights_of(0, (2, 3), (80, 80, 96, 96), ghh0, ghl0, gout0, hid_b0, (gb0[1], gb0[3]))
    up = shift(w[2], "z", 4, 1)
    w3 = shift(w[3], "z", 4, 3)
    ghh1, ghl1, gout1, *gb1 = grads((1,), False, xa, xb, hid_b1, "grads_b1", 4e9, gone)
    v = weights_of(
        1,
        (1, 2),
        (88, 104, 104, 88, 32),
        ghh1,
        ghl1,
        gout1,
        hid_b1,
        (gb1[1], gb1[3], x0a, x0b0, x0b1, pqa, pqb, gb0[2], gb1[2]),
    )
    down = shift(v[2], "z", 4, 3)
    v1 = shift(v[1], "z", 4, 1)
    g2 = shift(v[4], "z", 4, 2)
    up, w3 = lax.optimization_barrier((up, w3))
    down, v1 = lax.optimization_barrier((down, v1))
    w1 = shift(w[1] + up[0:80], "z", 4, 1)
    v3 = shift(v[3] + down[0:88], "z", 4, 3)
    new_tables, new_accumulator = call(
        update_kernel, [f32(2, 64, 512), f32(2, 512)], [SMEM_SPEC] + vmem(15), name="update", flops=5e9
    )(idx, ga[0], *gone, gb0[0], gb1[0], up, w3, v1, down, g2, counts_near, counts_far, decayed, accumulator[:, 0])
    first, second, lift_out, press_out = call(
        sum_kernel,
        [f32(1024, 128), f32(256, 128), f32(32, rank), f32(32, rank)],
        [SMEM_SPEC] + vmem(7),
        [pltpu.VMEM((local, 128), F32)],
        name="sum",
        flops=1e6,
    )(idx, head, w[0], w1, w3, v[0], v1, v3)
    return (
        jnp.transpose(new_tables, (0, 2, 1))[:, None],
        new_accumulator[:, None],
        first.reshape(64, 8, 2, 128).transpose(0, 2, 1, 3).reshape(64, 2, 1024),
        second.reshape(64, 2, 2, 128).transpose(0, 2, 1, 3).reshape(64, 2, 256),
        lift_out,
        press_out,
        logits,
    )


def solution(mesh):
    split = Mesh(mesh.devices.reshape(4, 2, 4, 2, 2), ("y", "xl", "z", "xh", "core"))
    member = ("z", "xh", "core")
    placed = (
        P(TOWER, member, None, None),
        P(TOWER, member, None),
        P(TOWER, member, None),
        P(TOWER, member, None, None),
        P(TOWER, member, None),
        P(None, TOWER, None),
        P(None, TOWER, None),
        P(),
        P(),
        P(),
        P(member, None),
    )
    return jax.shard_map(
        per_device,
        mesh=split,
        in_specs=placed,
        out_specs=(
            P(TOWER, member, None, None),
            P(TOWER, member, None),
            P(member, TOWER, None),
            P(member, TOWER, None),
            P(TOWER + member, None),
            P(TOWER + member, None),
            P(member, TOWER),
        ),
        check_vma=False,
    )
```

```python
import math

import jax
import jax.numpy as jnp
from jax import lax
from jax.experimental import pallas as pl
from jax.experimental.pallas import tpu as pltpu
from jax.sharding import Mesh, PartitionSpec as P

DECAY_RATE = 0.98
LEARN_RATE = 1.0
EPSILON = 1e-08
F32 = jnp.float32
BF16 = jnp.bfloat16
NN = (((1,), (0,)), ((), ()))
NT = (((1,), (1,)), ((), ()))
TOWER = ("y", "xl")
QUAD = ("xh", "core")
VMEM_LIMIT = 16 << 20
PIECE = 256


def halves(a):
    high = a.astype(BF16)
    return high, (a - high.astype(F32)).astype(BF16)


def dot1(a, b, dims):
    return lax.dot_general(a, b, dims, preferred_element_type=F32)


def dot3(a, b, dims=NN):
    return dot1(a[0], b[0], dims) + (dot1(a[0], b[1], dims) + dot1(a[1], b[0], dims))


def dot32(a, b, dims=NN):
    return dot3(halves(a), halves(b), dims)


def vmem(count):
    return [pl.BlockSpec(memory_space=pltpu.VMEM)] * count


def call(kernel, outs, spec_in, scratch=(), name=None, flops=0):
    return pl.pallas_call(
        kernel,
        cost_estimate=pl.CostEstimate(flops=int(flops), transcendentals=0, bytes_accessed=1 << 20),
        out_shape=outs,
        in_specs=spec_in,
        out_specs=vmem(len(outs)),
        scratch_shapes=list(scratch),
        compiler_params=pltpu.CompilerParams(vmem_limit_bytes=VMEM_LIMIT),
        name=name,
    )


SMEM_SPEC = pl.BlockSpec(memory_space=pltpu.SMEM)


def decay(touch, elapsed, tables, decayed):
    towers, width, rows = tables.shape
    touches = touch.shape[1]
    for t in range(towers):
        ids = jnp.broadcast_to(touch[t : t + 1, :].astype(F32), (touches, touches)).T
        rates = jnp.exp(elapsed[t : t + 1, :].astype(F32) * math.log(DECAY_RATE))
        rates = jnp.broadcast_to(rates, (touches, touches)).T
        factor = []
        for block in range(rows // touches):
            row = lax.broadcasted_iota(jnp.int32, (touches, touches), 1).astype(F32) + float(block * touches)
            match = ids == row
            hits = jnp.sum(jnp.where(match, 1.0, 0.0), axis=0, keepdims=True)
            chosen = jnp.sum(jnp.where(match, rates, 0.0), axis=0, keepdims=True)
            factor.append(jnp.where(hits > 0.0, chosen, 1.0))
        decayed[t] = tables[t] * jnp.concatenate(factor, axis=1)


def pool_half(idx, side, bag, decayed, pooled, counts):
    towers, width, rows = decayed.shape
    part = pooled[0].shape[1]
    for t in range(towers):
        both = jnp.concatenate(halves(decayed[t]), axis=0)
        for k, out in enumerate(pooled):
            chunk = lax.rem(idx[0] + k, 4)
            at = pl.multiple_of(chunk * 2 * part + side * part, part)
            ids = bag[t, :, pl.ds(at, part)]
            row = lax.broadcasted_iota(jnp.int32, (rows, part), 0)
            count = jnp.zeros((rows, part), F32)
            for b in range(ids.shape[0]):
                count = count + jnp.where(row == ids[b : b + 1, :], 1.0, 0.0)
            count = count.astype(BF16)
            counts[t, chunk] = count
            total = dot1(both, count, NN)
            out[t * width : (t + 1) * width, :] = total[:width] + total[width:]


def pool_far_kernel(idx, bag_hbm, touch_hbm, elapsed_hbm, tables_hbm, p0, p1, p2, p3, counts, decayed, bag, touch, elapsed, tables, sems):
    pairs = ((bag_hbm, bag), (touch_hbm, touch), (elapsed_hbm, elapsed), (tables_hbm, tables))
    copies = [pltpu.make_async_copy(a, b, sems.at[n]) for n, (a, b) in enumerate(pairs)]
    for copy in copies:
        copy.start()
    for copy in copies:
        copy.wait()
    decay(touch, elapsed, tables, decayed)
    pool_half(idx, 1 - idx[1], bag, decayed, (p0, p1, p2, p3), counts)


def pool_near_kernel(idx, bag, decayed, p0, p1, p2, p3, counts):
    pool_half(idx, idx[1], bag, decayed, (p0, p1, p2, p3), counts)


def pack_kernel(idx, p0, p1, p2, p3, out):
    for k, ref in enumerate((p0, p1, p2, p3)):
        out[lax.rem(idx[0] + 4 - k, 4)] = ref[...]


def turn_kernel(at, w_hbm, high, low, w, sems):
    pieces, rows = w.shape[:2]
    copies = [pltpu.make_async_copy(w_hbm.at[pl.ds((at * pieces + n) * rows, rows)], w.at[n], sems.at[n]) for n in range(pieces)]
    for copy in copies:
        copy.start()
    for n, copy in enumerate(copies):
        copy.wait()
        flat = w.at[n].reshape(rows * 16, 128)
        for t in range(2):
            for b in range(8):
                h, l = halves(flat[pl.ds(b * 2 + t, rows, stride=16), :].T)
                high[t, b * 128 : (b + 1) * 128, n * rows : (n + 1) * rows] = h
                low[t, b * 128 : (b + 1) * 128, n * rows : (n + 1) * rows] = l


def pick_kernel(idx, w_hbm, head, high, low, column, w, wide, sems):
    rows = w.shape[1]
    quad = 2 * idx[1] + idx[2]
    copies = []
    for k in range(4):
        table = lax.rem(idx[0] + k, 4) * 4 + quad
        copies.append(pltpu.make_async_copy(w_hbm.at[pl.ds(pl.multiple_of(table * rows, rows), rows)], w.at[k], sems.at[k]))
    for copy in copies:
        copy.start()
    wide[...] = jnp.broadcast_to(head[...], (128, head.shape[1])).T
    device = (idx[0] * 2 + idx[1]) * 2 + idx[2]
    column[...] = wide[pl.ds(pl.multiple_of(device * 32, 32), 32), :]
    for k, copy in enumerate(copies):
        copy.wait()
        flat = w.at[k].reshape(rows * 16, 128)
        for t in range(2):
            for b in range(8):
                h, l = halves(flat[pl.ds(b * 2 + t, rows, stride=16), :])
                high[t, k * rows : (k + 1) * rows, b * 128 : (b + 1) * 128] = h
                low[t, k * rows : (k + 1) * rows, b * 128 : (b + 1) * 128] = l


def prepare_kernel(idx, second, lift_hbm, press_hbm, heads, high_t, low_t, lift, press, head, sems):
    tower = idx[3]
    rows = pl.ds(pl.multiple_of(tower * lift.shape[0], lift.shape[0]), lift.shape[0])
    pairs = ((lift_hbm.at[rows, :], lift), (press_hbm.at[rows, :], press))
    copies = [pltpu.make_async_copy(a, b, sems.at[n]) for n, (a, b) in enumerate(pairs)]
    for copy in copies:
        copy.start()
    head[...] = jnp.concatenate([heads[pl.ds(tower * 4 + b, 1), :] for b in range(4)], axis=1)
    count = second.shape[0]
    flat = second.reshape(count * 4, 128)
    for t in range(2):
        for b in range(2):
            lanes = slice(b * 128, (b + 1) * 128)
            h, l = halves(flat[pl.ds(b * 2 + t, count, stride=4), :].T)
            high_t[t, lanes, :] = h
            low_t[t, lanes, :] = l
    for copy in copies:
        copy.wait()


def natural_kernel(w, high, low):
    rows = w.shape[0]
    flat = w.reshape(rows * 4, 128)
    for t in range(2):
        for b in range(2):
            lanes = slice(b * 128, (b + 1) * 128)
            h, l = halves(flat[pl.ds(b * 2 + t, rows, stride=4), :])
            high[t, :, lanes] = h
            low[t, :, lanes] = l


def forward_kernel(towers, with_pay, idx, x1, x2, y1, y2, w1ha, w1la, w1hb, w1lb, w2h, w2l, press, lift, head, hidden, start, *rest):
    fh, fl = rest[-2:]
    sets = (x1, x2, y1, y2)
    zs, pair, samples = x1.shape
    width = pair // 2
    xh, core = idx[1], idx[2]
    place = ((xh, core), (1 - xh, core), (xh, 1 - core), (1 - xh, 1 - core))
    width_out = w2h.shape[1]

    def one_tower(t, slot):
        for (a, b), ref in zip(place, sets):
            for z in range(zs):
                h, l = halves(ref[z, pl.ds(pl.multiple_of(t * width, width), width), :])
                at = pl.multiple_of(((z * 2 + a) * 2 + b) * width, width)
                fh[pl.ds(at, width), :] = h
                fl[pl.ds(at, width), :] = l
        deep = w1ha.shape[2]
        value = dot3((w1ha[t], w1la[t]), (fh[0:deep, :], fl[0:deep, :]))
        value = value + dot3((w1hb[t], w1lb[t]), (fh[deep:, :], fl[deep:, :]))
        hidden[slot] = value
        act = halves(value * jax.nn.sigmoid(value))
        start[pl.ds(pl.multiple_of(slot * width_out, width_out), width_out), :] = dot3((w2h[t], w2l[t]), act)

    if len(towers) == 2:

        def step(t, carry):
            one_tower(t, t)
            return carry

        lax.fori_loop(0, 2, step, 0)
    else:
        one_tower(towers[0], 0)
    if with_pay:
        pay = rest[0]
        own = samples // 2
        rank = press.shape[1]
        x0 = halves(start[:, pl.ds(pl.multiple_of(core * own, own), own)])
        p = dot3(halves(press[...].T), x0)
        q = dot3(halves(lift[...].T * head[...]), x0)
        d = dot3(halves(jnp.broadcast_to(head[...], (8, head.shape[1]))), x0)
        pay[0:rank, :] = p
        pay[rank : 2 * rank, :] = q
        pay[2 * rank : 2 * rank + 8, :] = d


def logit_kernel(idx, mine, other, labels, pay, logits):
    total = mine[...] + other[...]
    rank = (total.shape[0] - 8) // 2
    value = jnp.sum(total[0:rank] * total[rank : 2 * rank], axis=0, keepdims=True) + total[2 * rank : 2 * rank + 1]
    turned = pltpu.roll(jnp.broadcast_to(value, (8, 128)), lax.rem(128 - 16 * idx[3], 128), 1)
    logits[...] = turned[0:1, 0:16]
    error = jax.nn.sigmoid(value) - labels[...].astype(F32)
    pay[0 : 2 * rank, :] = total[0 : 2 * rank]
    pay[2 * rank : 2 * rank + 8, :] = jnp.broadcast_to(error, (8, error.shape[1]))


def grads_kernel(towers, with_pq, extra, idx, mine, other, hidden, w1h, w1l, w2h, w2l, press, lift, head, *refs):
    ghh, ghl, gout, g0, g1, g2, g3, *pq = refs[extra:]
    rank = press.shape[1]
    width = w1h.shape[1] // 4
    width_out = w2h.shape[2]
    first_core = idx[2] == 0
    left = jnp.where(first_core, mine[...], other[...])
    right = jnp.where(first_core, other[...], mine[...])
    both = jnp.concatenate([left, right], axis=1)
    error = both[2 * rank : 2 * rank + 1]
    if with_pq:
        pq[0][...] = error * both[0 : 2 * rank]
    p, q = halves(both[0:rank]), halves(both[rank : 2 * rank])
    column = jnp.broadcast_to(head[...], (128, head.shape[1])).T[:, 0:1]
    for slot, t in enumerate(towers):
        rows = slice(t * width_out, (t + 1) * width_out)
        scaling = dot3(halves(lift[rows, :]), p)
        back = dot3(halves(press[rows, :]), q)
        go = error * (column[rows] * (scaling + 1.0) + back)
        gout[slot] = go
        go = halves(go)
        grad = None
        for n in range(w2h.shape[1] // PIECE):
            part = slice(n * PIECE, (n + 1) * PIECE)
            ga = dot3((w2h[t, part, :], w2l[t, part, :]), go)
            value = hidden[slot, part, :]
            s = jax.nn.sigmoid(value)
            gh = halves(ga * (s * (1.0 + value * (1.0 - s))))
            ghh[slot, part, :] = gh[0]
            ghl[slot, part, :] = gh[1]
            out = dot3((w1h[t, :, part], w1l[t, :, part]), gh)
            grad = out if grad is None else grad + out
        for k, out in enumerate((g0, g1, g2, g3)):
            out[slot] = grad[k * width : (k + 1) * width]


def weights_kernel(t, riders, idx, near, far, ghha, ghla, ghhb, ghlb, gouta, goutb, hid_a, hid_b, *rest):
    if t == 1:
        rest, far_block = rest[:-1], rest[-1]
    blocks, rest = rest[-4:], rest[:-4]
    z, quad = idx[0], 2 * idx[1] + idx[2]
    width = near.shape[1] // 2
    rows = slice(t * width, (t + 1) * width)
    fa, fb, acta, actb = [], [], [], []
    for k in range(4):
        at = lax.rem(z + k, 4)
        fa.append(near[at, rows, :])
        fb.append(far[at, rows, :])
        pick = pl.ds(pl.multiple_of((at * 4 + quad) * width, width), width)
        value = hid_a[t, pick, :]
        acta.append(value * jax.nn.sigmoid(value))
        value = hid_b[0, pick, :]
        actb.append(value * jax.nn.sigmoid(value))
    join = lambda parts: halves(jnp.concatenate(parts, axis=0))
    grad = dot3(join(fa), (ghha[t], ghla[t]), NT) + dot3(join(fb), (ghhb[0], ghlb[0]), NT)
    for k in range(4):
        blocks[k][0:width, :] = grad[k * width : (k + 1) * width]
    grad = dot3(join(acta), halves(gouta[t]), NT) + dot3(join(actb), halves(goutb[0]), NT)
    for k in range(4):
        for b in range(4):
            blocks[k][width : width + 16, b * 256 : (b + 1) * 256] = grad[k * width + 16 * b : k * width + 16 * b + 16]
    low = width // 4
    for n, k in enumerate(riders):
        base = blocks[k].shape[0] - low
        for b in range(4):
            blocks[k][base:, b * 256 : (b + 1) * 256] = rest[n][0, b * low : (b + 1) * low, :]
    if t == 1:
        x0a, x0b0, x0b1, pqa, pqb, gb0, gb1 = rest[2:]
        for n, gb in enumerate((gb0, gb1)):
            for b in range(4):
                far_block[n * low : (n + 1) * low, b * 256 : (b + 1) * 256] = gb[0, b * low : (b + 1) * low, :]
        parts_a, parts_b = [], []
        for k in range(4):
            block = lax.rem(z + k, 4) * 4 + quad
            parts_a.append(x0a[pl.ds(pl.multiple_of(block * 32, 32), 32), :])
            inner = pl.ds(pl.multiple_of(lax.rem(block, 8) * 32, 32), 32)
            parts_b.append(jnp.where(block < 8, x0b0[inner, :], x0b1[inner, :]))
        both = dot3(join(parts_a), halves(pqa[...]), NT) + dot3(join(parts_b), halves(pqb[...]), NT)
        for k in range(4):
            for b in range(4):
                blocks[k][width + 16 : width + 24, b * 256 : (b + 1) * 256] = both[32 * k + 8 * b : 32 * k + 8 * b + 8]


def update_kernel(idx, ga0, ga1, ga2, ga3, gb0, gb1, w_up, w_down, v_up, v_down, opposite, near, far, decayed, accumulator, new_tables, new_accumulator):
    z = idx[0]
    towers, width, rows = decayed.shape
    low = width // 4

    def rider(ref, start=None):
        start = ref.shape[0] - low if start is None else start
        block = ref[start : start + low, :]
        return jnp.concatenate([block[:, b * 256 : (b + 1) * 256] for b in range(4)], axis=0)

    for t in range(towers):
        pieces = (
            (ga0[t], (gb0, gb1)[t][0]),
            (ga1[t], rider((w_up, v_up)[t])),
            (ga2[t], rider(opposite, low * t)),
            (ga3[t], rider((w_down, v_down)[t])),
        )
        total = jnp.zeros((2 * width, rows), F32)
        for k, (a, b) in enumerate(pieces):
            at = lax.rem(z + 4 - k, 4)
            total = total + dot1(jnp.concatenate(halves(a), axis=0), near[t, at], NT)
            total = total + dot1(jnp.concatenate(halves(b), axis=0), far[t, at], NT)
        grad = total[:width] + total[width:]
        square = jnp.sum(grad * grad, axis=0, keepdims=True) * (1.0 / width)
        fresh = accumulator[t : t + 1, :] + square
        new_accumulator[t : t + 1, :] = fresh
        new_tables[t] = decayed[t] - LEARN_RATE * grad / (jnp.sqrt(fresh) + EPSILON)


def sum_kernel(column, *refs):
    parts, (first, second, lift, press) = refs[:6], refs[6:]
    for t in range(2):
        a, b, c = parts[3 * t : 3 * t + 3]
        total = a[...] + (b[0 : a.shape[0]] + c[0 : a.shape[0]])
        for k in range(8):
            first[pl.ds(2 * k + t, 64, stride=16), :] = total[0:64, k * 128 : (k + 1) * 128]
        for b in range(4):
            for o in range(2):
                lanes = slice(b * 256 + o * 128, b * 256 + (o + 1) * 128)
                second[pl.ds(b * 64 + 2 * o + t, 16, stride=4), :] = total[64:80, lanes]
        if t == 1:
            for b in range(4):
                at = slice(8 * b, 8 * b + 8)
                lift[at, :] = column[at] * total[80:88, b * 256 : b * 256 + 128]
                press[at, :] = total[80:88, b * 256 + 128 : (b + 1) * 256]


def shift(x, axis, size, by):
    return lax.ppermute(x, axis, [(i, (i + by) % size) for i in range(size)])


def flip(x, axis, size, bit):
    return lax.ppermute(x, axis, [(i, i ^ bit) for i in range(size)])


def per_device(bag_ids, touch_ids, elapsed, tables, accumulator, first_weight, second_weight, lift_weight, press_weight, head_weight, labels):
    f32 = lambda *shape: jax.ShapeDtypeStruct(shape, F32)
    bf16 = lambda *shape: jax.ShapeDtypeStruct(shape, BF16)
    axes = [lax.axis_index(name) for name in ("z", "xh", "core", TOWER)]
    idx = jnp.stack(axes).astype(jnp.int32)
    rank = lift_weight.shape[1]
    local = lift_weight.shape[0] // 8
    any_spec = pl.BlockSpec(memory_space=pl.ANY)

    tables_t = jnp.transpose(tables[:, 0], (0, 2, 1))
    bag = bag_ids[:, 0]
    hbm = lambda x: pltpu.with_memory_space_constraint(x, pltpu.HBM)
    *far, counts_far, decayed, bag_here = call(
        pool_far_kernel,
        [f32(128, 256)] * 4 + [bf16(2, 4, 512, 256), f32(2, 64, 512), jax.ShapeDtypeStruct((2, 4, 2048), jnp.int32)],
        [SMEM_SPEC] + [any_spec] * 4,
        [
            pltpu.VMEM((2, 128), jnp.int32),
            pltpu.VMEM((2, 128), jnp.int32),
            pltpu.VMEM((2, 64, 512), F32),
            pltpu.SemaphoreType.DMA((4,)),
        ],
        name="pool_far",
        flops=1e6,
    )(idx, hbm(bag), hbm(touch_ids[:, 0]), hbm(elapsed[:, 0]), hbm(tables_t))
    pack = call(pack_kernel, [f32(4, 128, 256)], [SMEM_SPEC] + vmem(4), name="pack", flops=1e6)
    far = [far[0]] + [shift(far[k], "z", 4, k) for k in (1, 2, 3)]
    *near, counts_near = call(
        pool_near_kernel, [f32(128, 256)] * 4 + [bf16(2, 4, 512, 256)], [SMEM_SPEC] + vmem(2), name="pool_near", flops=1e6
    )(idx, bag_here, decayed)
    view = first_weight.reshape(1024, 2, 8, 128).transpose(0, 2, 1, 3).reshape(1024, 16, 128)

    def turn(view, at):
        return pl.pallas_call(
            lambda *refs: turn_kernel(at, *refs),
            in_specs=[any_spec],
            out_specs=vmem(2),
            out_shape=[bf16(2, 1024, 512)] * 2,
            scratch_shapes=[pltpu.VMEM((4, 128, 16, 128), F32), pltpu.SemaphoreType.DMA((4,))],
            compiler_params=pltpu.CompilerParams(vmem_limit_bytes=VMEM_LIMIT),
            cost_estimate=pl.CostEstimate(flops=int(1e6), transcendentals=0, bytes_accessed=1 << 20),
            name="turn_%d" % at,
        )(hbm(view))

    view, _ = lax.optimization_barrier((view, decayed))
    w1ha, w1la = turn(view, 0)
    *far, _, _ = lax.optimization_barrier((*far, near[0], w1ha))
    (fq_far,) = pack(idx, *far)
    x2 = flip(fq_far, "xh", 2, 1)
    near = [near[0]] + [shift(near[k], "z", 4, k) for k in (1, 2, 3)]
    view, _ = lax.optimization_barrier((view, fq_far))
    w1hb, w1lb = turn(view, 1)
    *near, _ = lax.optimization_barrier((*near, w1hb))
    (fq_near,) = pack(idx, *near)
    y1 = flip(fq_near, "core", 2, 1)
    y2 = flip(x2, "core", 2, 1)
    x2b = flip(fq_near, "xh", 2, 1)
    y1b = flip(fq_far, "core", 2, 1)
    y2b = flip(x2b, "core", 2, 1)

    _, lift_weight, press_weight = lax.optimization_barrier((w1hb, lift_weight, press_weight))
    second_view = second_weight.reshape(1024, 2, 2, 128).transpose(0, 2, 1, 3).reshape(1024, 4, 128)
    w2th, w2tl, lift, press, head = call(
        prepare_kernel,
        [bf16(2, 256, 1024)] * 2 + [f32(local, rank), f32(local, rank), f32(1, local)],
        [SMEM_SPEC] + vmem(1) + [any_spec] * 2 + vmem(1),
        [pltpu.SemaphoreType.DMA((2,))],
        name="prepare",
        flops=1e6,
    )(idx, second_view, hbm(lift_weight), hbm(press_weight), head_weight.reshape(32, 128))

    scratch = [pltpu.VMEM((1024, 256), BF16)] * 2
    weights = (w1ha, w1la, w1hb, w1lb, w2th, w2tl, press, lift, head)
    hid_a, x0a, pay = call(
        lambda *refs: forward_kernel((0, 1), True, *refs),
        [f32(2, 1024, 256), f32(512, 256), f32(2 * rank + 8, 128)],
        [SMEM_SPEC] + vmem(13),
        scratch,
        name="forward_a",
        flops=1e6,
    )(idx, fq_near, x2, y1, y2, *weights)

    def later_half(at, t, y2b):
        return call(
            lambda *refs: forward_kernel((t,), False, *refs),
            [f32(1, 1024, 256), f32(256, 256)],
            [SMEM_SPEC] + vmem(13),
            scratch,
            name="forward_b%d" % t,
            flops=4e9,
        )(at, fq_far, x2b, y1b, y2b, *weights)

    view, second_view, pay = lax.optimization_barrier((view, second_view, pay))
    other = flip(pay, TOWER, 8, 1)
    w1qh, w1ql, column = call(
        pick_kernel,
        [bf16(2, 256, 1024)] * 2 + [f32(32, 128)],
        [SMEM_SPEC, any_spec] + vmem(1),
        [pltpu.VMEM((4, 64, 16, 128), F32), pltpu.VMEM((local, 128), F32), pltpu.SemaphoreType.DMA((4,))],
        name="pick",
        flops=1e6,
    )(idx, hbm(view), head)
    w2h, w2l = call(natural_kernel, [bf16(2, 1024, 256)] * 2, vmem(1), name="natural", flops=1e6)(second_view)
    other, w1qh, w2h, x2b = lax.optimization_barrier((other, w1qh, w2h, x2b))
    pay = pay + other
    after, pay = lax.optimization_barrier((idx, pay))
    other = flip(pay, TOWER, 8, 2)
    y2b = flip(x2b, "core", 2, 1)
    hid_b0, x0b0 = later_half(after, 0, y2b)
    other, x0b0 = lax.optimization_barrier((other, x0b0))
    pay = pay + other
    after, pay = lax.optimization_barrier((idx, pay))
    other = flip(pay, TOWER, 8, 6)
    hid_b1, x0b1 = later_half(after, 1, y2b)
    other, x0b1 = lax.optimization_barrier((other, x0b1))
    pay, logits = call(logit_kernel, [f32(2 * rank + 8, 128), f32(1, 16)], [SMEM_SPEC] + vmem(3), name="logit", flops=1e6)(
        idx, pay, other, labels
    )
    c1 = flip(pay, "core", 2, 1)
    xa = flip(pay, "xh", 2, 1)

    def grads(towers, with_pq, mine, other, hidden, name, flops, extra=()):
        n = len(towers)
        return call(
            lambda *refs: grads_kernel(towers, with_pq, len(extra), *refs),
            [bf16(n, 1024, 256)] * 2 + [f32(n, 256, 256)] + [f32(n, 64, 256)] * 4 + [f32(2 * rank, 256)] * with_pq,
            [SMEM_SPEC] + vmem(10 + len(extra)),
            name=name,
            flops=flops,
        )(idx, mine, other, hidden, w1qh, w1ql, w2h, w2l, press, lift, head, *extra)

    ghha, ghla, gouta, *ga, pqa = grads((0, 1), True, pay, c1, hid_a, "grads_a", 4e9)

    gone = [shift(ga[k], "z", 4, k) for k in (1, 2, 3)]
    xa, pqa = lax.optimization_barrier((xa, pqa))
    xb = flip(xa, "core", 2, 1)

    def weights_of(t, riders, rows, ghhb, ghlb, goutb, hid_b, extra):
        return call(
            lambda *refs: weights_kernel(t, riders, *refs),
            [f32(n, 1024) for n in rows],
            [SMEM_SPEC] + vmem(10 + len(extra)),
            name="weights_%d" % t,
            flops=3e9,
        )(idx, fq_near, fq_far, ghha, ghla, ghhb, ghlb, gouta, goutb, hid_a, hid_b, *extra)

    ghh0, ghl0, gout0, *gb0, pqb = grads((0,), True, xa, xb, hid_b0, "grads_b0", 4e9)
    w = weights_of(0, (2, 3), (80, 80, 96, 96), ghh0, ghl0, gout0, hid_b0, (gb0[1], gb0[3]))
    up = shift(w[2], "z", 4, 1)
    w3 = shift(w[3], "z", 4, 3)
    ghh1, ghl1, gout1, *gb1 = grads((1,), False, xa, xb, hid_b1, "grads_b1", 4e9, gone)
    v = weights_of(
        1,
        (1, 2),
        (88, 104, 104, 88, 32),
        ghh1,
        ghl1,
        gout1,
        hid_b1,
        (gb1[1], gb1[3], x0a, x0b0, x0b1, pqa, pqb, gb0[2], gb1[2]),
    )
    down = shift(v[2], "z", 4, 3)
    v1 = shift(v[1], "z", 4, 1)
    g2 = shift(v[4], "z", 4, 2)
    up, w3 = lax.optimization_barrier((up, w3))
    down, v1 = lax.optimization_barrier((down, v1))
    w1 = shift(w[1] + up[0:80], "z", 4, 1)
    v3 = shift(v[3] + down[0:88], "z", 4, 3)
    new_tables, new_accumulator = call(
        update_kernel, [f32(2, 64, 512), f32(2, 512)], [SMEM_SPEC] + vmem(15), name="update", flops=5e9
    )(idx, ga[0], *gone, gb0[0], gb1[0], up, w3, v1, down, g2, counts_near, counts_far, decayed, accumulator[:, 0])
    first, second, lift_out, press_out = call(
        sum_kernel,
        [f32(1024, 128), f32(256, 128), f32(32, rank), f32(32, rank)],
        vmem(7),
        name="sum",
        flops=1e6,
    )(column, w[0], w1, w3, v[0], v1, v3)
    return (
        jnp.transpose(new_tables, (0, 2, 1))[:, None],
        new_accumulator[:, None],
        first.reshape(64, 8, 2, 128).transpose(0, 2, 1, 3).reshape(64, 2, 1024),
        second.reshape(64, 2, 2, 128).transpose(0, 2, 1, 3).reshape(64, 2, 256),
        lift_out,
        press_out,
        logits,
    )


def solution(mesh):
    split = Mesh(mesh.devices.reshape(4, 2, 4, 2, 2), ("y", "xl", "z", "xh", "core"))
    member = ("z", "xh", "core")
    placed = (
        P(TOWER, member, None, None),
        P(TOWER, member, None),
        P(TOWER, member, None),
        P(TOWER, member, None, None),
        P(TOWER, member, None),
        P(None, TOWER, None),
        P(None, TOWER, None),
        P(),
        P(),
        P(),
        P(member, None),
    )
    return jax.shard_map(
        per_device,
        mesh=split,
        in_specs=placed,
        out_specs=(
            P(TOWER, member, None, None),
            P(TOWER, member, None),
            P(member, TOWER, None),
            P(member, TOWER, None),
            P(TOWER + member, None),
            P(TOWER + member, None),
            P(member, TOWER),
        ),
        check_vma=False,
    )
```

```python
import math

import jax
import jax.numpy as jnp
from jax import lax
from jax.experimental import pallas as pl
from jax.experimental.pallas import tpu as pltpu
from jax.sharding import Mesh, PartitionSpec as P

DECAY_RATE = 0.98
LEARN_RATE = 1.0
EPSILON = 1e-08
F32 = jnp.float32
BF16 = jnp.bfloat16
NN = (((1,), (0,)), ((), ()))
NT = (((1,), (1,)), ((), ()))
TOWER = ("y", "xl")
QUAD = ("xh", "core")
VMEM_LIMIT = 16 << 20
PIECE = 256


def halves(a):
    high = a.astype(BF16)
    return high, (a - high.astype(F32)).astype(BF16)


def dot1(a, b, dims):
    return lax.dot_general(a, b, dims, preferred_element_type=F32)


def dot3(a, b, dims=NN):
    return dot1(a[0], b[0], dims) + (dot1(a[0], b[1], dims) + dot1(a[1], b[0], dims))


def dot32(a, b, dims=NN):
    return dot3(halves(a), halves(b), dims)


def vmem(count):
    return [pl.BlockSpec(memory_space=pltpu.VMEM)] * count


def call(kernel, outs, spec_in, scratch=(), name=None, flops=0):
    return pl.pallas_call(
        kernel,
        cost_estimate=pl.CostEstimate(flops=int(flops), transcendentals=0, bytes_accessed=1 << 20),
        out_shape=outs,
        in_specs=spec_in,
        out_specs=vmem(len(outs)),
        scratch_shapes=list(scratch),
        compiler_params=pltpu.CompilerParams(vmem_limit_bytes=VMEM_LIMIT),
        name=name,
    )


SMEM_SPEC = pl.BlockSpec(memory_space=pltpu.SMEM)


def decay(touch, elapsed, tables, decayed):
    towers, width, rows = tables.shape
    touches = touch.shape[1]
    for t in range(towers):
        ids = jnp.broadcast_to(touch[t : t + 1, :].astype(F32), (touches, touches)).T
        rates = jnp.exp(elapsed[t : t + 1, :].astype(F32) * math.log(DECAY_RATE))
        rates = jnp.broadcast_to(rates, (touches, touches)).T
        factor = []
        for block in range(rows // touches):
            row = lax.broadcasted_iota(jnp.int32, (touches, touches), 1).astype(F32) + float(block * touches)
            match = ids == row
            hits = jnp.sum(jnp.where(match, 1.0, 0.0), axis=0, keepdims=True)
            chosen = jnp.sum(jnp.where(match, rates, 0.0), axis=0, keepdims=True)
            factor.append(jnp.where(hits > 0.0, chosen, 1.0))
        decayed[t] = tables[t] * jnp.concatenate(factor, axis=1)


def pool_half(idx, side, bag, decayed, pooled, counts):
    towers, width, rows = decayed.shape
    part = pooled[0].shape[1]
    for t in range(towers):
        both = jnp.concatenate(halves(decayed[t]), axis=0)
        for k, out in enumerate(pooled):
            chunk = lax.rem(idx[0] + k, 4)
            at = pl.multiple_of(chunk * 2 * part + side * part, part)
            ids = bag[t, :, pl.ds(at, part)]
            row = lax.broadcasted_iota(jnp.int32, (rows, part), 0)
            count = jnp.zeros((rows, part), F32)
            for b in range(ids.shape[0]):
                count = count + jnp.where(row == ids[b : b + 1, :], 1.0, 0.0)
            count = count.astype(BF16)
            counts[t, chunk] = count
            total = dot1(both, count, NN)
            out[t * width : (t + 1) * width, :] = total[:width] + total[width:]


def pool_far_kernel(idx, bag_hbm, touch_hbm, elapsed_hbm, tables_hbm, p0, p1, p2, p3, counts, decayed, bag, touch, elapsed, tables, sems):
    pairs = ((bag_hbm, bag), (touch_hbm, touch), (elapsed_hbm, elapsed), (tables_hbm, tables))
    copies = [pltpu.make_async_copy(a, b, sems.at[n]) for n, (a, b) in enumerate(pairs)]
    for copy in copies:
        copy.start()
    for copy in copies:
        copy.wait()
    decay(touch, elapsed, tables, decayed)
    pool_half(idx, 1 - idx[1], bag, decayed, (p0, p1, p2, p3), counts)


def pool_near_kernel(idx, bag, decayed, p0, p1, p2, p3, counts):
    pool_half(idx, idx[1], bag, decayed, (p0, p1, p2, p3), counts)


def pack_kernel(idx, p0, p1, p2, p3, out):
    for k, ref in enumerate((p0, p1, p2, p3)):
        out[lax.rem(idx[0] + 4 - k, 4)] = ref[...]


def turn_kernel(at, w_hbm, high, low, w, sems):
    pieces, rows = w.shape[:2]
    copies = [pltpu.make_async_copy(w_hbm.at[pl.ds((at * pieces + n) * rows, rows)], w.at[n], sems.at[n]) for n in range(pieces)]
    for copy in copies:
        copy.start()
    for n, copy in enumerate(copies):
        copy.wait()
        flat = w.at[n].reshape(rows * 16, 128)
        for t in range(2):
            for b in range(8):
                h, l = halves(flat[pl.ds(b * 2 + t, rows, stride=16), :].T)
                high[t, b * 128 : (b + 1) * 128, n * rows : (n + 1) * rows] = h
                low[t, b * 128 : (b + 1) * 128, n * rows : (n + 1) * rows] = l


def pick_kernel(idx, w_hbm, head, high, low, column, w, wide, sems):
    rows = w.shape[1]
    quad = 2 * idx[1] + idx[2]
    copies = []
    for k in range(4):
        table = lax.rem(idx[0] + k, 4) * 4 + quad
        copies.append(pltpu.make_async_copy(w_hbm.at[pl.ds(pl.multiple_of(table * rows, rows), rows)], w.at[k], sems.at[k]))
    for copy in copies:
        copy.start()
    wide[...] = jnp.broadcast_to(head[...], (128, head.shape[1])).T
    device = (idx[0] * 2 + idx[1]) * 2 + idx[2]
    column[...] = wide[pl.ds(pl.multiple_of(device * 32, 32), 32), :]
    for k, copy in enumerate(copies):
        copy.wait()
        flat = w.at[k].reshape(rows * 16, 128)
        for t in range(2):
            for b in range(8):
                h, l = halves(flat[pl.ds(b * 2 + t, rows, stride=16), :])
                high[t, k * rows : (k + 1) * rows, b * 128 : (b + 1) * 128] = h
                low[t, k * rows : (k + 1) * rows, b * 128 : (b + 1) * 128] = l


def prepare_kernel(idx, second, lift_hbm, press_hbm, heads, high_t, low_t, lift, press, head, sems):
    tower = idx[3]
    rows = pl.ds(pl.multiple_of(tower * lift.shape[0], lift.shape[0]), lift.shape[0])
    pairs = ((lift_hbm.at[rows, :], lift), (press_hbm.at[rows, :], press))
    copies = [pltpu.make_async_copy(a, b, sems.at[n]) for n, (a, b) in enumerate(pairs)]
    for copy in copies:
        copy.start()
    head[...] = jnp.concatenate([heads[pl.ds(tower * 4 + b, 1), :] for b in range(4)], axis=1)
    count = second.shape[0]
    flat = second.reshape(count * 4, 128)
    for t in range(2):
        for b in range(2):
            lanes = slice(b * 128, (b + 1) * 128)
            h, l = halves(flat[pl.ds(b * 2 + t, count, stride=4), :].T)
            high_t[t, lanes, :] = h
            low_t[t, lanes, :] = l
    for copy in copies:
        copy.wait()


def natural_kernel(w, high, low):
    rows = w.shape[0]
    flat = w.reshape(rows * 4, 128)
    for t in range(2):
        for b in range(2):
            lanes = slice(b * 128, (b + 1) * 128)
            h, l = halves(flat[pl.ds(b * 2 + t, rows, stride=4), :])
            high[t, :, lanes] = h
            low[t, :, lanes] = l


def forward_kernel(towers, with_pay, idx, x1, x2, y1, y2, w1ha, w1la, w1hb, w1lb, w2h, w2l, press, lift, head, hidden, start, *rest):
    fh, fl = rest[-2:]
    sets = (x1, x2, y1, y2)
    zs, pair, samples = x1.shape
    width = pair // 2
    xh, core = idx[1], idx[2]
    place = ((xh, core), (1 - xh, core), (xh, 1 - core), (1 - xh, 1 - core))
    width_out = w2h.shape[1]

    def one_tower(t, slot):
        for (a, b), ref in zip(place, sets):
            for z in range(zs):
                h, l = halves(ref[z, pl.ds(pl.multiple_of(t * width, width), width), :])
                at = pl.multiple_of(((z * 2 + a) * 2 + b) * width, width)
                fh[pl.ds(at, width), :] = h
                fl[pl.ds(at, width), :] = l
        deep = w1ha.shape[2]
        value = dot3((w1ha[t], w1la[t]), (fh[0:deep, :], fl[0:deep, :]))
        value = value + dot3((w1hb[t], w1lb[t]), (fh[deep:, :], fl[deep:, :]))
        hidden[slot] = value
        act = halves(value * jax.nn.sigmoid(value))
        start[pl.ds(pl.multiple_of(slot * width_out, width_out), width_out), :] = dot3((w2h[t], w2l[t]), act)

    if len(towers) == 2:

        def step(t, carry):
            one_tower(t, t)
            return carry

        lax.fori_loop(0, 2, step, 0)
    else:
        one_tower(towers[0], 0)
    if with_pay:
        pay = rest[0]
        own = samples // 2
        rank = press.shape[1]
        x0 = halves(start[:, pl.ds(pl.multiple_of(core * own, own), own)])
        p = dot3(halves(press[...].T), x0)
        q = dot3(halves(lift[...].T * head[...]), x0)
        d = dot3(halves(jnp.broadcast_to(head[...], (8, head.shape[1]))), x0)
        pay[0:rank, :] = p
        pay[rank : 2 * rank, :] = q
        pay[2 * rank : 2 * rank + 8, :] = d


def logit_kernel(idx, mine, other, labels, pay, logits):
    total = mine[...] + other[...]
    rank = (total.shape[0] - 8) // 2
    value = jnp.sum(total[0:rank] * total[rank : 2 * rank], axis=0, keepdims=True) + total[2 * rank : 2 * rank + 1]
    turned = pltpu.roll(jnp.broadcast_to(value, (8, 128)), lax.rem(128 - 16 * idx[3], 128), 1)
    logits[...] = turned[0:1, 0:16]
    error = jax.nn.sigmoid(value) - labels[...].astype(F32)
    pay[0 : 2 * rank, :] = total[0 : 2 * rank]
    pay[2 * rank : 2 * rank + 8, :] = jnp.broadcast_to(error, (8, error.shape[1]))


def grads_kernel(towers, with_pq, extra, idx, mine, other, hidden, w1h, w1l, w2h, w2l, press, lift, head, *refs):
    ghh, ghl, gout, g0, g1, g2, g3, *pq = refs[extra:]
    rank = press.shape[1]
    width = w1h.shape[1] // 4
    width_out = w2h.shape[2]
    first_core = idx[2] == 0
    left = jnp.where(first_core, mine[...], other[...])
    right = jnp.where(first_core, other[...], mine[...])
    both = jnp.concatenate([left, right], axis=1)
    error = both[2 * rank : 2 * rank + 1]
    if with_pq:
        pq[0][...] = error * both[0 : 2 * rank]
    p, q = halves(both[0:rank]), halves(both[rank : 2 * rank])
    column = jnp.broadcast_to(head[...], (128, head.shape[1])).T[:, 0:1]
    for slot, t in enumerate(towers):
        rows = slice(t * width_out, (t + 1) * width_out)
        scaling = dot3(halves(lift[rows, :]), p)
        back = dot3(halves(press[rows, :]), q)
        go = error * (column[rows] * (scaling + 1.0) + back)
        gout[slot] = go
        go = halves(go)
        grad = None
        for n in range(w2h.shape[1] // PIECE):
            part = slice(n * PIECE, (n + 1) * PIECE)
            ga = dot3((w2h[t, part, :], w2l[t, part, :]), go)
            value = hidden[slot, part, :]
            s = jax.nn.sigmoid(value)
            gh = halves(ga * (s * (1.0 + value * (1.0 - s))))
            ghh[slot, part, :] = gh[0]
            ghl[slot, part, :] = gh[1]
            out = dot3((w1h[t, :, part], w1l[t, :, part]), gh)
            grad = out if grad is None else grad + out
        for k, out in enumerate((g0, g1, g2, g3)):
            out[slot] = grad[k * width : (k + 1) * width]


def weights_kernel(t, riders, idx, near, far, ghha, ghla, ghhb, ghlb, gouta, goutb, hid_a, hid_b, *rest):
    if t == 1:
        rest, far_block = rest[:-1], rest[-1]
    blocks, rest = rest[-4:], rest[:-4]
    z, quad = idx[0], 2 * idx[1] + idx[2]
    width = near.shape[1] // 2
    rows = slice(t * width, (t + 1) * width)
    fa, fb, acta, actb = [], [], [], []
    for k in range(4):
        at = lax.rem(z + k, 4)
        fa.append(near[at, rows, :])
        fb.append(far[at, rows, :])
        pick = pl.ds(pl.multiple_of((at * 4 + quad) * width, width), width)
        value = hid_a[t, pick, :]
        acta.append(value * jax.nn.sigmoid(value))
        value = hid_b[0, pick, :]
        actb.append(value * jax.nn.sigmoid(value))
    join = lambda parts: halves(jnp.concatenate(parts, axis=0))
    grad = dot3(join(fa), (ghha[t], ghla[t]), NT) + dot3(join(fb), (ghhb[0], ghlb[0]), NT)
    for k in range(4):
        blocks[k][0:width, :] = grad[k * width : (k + 1) * width]
    grad = dot3(join(acta), halves(gouta[t]), NT) + dot3(join(actb), halves(goutb[0]), NT)
    for k in range(4):
        for b in range(4):
            blocks[k][width : width + 16, b * 256 : (b + 1) * 256] = grad[k * width + 16 * b : k * width + 16 * b + 16]
    low = width // 4
    for n, k in enumerate(riders):
        base = blocks[k].shape[0] - low
        for b in range(4):
            blocks[k][base:, b * 256 : (b + 1) * 256] = rest[n][0, b * low : (b + 1) * low, :]
    if t == 1:
        x0a, x0b0, x0b1, pqa, pqb, gb0, gb1 = rest[2:]
        for n, gb in enumerate((gb0, gb1)):
            for b in range(4):
                far_block[n * low : (n + 1) * low, b * 256 : (b + 1) * 256] = gb[0, b * low : (b + 1) * low, :]
        parts_a, parts_b = [], []
        for k in range(4):
            block = lax.rem(z + k, 4) * 4 + quad
            parts_a.append(x0a[pl.ds(pl.multiple_of(block * 32, 32), 32), :])
            inner = pl.ds(pl.multiple_of(lax.rem(block, 8) * 32, 32), 32)
            parts_b.append(jnp.where(block < 8, x0b0[inner, :], x0b1[inner, :]))
        both = dot3(join(parts_a), halves(pqa[...]), NT) + dot3(join(parts_b), halves(pqb[...]), NT)
        for k in range(4):
            for b in range(4):
                blocks[k][width + 16 : width + 24, b * 256 : (b + 1) * 256] = both[32 * k + 8 * b : 32 * k + 8 * b + 8]


def update_kernel(idx, ga0, ga1, ga2, ga3, gb0, gb1, w_up, w_down, v_up, v_down, opposite, near, far, decayed, accumulator, new_tables, new_accumulator):
    z = idx[0]
    towers, width, rows = decayed.shape
    low = width // 4

    def rider(ref, start=None):
        start = ref.shape[0] - low if start is None else start
        block = ref[start : start + low, :]
        return jnp.concatenate([block[:, b * 256 : (b + 1) * 256] for b in range(4)], axis=0)

    for t in range(towers):
        pieces = (
            (ga0[t], (gb0, gb1)[t][0]),
            (ga1[t], rider((w_up, v_up)[t])),
            (ga2[t], rider(opposite, low * t)),
            (ga3[t], rider((w_down, v_down)[t])),
        )
        total = jnp.zeros((2 * width, rows), F32)
        for k, (a, b) in enumerate(pieces):
            at = lax.rem(z + 4 - k, 4)
            total = total + dot1(jnp.concatenate(halves(a), axis=0), near[t, at], NT)
            total = total + dot1(jnp.concatenate(halves(b), axis=0), far[t, at], NT)
        grad = total[:width] + total[width:]
        square = jnp.sum(grad * grad, axis=0, keepdims=True) * (1.0 / width)
        fresh = accumulator[t : t + 1, :] + square
        new_accumulator[t : t + 1, :] = fresh
        new_tables[t] = decayed[t] - LEARN_RATE * grad / (jnp.sqrt(fresh) + EPSILON)


def sum_kernel(column, *refs):
    parts, (first, second, lift, press) = refs[:6], refs[6:]
    for t in range(2):
        a, b, c = parts[3 * t : 3 * t + 3]
        total = a[...] + (b[0 : a.shape[0]] + c[0 : a.shape[0]])
        for k in range(8):
            first[pl.ds(2 * k + t, 64, stride=16), :] = total[0:64, k * 128 : (k + 1) * 128]
        for b in range(4):
            for o in range(2):
                lanes = slice(b * 256 + o * 128, b * 256 + (o + 1) * 128)
                second[pl.ds(b * 64 + 2 * o + t, 16, stride=4), :] = total[64:80, lanes]
        if t == 1:
            for b in range(4):
                at = slice(8 * b, 8 * b + 8)
                lift[at, :] = column[at] * total[80:88, b * 256 : b * 256 + 128]
                press[at, :] = total[80:88, b * 256 + 128 : (b + 1) * 256]


def shift(x, axis, size, by):
    return lax.ppermute(x, axis, [(i, (i + by) % size) for i in range(size)])


def flip(x, axis, size, bit):
    return lax.ppermute(x, axis, [(i, i ^ bit) for i in range(size)])


def per_device(bag_ids, touch_ids, elapsed, tables, accumulator, first_weight, second_weight, lift_weight, press_weight, head_weight, labels):
    f32 = lambda *shape: jax.ShapeDtypeStruct(shape, F32)
    bf16 = lambda *shape: jax.ShapeDtypeStruct(shape, BF16)
    axes = [lax.axis_index(name) for name in ("z", "xh", "core", TOWER)]
    idx = jnp.stack(axes).astype(jnp.int32)
    rank = lift_weight.shape[1]
    local = lift_weight.shape[0] // 8
    any_spec = pl.BlockSpec(memory_space=pl.ANY)

    tables_t = jnp.transpose(tables[:, 0], (0, 2, 1))
    bag = bag_ids[:, 0]
    hbm = lambda x: pltpu.with_memory_space_constraint(x, pltpu.HBM)
    *far, counts_far, decayed, bag_here = call(
        pool_far_kernel,
        [f32(128, 256)] * 4 + [bf16(2, 4, 512, 256), f32(2, 64, 512), jax.ShapeDtypeStruct((2, 4, 2048), jnp.int32)],
        [SMEM_SPEC] + [any_spec] * 4,
        [
            pltpu.VMEM((2, 128), jnp.int32),
            pltpu.VMEM((2, 128), jnp.int32),
            pltpu.VMEM((2, 64, 512), F32),
            pltpu.SemaphoreType.DMA((4,)),
        ],
        name="pool_far",
        flops=1e6,
    )(idx, hbm(bag), hbm(touch_ids[:, 0]), hbm(elapsed[:, 0]), hbm(tables_t))
    pack = call(pack_kernel, [f32(4, 128, 256)], [SMEM_SPEC] + vmem(4), name="pack", flops=1e6)
    far = [far[0]] + [shift(far[k], "z", 4, k) for k in (1, 2, 3)]
    *near, counts_near = call(
        pool_near_kernel, [f32(128, 256)] * 4 + [bf16(2, 4, 512, 256)], [SMEM_SPEC] + vmem(2), name="pool_near", flops=1e6
    )(idx, bag_here, decayed)
    view = first_weight.reshape(1024, 2, 8, 128).transpose(0, 2, 1, 3).reshape(1024, 16, 128)

    def turn(view, at):
        return pl.pallas_call(
            lambda *refs: turn_kernel(at, *refs),
            in_specs=[any_spec],
            out_specs=vmem(2),
            out_shape=[bf16(2, 1024, 512)] * 2,
            scratch_shapes=[pltpu.VMEM((4, 128, 16, 128), F32), pltpu.SemaphoreType.DMA((4,))],
            compiler_params=pltpu.CompilerParams(vmem_limit_bytes=VMEM_LIMIT),
            cost_estimate=pl.CostEstimate(flops=int(1e6), transcendentals=0, bytes_accessed=1 << 20),
            name="turn_%d" % at,
        )(hbm(view))

    view, _ = lax.optimization_barrier((view, decayed))
    w1ha, w1la = turn(view, 0)
    *far, _, _ = lax.optimization_barrier((*far, near[0], w1ha))
    (fq_far,) = pack(idx, *far)
    x2 = flip(fq_far, "xh", 2, 1)
    near = [near[0]] + [shift(near[k], "z", 4, k) for k in (1, 2, 3)]
    view, _ = lax.optimization_barrier((view, fq_far))
    w1hb, w1lb = turn(view, 1)
    *near, _ = lax.optimization_barrier((*near, w1hb))
    (fq_near,) = pack(idx, *near)
    y1 = flip(fq_near, "core", 2, 1)
    y2 = flip(x2, "core", 2, 1)
    x2b = flip(fq_near, "xh", 2, 1)
    y1b = flip(fq_far, "core", 2, 1)
    y2b = flip(x2b, "core", 2, 1)

    _, lift_weight, press_weight = lax.optimization_barrier((w1hb, lift_weight, press_weight))
    second_view = second_weight.reshape(1024, 2, 2, 128).transpose(0, 2, 1, 3).reshape(1024, 4, 128)
    w2th, w2tl, lift, press, head = call(
        prepare_kernel,
        [bf16(2, 256, 1024)] * 2 + [f32(local, rank), f32(local, rank), f32(1, local)],
        [SMEM_SPEC] + vmem(1) + [any_spec] * 2 + vmem(1),
        [pltpu.SemaphoreType.DMA((2,))],
        name="prepare",
        flops=1e6,
    )(idx, second_view, hbm(lift_weight), hbm(press_weight), head_weight.reshape(32, 128))

    scratch = [pltpu.VMEM((1024, 256), BF16)] * 2
    weights = (w1ha, w1la, w1hb, w1lb, w2th, w2tl, press, lift, head)
    hid_a, x0a, pay = call(
        lambda *refs: forward_kernel((0, 1), True, *refs),
        [f32(2, 1024, 256), f32(512, 256), f32(2 * rank + 8, 128)],
        [SMEM_SPEC] + vmem(13),
        scratch,
        name="forward_a",
        flops=1e6,
    )(idx, fq_near, x2, y1, y2, *weights)

    def later_half(at, t, y2b):
        return call(
            lambda *refs: forward_kernel((t,), False, *refs),
            [f32(1, 1024, 256), f32(256, 256)],
            [SMEM_SPEC] + vmem(13),
            scratch,
            name="forward_b%d" % t,
            flops=4e9,
        )(at, fq_far, x2b, y1b, y2b, *weights)

    view, second_view, pay = lax.optimization_barrier((view, second_view, pay))
    other = flip(pay, TOWER, 8, 2)
    w1qh, w1ql, column = call(
        pick_kernel,
        [bf16(2, 256, 1024)] * 2 + [f32(32, 128)],
        [SMEM_SPEC, any_spec] + vmem(1),
        [pltpu.VMEM((4, 64, 16, 128), F32), pltpu.VMEM((local, 128), F32), pltpu.SemaphoreType.DMA((4,))],
        name="pick",
        flops=1e6,
    )(idx, hbm(view), head)
    w2h, w2l = call(natural_kernel, [bf16(2, 1024, 256)] * 2, vmem(1), name="natural", flops=1e6)(second_view)
    other, w1qh, w2h, x2b = lax.optimization_barrier((other, w1qh, w2h, x2b))
    pay = pay + other
    after, pay = lax.optimization_barrier((idx, pay))
    other = flip(pay, TOWER, 8, 6)
    y2b = flip(x2b, "core", 2, 1)
    hid_b0, x0b0 = later_half(after, 0, y2b)
    other, x0b0 = lax.optimization_barrier((other, x0b0))
    pay = pay + other
    after, pay = lax.optimization_barrier((idx, pay))
    other = flip(pay, TOWER, 8, 1)
    hid_b1, x0b1 = later_half(after, 1, y2b)
    other, x0b1 = lax.optimization_barrier((other, x0b1))
    pay, logits = call(logit_kernel, [f32(2 * rank + 8, 128), f32(1, 16)], [SMEM_SPEC] + vmem(3), name="logit", flops=1e6)(
        idx, pay, other, labels
    )
    c1 = flip(pay, "core", 2, 1)
    xa = flip(pay, "xh", 2, 1)

    def grads(towers, with_pq, mine, other, hidden, name, flops, extra=()):
        n = len(towers)
        return call(
            lambda *refs: grads_kernel(towers, with_pq, len(extra), *refs),
            [bf16(n, 1024, 256)] * 2 + [f32(n, 256, 256)] + [f32(n, 64, 256)] * 4 + [f32(2 * rank, 256)] * with_pq,
            [SMEM_SPEC] + vmem(10 + len(extra)),
            name=name,
            flops=flops,
        )(idx, mine, other, hidden, w1qh, w1ql, w2h, w2l, press, lift, head, *extra)

    ghha, ghla, gouta, *ga, pqa = grads((0, 1), True, pay, c1, hid_a, "grads_a", 4e9)

    gone = [shift(ga[k], "z", 4, k) for k in (1, 2, 3)]
    xa, pqa = lax.optimization_barrier((xa, pqa))
    xb = flip(xa, "core", 2, 1)

    def weights_of(t, riders, rows, ghhb, ghlb, goutb, hid_b, extra):
        return call(
            lambda *refs: weights_kernel(t, riders, *refs),
            [f32(n, 1024) for n in rows],
            [SMEM_SPEC] + vmem(10 + len(extra)),
            name="weights_%d" % t,
            flops=3e9,
        )(idx, fq_near, fq_far, ghha, ghla, ghhb, ghlb, gouta, goutb, hid_a, hid_b, *extra)

    ghh0, ghl0, gout0, *gb0, pqb = grads((0,), True, xa, xb, hid_b0, "grads_b0", 4e9)
    w = weights_of(0, (2, 3), (80, 80, 96, 96), ghh0, ghl0, gout0, hid_b0, (gb0[1], gb0[3]))
    up = shift(w[2], "z", 4, 1)
    w3 = shift(w[3], "z", 4, 3)
    ghh1, ghl1, gout1, *gb1 = grads((1,), False, xa, xb, hid_b1, "grads_b1", 4e9, gone)
    v = weights_of(
        1,
        (1, 2),
        (88, 104, 104, 88, 32),
        ghh1,
        ghl1,
        gout1,
        hid_b1,
        (gb1[1], gb1[3], x0a, x0b0, x0b1, pqa, pqb, gb0[2], gb1[2]),
    )
    down = shift(v[2], "z", 4, 3)
    v1 = shift(v[1], "z", 4, 1)
    g2 = shift(v[4], "z", 4, 2)
    up, w3 = lax.optimization_barrier((up, w3))
    down, v1 = lax.optimization_barrier((down, v1))
    w1 = shift(w[1] + up[0:80], "z", 4, 1)
    v3 = shift(v[3] + down[0:88], "z", 4, 3)
    new_tables, new_accumulator = call(
        update_kernel, [f32(2, 64, 512), f32(2, 512)], [SMEM_SPEC] + vmem(15), name="update", flops=5e9
    )(idx, ga[0], *gone, gb0[0], gb1[0], up, w3, v1, down, g2, counts_near, counts_far, decayed, accumulator[:, 0])
    first, second, lift_out, press_out = call(
        sum_kernel,
        [f32(1024, 128), f32(256, 128), f32(32, rank), f32(32, rank)],
        vmem(7),
        name="sum",
        flops=1e6,
    )(column, w[0], w1, w3, v[0], v1, v3)
    return (
        jnp.transpose(new_tables, (0, 2, 1))[:, None],
        new_accumulator[:, None],
        first.reshape(64, 8, 2, 128).transpose(0, 2, 1, 3).reshape(64, 2, 1024),
        second.reshape(64, 2, 2, 128).transpose(0, 2, 1, 3).reshape(64, 2, 256),
        lift_out,
        press_out,
        logits,
    )


def solution(mesh):
    split = Mesh(mesh.devices.reshape(4, 2, 4, 2, 2), ("y", "xl", "z", "xh", "core"))
    member = ("z", "xh", "core")
    placed = (
        P(TOWER, member, None, None),
        P(TOWER, member, None),
        P(TOWER, member, None),
        P(TOWER, member, None, None),
        P(TOWER, member, None),
        P(None, TOWER, None),
        P(None, TOWER, None),
        P(),
        P(),
        P(),
        P(member, None),
    )
    return jax.shard_map(
        per_device,
        mesh=split,
        in_specs=placed,
        out_specs=(
            P(TOWER, member, None, None),
            P(TOWER, member, None),
            P(member, TOWER, None),
            P(member, TOWER, None),
            P(TOWER + member, None),
            P(TOWER + member, None),
            P(member, TOWER),
        ),
        check_vma=False,
    )
```

```python
import math

import jax
import jax.numpy as jnp
from jax import lax
from jax.experimental import pallas as pl
from jax.experimental.pallas import tpu as pltpu
from jax.sharding import Mesh, PartitionSpec as P

DECAY_RATE = 0.98
LEARN_RATE = 1.0
EPSILON = 1e-08
F32 = jnp.float32
BF16 = jnp.bfloat16
NN = (((1,), (0,)), ((), ()))
NT = (((1,), (1,)), ((), ()))
TOWER = ("y", "xl")
QUAD = ("xh", "core")
VMEM_LIMIT = 16 << 20
PIECE = 256


def halves(a):
    high = a.astype(BF16)
    return high, (a - high.astype(F32)).astype(BF16)


def dot1(a, b, dims):
    return lax.dot_general(a, b, dims, preferred_element_type=F32)


def dot3(a, b, dims=NN):
    return dot1(a[0], b[0], dims) + (dot1(a[0], b[1], dims) + dot1(a[1], b[0], dims))


def dot32(a, b, dims=NN):
    return dot3(halves(a), halves(b), dims)


def vmem(count):
    return [pl.BlockSpec(memory_space=pltpu.VMEM)] * count


def call(kernel, outs, spec_in, scratch=(), name=None, flops=0):
    return pl.pallas_call(
        kernel,
        cost_estimate=pl.CostEstimate(flops=int(flops), transcendentals=0, bytes_accessed=1 << 20),
        out_shape=outs,
        in_specs=spec_in,
        out_specs=vmem(len(outs)),
        scratch_shapes=list(scratch),
        compiler_params=pltpu.CompilerParams(vmem_limit_bytes=VMEM_LIMIT),
        name=name,
    )


SMEM_SPEC = pl.BlockSpec(memory_space=pltpu.SMEM)


def decay(touch, elapsed, tables, decayed):
    towers, width, rows = tables.shape
    touches = touch.shape[1]
    for t in range(towers):
        ids = jnp.broadcast_to(touch[t : t + 1, :].astype(F32), (touches, touches)).T
        rates = jnp.exp(elapsed[t : t + 1, :].astype(F32) * math.log(DECAY_RATE))
        rates = jnp.broadcast_to(rates, (touches, touches)).T
        factor = []
        for block in range(rows // touches):
            row = lax.broadcasted_iota(jnp.int32, (touches, touches), 1).astype(F32) + float(block * touches)
            match = ids == row
            hits = jnp.sum(jnp.where(match, 1.0, 0.0), axis=0, keepdims=True)
            chosen = jnp.sum(jnp.where(match, rates, 0.0), axis=0, keepdims=True)
            factor.append(jnp.where(hits > 0.0, chosen, 1.0))
        decayed[t] = tables[t] * jnp.concatenate(factor, axis=1)


def pool_half(idx, side, bag, decayed, pooled, counts):
    towers, width, rows = decayed.shape
    part = pooled[0].shape[1]
    for t in range(towers):
        both = jnp.concatenate(halves(decayed[t]), axis=0)
        for k, out in enumerate(pooled):
            chunk = lax.rem(idx[0] + k, 4)
            at = pl.multiple_of(chunk * 2 * part + side * part, part)
            ids = bag[t, :, pl.ds(at, part)]
            row = lax.broadcasted_iota(jnp.int32, (rows, part), 0)
            count = jnp.zeros((rows, part), F32)
            for b in range(ids.shape[0]):
                count = count + jnp.where(row == ids[b : b + 1, :], 1.0, 0.0)
            count = count.astype(BF16)
            counts[t, chunk] = count
            total = dot1(both, count, NN)
            out[t * width : (t + 1) * width, :] = total[:width] + total[width:]


def pool_far_kernel(idx, bag_hbm, touch_hbm, elapsed_hbm, tables_hbm, p0, p1, p2, p3, counts, decayed, bag, touch, elapsed, tables, sems):
    pairs = ((bag_hbm, bag), (touch_hbm, touch), (elapsed_hbm, elapsed), (tables_hbm, tables))
    copies = [pltpu.make_async_copy(a, b, sems.at[n]) for n, (a, b) in enumerate(pairs)]
    for copy in copies:
        copy.start()
    for copy in copies:
        copy.wait()
    decay(touch, elapsed, tables, decayed)
    pool_half(idx, 1 - idx[1], bag, decayed, (p0, p1, p2, p3), counts)


def pool_near_kernel(idx, bag, decayed, p0, p1, p2, p3, counts):
    pool_half(idx, idx[1], bag, decayed, (p0, p1, p2, p3), counts)


def pack_kernel(idx, p0, p1, p2, p3, out):
    for k, ref in enumerate((p0, p1, p2, p3)):
        out[lax.rem(idx[0] + 4 - k, 4)] = ref[...]


def turn_kernel(at, w_hbm, high, low, w, sems):
    pieces, rows = w.shape[:2]
    copies = [pltpu.make_async_copy(w_hbm.at[pl.ds((at * pieces + n) * rows, rows)], w.at[n], sems.at[n]) for n in range(pieces)]
    for copy in copies:
        copy.start()
    for n, copy in enumerate(copies):
        copy.wait()
        flat = w.at[n].reshape(rows * 16, 128)
        for t in range(2):
            for b in range(8):
                h, l = halves(flat[pl.ds(b * 2 + t, rows, stride=16), :].T)
                high[t, b * 128 : (b + 1) * 128, n * rows : (n + 1) * rows] = h
                low[t, b * 128 : (b + 1) * 128, n * rows : (n + 1) * rows] = l


def pick_kernel(idx, w_hbm, head, high, low, column, w, wide, sems):
    rows = w.shape[1]
    quad = 2 * idx[1] + idx[2]
    copies = []
    for k in range(4):
        table = lax.rem(idx[0] + k, 4) * 4 + quad
        copies.append(pltpu.make_async_copy(w_hbm.at[pl.ds(pl.multiple_of(table * rows, rows), rows)], w.at[k], sems.at[k]))
    for copy in copies:
        copy.start()
    wide[...] = jnp.broadcast_to(head[...], (128, head.shape[1])).T
    device = (idx[0] * 2 + idx[1]) * 2 + idx[2]
    column[...] = wide[pl.ds(pl.multiple_of(device * 32, 32), 32), :]
    for k, copy in enumerate(copies):
        copy.wait()
        flat = w.at[k].reshape(rows * 16, 128)
        for t in range(2):
            for b in range(8):
                h, l = halves(flat[pl.ds(b * 2 + t, rows, stride=16), :])
                high[t, k * rows : (k + 1) * rows, b * 128 : (b + 1) * 128] = h
                low[t, k * rows : (k + 1) * rows, b * 128 : (b + 1) * 128] = l


def prepare_kernel(idx, second, lift_hbm, press_hbm, heads, high_t, low_t, lift, press, head, sems):
    tower = idx[3]
    rows = pl.ds(pl.multiple_of(tower * lift.shape[0], lift.shape[0]), lift.shape[0])
    pairs = ((lift_hbm.at[rows, :], lift), (press_hbm.at[rows, :], press))
    copies = [pltpu.make_async_copy(a, b, sems.at[n]) for n, (a, b) in enumerate(pairs)]
    for copy in copies:
        copy.start()
    head[...] = jnp.concatenate([heads[pl.ds(tower * 4 + b, 1), :] for b in range(4)], axis=1)
    count = second.shape[0]
    flat = second.reshape(count * 4, 128)
    for t in range(2):
        for b in range(2):
            lanes = slice(b * 128, (b + 1) * 128)
            h, l = halves(flat[pl.ds(b * 2 + t, count, stride=4), :].T)
            high_t[t, lanes, :] = h
            low_t[t, lanes, :] = l
    for copy in copies:
        copy.wait()


def natural_kernel(w, high, low):
    rows = w.shape[0]
    flat = w.reshape(rows * 4, 128)
    for t in range(2):
        for b in range(2):
            lanes = slice(b * 128, (b + 1) * 128)
            h, l = halves(flat[pl.ds(b * 2 + t, rows, stride=4), :])
            high[t, :, lanes] = h
            low[t, :, lanes] = l


def forward_kernel(towers, with_pay, idx, x1, x2, y1, y2, w1ha, w1la, w1hb, w1lb, w2h, w2l, press, lift, head, hidden, start, *rest):
    fh, fl = rest[-2:]
    sets = (x1, x2, y1, y2)
    zs, pair, samples = x1.shape
    width = pair // 2
    xh, core = idx[1], idx[2]
    place = ((xh, core), (1 - xh, core), (xh, 1 - core), (1 - xh, 1 - core))
    width_out = w2h.shape[1]

    def one_tower(t, slot):
        for (a, b), ref in zip(place, sets):
            for z in range(zs):
                h, l = halves(ref[z, pl.ds(pl.multiple_of(t * width, width), width), :])
                at = pl.multiple_of(((z * 2 + a) * 2 + b) * width, width)
                fh[pl.ds(at, width), :] = h
                fl[pl.ds(at, width), :] = l
        deep = w1ha.shape[2]
        value = dot3((w1ha[t], w1la[t]), (fh[0:deep, :], fl[0:deep, :]))
        value = value + dot3((w1hb[t], w1lb[t]), (fh[deep:, :], fl[deep:, :]))
        hidden[slot] = value
        act = halves(value * jax.nn.sigmoid(value))
        start[pl.ds(pl.multiple_of(slot * width_out, width_out), width_out), :] = dot3((w2h[t], w2l[t]), act)

    if len(towers) == 2:

        def step(t, carry):
            one_tower(t, t)
            return carry

        lax.fori_loop(0, 2, step, 0)
    else:
        one_tower(towers[0], 0)
    if with_pay:
        pay = rest[0]
        own = samples // 2
        rank = press.shape[1]
        x0 = halves(start[:, pl.ds(pl.multiple_of(core * own, own), own)])
        p = dot3(halves(press[...].T), x0)
        q = dot3(halves(lift[...].T * head[...]), x0)
        d = dot3(halves(jnp.broadcast_to(head[...], (8, head.shape[1]))), x0)
        pay[0:rank, :] = p
        pay[rank : 2 * rank, :] = q
        pay[2 * rank : 2 * rank + 8, :] = d


def logit_kernel(idx, mine, other, labels, pay, logits):
    total = mine[...] + other[...]
    rank = (total.shape[0] - 8) // 2
    value = jnp.sum(total[0:rank] * total[rank : 2 * rank], axis=0, keepdims=True) + total[2 * rank : 2 * rank + 1]
    turned = pltpu.roll(jnp.broadcast_to(value, (8, 128)), lax.rem(128 - 16 * idx[3], 128), 1)
    logits[...] = turned[0:1, 0:16]
    error = jax.nn.sigmoid(value) - labels[...].astype(F32)
    pay[0 : 2 * rank, :] = total[0 : 2 * rank]
    pay[2 * rank : 2 * rank + 8, :] = jnp.broadcast_to(error, (8, error.shape[1]))


def grads_kernel(towers, with_pq, extra, idx, mine, other, hidden, w1h, w1l, w2h, w2l, press, lift, head, *refs):
    ghh, ghl, gout, g0, g1, g2, g3, *pq = refs[extra:]
    rank = press.shape[1]
    width = w1h.shape[1] // 4
    width_out = w2h.shape[2]
    first_core = idx[2] == 0
    left = jnp.where(first_core, mine[...], other[...])
    right = jnp.where(first_core, other[...], mine[...])
    both = jnp.concatenate([left, right], axis=1)
    error = both[2 * rank : 2 * rank + 1]
    if with_pq:
        pq[0][...] = error * both[0 : 2 * rank]
    p, q = halves(both[0:rank]), halves(both[rank : 2 * rank])
    column = jnp.broadcast_to(head[...], (128, head.shape[1])).T[:, 0:1]
    for slot, t in enumerate(towers):
        rows = slice(t * width_out, (t + 1) * width_out)
        scaling = dot3(halves(lift[rows, :]), p)
        back = dot3(halves(press[rows, :]), q)
        go = error * (column[rows] * (scaling + 1.0) + back)
        gout[slot] = go
        go = halves(go)
        grad = None
        for n in range(w2h.shape[1] // PIECE):
            part = slice(n * PIECE, (n + 1) * PIECE)
            ga = dot3((w2h[t, part, :], w2l[t, part, :]), go)
            value = hidden[slot, part, :]
            s = jax.nn.sigmoid(value)
            gh = halves(ga * (s * (1.0 + value * (1.0 - s))))
            ghh[slot, part, :] = gh[0]
            ghl[slot, part, :] = gh[1]
            out = dot3((w1h[t, :, part], w1l[t, :, part]), gh)
            grad = out if grad is None else grad + out
        for k, out in enumerate((g0, g1, g2, g3)):
            out[slot] = grad[k * width : (k + 1) * width]


def weights_kernel(t, riders, idx, near, far, ghha, ghla, ghhb, ghlb, gouta, goutb, hid_a, hid_b, *rest):
    if t == 1:
        rest, far_block = rest[:-1], rest[-1]
    blocks, rest = rest[-4:], rest[:-4]
    z, quad = idx[0], 2 * idx[1] + idx[2]
    width = near.shape[1] // 2
    rows = slice(t * width, (t + 1) * width)
    fa, fb, acta, actb = [], [], [], []
    for k in range(4):
        at = lax.rem(z + k, 4)
        fa.append(near[at, rows, :])
        fb.append(far[at, rows, :])
        pick = pl.ds(pl.multiple_of((at * 4 + quad) * width, width), width)
        value = hid_a[t, pick, :]
        acta.append(value * jax.nn.sigmoid(value))
        value = hid_b[0, pick, :]
        actb.append(value * jax.nn.sigmoid(value))
    join = lambda parts: halves(jnp.concatenate(parts, axis=0))
    grad = dot3(join(fa), (ghha[t], ghla[t]), NT) + dot3(join(fb), (ghhb[0], ghlb[0]), NT)
    for k in range(4):
        blocks[k][0:width, :] = grad[k * width : (k + 1) * width]
    grad = dot3(join(acta), halves(gouta[t]), NT) + dot3(join(actb), halves(goutb[0]), NT)
    for k in range(4):
        for b in range(4):
            blocks[k][width : width + 16, b * 256 : (b + 1) * 256] = grad[k * width + 16 * b : k * width + 16 * b + 16]
    low = width // 4
    for n, k in enumerate(riders):
        base = blocks[k].shape[0] - low
        for b in range(4):
            blocks[k][base:, b * 256 : (b + 1) * 256] = rest[n][0, b * low : (b + 1) * low, :]
    if t == 1:
        x0a, x0b0, x0b1, pqa, pqb, gb0, gb1 = rest[2:]
        for n, gb in enumerate((gb0, gb1)):
            for b in range(4):
                far_block[n * low : (n + 1) * low, b * 256 : (b + 1) * 256] = gb[0, b * low : (b + 1) * low, :]
        parts_a, parts_b = [], []
        for k in range(4):
            block = lax.rem(z + k, 4) * 4 + quad
            parts_a.append(x0a[pl.ds(pl.multiple_of(block * 32, 32), 32), :])
            inner = pl.ds(pl.multiple_of(lax.rem(block, 8) * 32, 32), 32)
            parts_b.append(jnp.where(block < 8, x0b0[inner, :], x0b1[inner, :]))
        both = dot3(join(parts_a), halves(pqa[...]), NT) + dot3(join(parts_b), halves(pqb[...]), NT)
        for k in range(4):
            for b in range(4):
                blocks[k][width + 16 : width + 24, b * 256 : (b + 1) * 256] = both[32 * k + 8 * b : 32 * k + 8 * b + 8]


def update_kernel(idx, ga0, ga1, ga2, ga3, gb0, gb1, w_up, w_down, v_up, v_down, opposite, near, far, decayed, accumulator, new_tables, new_accumulator):
    z = idx[0]
    towers, width, rows = decayed.shape
    low = width // 4

    def rider(ref, start=None):
        start = ref.shape[0] - low if start is None else start
        block = ref[start : start + low, :]
        return jnp.concatenate([block[:, b * 256 : (b + 1) * 256] for b in range(4)], axis=0)

    for t in range(towers):
        pieces = (
            (ga0[t], (gb0, gb1)[t][0]),
            (ga1[t], rider((w_up, v_up)[t])),
            (ga2[t], rider(opposite, low * t)),
            (ga3[t], rider((w_down, v_down)[t])),
        )
        total = jnp.zeros((2 * width, rows), F32)
        for k, (a, b) in enumerate(pieces):
            at = lax.rem(z + 4 - k, 4)
            total = total + dot1(jnp.concatenate(halves(a), axis=0), near[t, at], NT)
            total = total + dot1(jnp.concatenate(halves(b), axis=0), far[t, at], NT)
        grad = total[:width] + total[width:]
        square = jnp.sum(grad * grad, axis=0, keepdims=True) * (1.0 / width)
        fresh = accumulator[t : t + 1, :] + square
        new_accumulator[t : t + 1, :] = fresh
        new_tables[t] = decayed[t] - LEARN_RATE * grad / (jnp.sqrt(fresh) + EPSILON)


def sum_kernel(column, *refs):
    parts, (first, second, lift, press) = refs[:6], refs[6:]
    for t in range(2):
        a, b, c = parts[3 * t : 3 * t + 3]
        total = a[...] + (b[0 : a.shape[0]] + c[0 : a.shape[0]])
        for k in range(8):
            first[pl.ds(2 * k + t, 64, stride=16), :] = total[0:64, k * 128 : (k + 1) * 128]
        for b in range(4):
            for o in range(2):
                lanes = slice(b * 256 + o * 128, b * 256 + (o + 1) * 128)
                second[pl.ds(b * 64 + 2 * o + t, 16, stride=4), :] = total[64:80, lanes]
        if t == 1:
            for b in range(4):
                at = slice(8 * b, 8 * b + 8)
                lift[at, :] = column[at] * total[80:88, b * 256 : b * 256 + 128]
                press[at, :] = total[80:88, b * 256 + 128 : (b + 1) * 256]


def shift(x, axis, size, by):
    return lax.ppermute(x, axis, [(i, (i + by) % size) for i in range(size)])


def flip(x, axis, size, bit):
    return lax.ppermute(x, axis, [(i, i ^ bit) for i in range(size)])


def per_device(bag_ids, touch_ids, elapsed, tables, accumulator, first_weight, second_weight, lift_weight, press_weight, head_weight, labels):
    f32 = lambda *shape: jax.ShapeDtypeStruct(shape, F32)
    bf16 = lambda *shape: jax.ShapeDtypeStruct(shape, BF16)
    axes = [lax.axis_index(name) for name in ("z", "xh", "core", TOWER)]
    idx = jnp.stack(axes).astype(jnp.int32)
    rank = lift_weight.shape[1]
    local = lift_weight.shape[0] // 8
    any_spec = pl.BlockSpec(memory_space=pl.ANY)

    tables_t = jnp.transpose(tables[:, 0], (0, 2, 1))
    bag = bag_ids[:, 0]
    hbm = lambda x: pltpu.with_memory_space_constraint(x, pltpu.HBM)
    *far, counts_far, decayed, bag_here = call(
        pool_far_kernel,
        [f32(128, 256)] * 4 + [bf16(2, 4, 512, 256), f32(2, 64, 512), jax.ShapeDtypeStruct((2, 4, 2048), jnp.int32)],
        [SMEM_SPEC] + [any_spec] * 4,
        [
            pltpu.VMEM((2, 128), jnp.int32),
            pltpu.VMEM((2, 128), jnp.int32),
            pltpu.VMEM((2, 64, 512), F32),
            pltpu.SemaphoreType.DMA((4,)),
        ],
        name="pool_far",
        flops=1e6,
    )(idx, hbm(bag), hbm(touch_ids[:, 0]), hbm(elapsed[:, 0]), hbm(tables_t))
    pack = call(pack_kernel, [f32(4, 128, 256)], [SMEM_SPEC] + vmem(4), name="pack", flops=1e6)
    far = [far[0]] + [shift(far[k], "z", 4, k) for k in (1, 2, 3)]
    *near, counts_near = call(
        pool_near_kernel, [f32(128, 256)] * 4 + [bf16(2, 4, 512, 256)], [SMEM_SPEC] + vmem(2), name="pool_near", flops=1e6
    )(idx, bag_here, decayed)
    view = first_weight.reshape(1024, 2, 8, 128).transpose(0, 2, 1, 3).reshape(1024, 16, 128)

    def turn(view, at):
        return pl.pallas_call(
            lambda *refs: turn_kernel(at, *refs),
            in_specs=[any_spec],
            out_specs=vmem(2),
            out_shape=[bf16(2, 1024, 512)] * 2,
            scratch_shapes=[pltpu.VMEM((4, 128, 16, 128), F32), pltpu.SemaphoreType.DMA((4,))],
            compiler_params=pltpu.CompilerParams(vmem_limit_bytes=VMEM_LIMIT),
            cost_estimate=pl.CostEstimate(flops=int(1e6), transcendentals=0, bytes_accessed=1 << 20),
            name="turn_%d" % at,
        )(hbm(view))

    view, _ = lax.optimization_barrier((view, decayed))
    w1ha, w1la = turn(view, 0)
    *far, _, _ = lax.optimization_barrier((*far, near[0], w1ha))
    (fq_far,) = pack(idx, *far)
    x2 = flip(fq_far, "xh", 2, 1)
    near = [near[0]] + [shift(near[k], "z", 4, k) for k in (1, 2, 3)]
    view, _ = lax.optimization_barrier((view, fq_far))
    w1hb, w1lb = turn(view, 1)
    _, lift_weight, press_weight = lax.optimization_barrier((w1hb, lift_weight, press_weight))
    second_view = second_weight.reshape(1024, 2, 2, 128).transpose(0, 2, 1, 3).reshape(1024, 4, 128)
    w2th, w2tl, lift, press, head = call(
        prepare_kernel,
        [bf16(2, 256, 1024)] * 2 + [f32(local, rank), f32(local, rank), f32(1, local)],
        [SMEM_SPEC] + vmem(1) + [any_spec] * 2 + vmem(1),
        [pltpu.SemaphoreType.DMA((2,))],
        name="prepare",
        flops=1e6,
    )(idx, second_view, hbm(lift_weight), hbm(press_weight), head_weight.reshape(32, 128))

    *near, _, _ = lax.optimization_barrier((*near, w1hb, w2th))
    (fq_near,) = pack(idx, *near)
    y1 = flip(fq_near, "core", 2, 1)
    y2 = flip(x2, "core", 2, 1)
    x2b = flip(fq_near, "xh", 2, 1)
    y1b = flip(fq_far, "core", 2, 1)
    y2b = flip(x2b, "core", 2, 1)

    scratch = [pltpu.VMEM((1024, 256), BF16)] * 2
    weights = (w1ha, w1la, w1hb, w1lb, w2th, w2tl, press, lift, head)
    hid_a, x0a, pay = call(
        lambda *refs: forward_kernel((0, 1), True, *refs),
        [f32(2, 1024, 256), f32(512, 256), f32(2 * rank + 8, 128)],
        [SMEM_SPEC] + vmem(13),
        scratch,
        name="forward_a",
        flops=1e6,
    )(idx, fq_near, x2, y1, y2, *weights)

    def later_half(at, t, y2b):
        return call(
            lambda *refs: forward_kernel((t,), False, *refs),
            [f32(1, 1024, 256), f32(256, 256)],
            [SMEM_SPEC] + vmem(13),
            scratch,
            name="forward_b%d" % t,
            flops=4e9,
        )(at, fq_far, x2b, y1b, y2b, *weights)

    view, second_view, pay = lax.optimization_barrier((view, second_view, pay))
    other = flip(pay, TOWER, 8, 2)
    w1qh, w1ql, column = call(
        pick_kernel,
        [bf16(2, 256, 1024)] * 2 + [f32(32, 128)],
        [SMEM_SPEC, any_spec] + vmem(1),
        [pltpu.VMEM((4, 64, 16, 128), F32), pltpu.VMEM((local, 128), F32), pltpu.SemaphoreType.DMA((4,))],
        name="pick",
        flops=1e6,
    )(idx, hbm(view), head)
    w2h, w2l = call(natural_kernel, [bf16(2, 1024, 256)] * 2, vmem(1), name="natural", flops=1e6)(second_view)
    other, w1qh, w2h, x2b = lax.optimization_barrier((other, w1qh, w2h, x2b))
    pay = pay + other
    after, pay = lax.optimization_barrier((idx, pay))
    other = flip(pay, TOWER, 8, 6)
    y2b = flip(x2b, "core", 2, 1)
    hid_b0, x0b0 = later_half(after, 0, y2b)
    other, x0b0 = lax.optimization_barrier((other, x0b0))
    pay = pay + other
    after, pay = lax.optimization_barrier((idx, pay))
    other = flip(pay, TOWER, 8, 1)
    hid_b1, x0b1 = later_half(after, 1, y2b)
    other, x0b1 = lax.optimization_barrier((other, x0b1))
    pay, logits = call(logit_kernel, [f32(2 * rank + 8, 128), f32(1, 16)], [SMEM_SPEC] + vmem(3), name="logit", flops=1e6)(
        idx, pay, other, labels
    )
    c1 = flip(pay, "core", 2, 1)
    xa = flip(pay, "xh", 2, 1)

    def grads(towers, with_pq, mine, other, hidden, name, flops, extra=()):
        n = len(towers)
        return call(
            lambda *refs: grads_kernel(towers, with_pq, len(extra), *refs),
            [bf16(n, 1024, 256)] * 2 + [f32(n, 256, 256)] + [f32(n, 64, 256)] * 4 + [f32(2 * rank, 256)] * with_pq,
            [SMEM_SPEC] + vmem(10 + len(extra)),
            name=name,
            flops=flops,
        )(idx, mine, other, hidden, w1qh, w1ql, w2h, w2l, press, lift, head, *extra)

    ghha, ghla, gouta, *ga, pqa = grads((0, 1), True, pay, c1, hid_a, "grads_a", 4e9)

    gone = [shift(ga[k], "z", 4, k) for k in (1, 2, 3)]
    xa, pqa = lax.optimization_barrier((xa, pqa))
    xb = flip(xa, "core", 2, 1)

    def weights_of(t, riders, rows, ghhb, ghlb, goutb, hid_b, extra):
        return call(
            lambda *refs: weights_kernel(t, riders, *refs),
            [f32(n, 1024) for n in rows],
            [SMEM_SPEC] + vmem(10 + len(extra)),
            name="weights_%d" % t,
            flops=3e9,
        )(idx, fq_near, fq_far, ghha, ghla, ghhb, ghlb, gouta, goutb, hid_a, hid_b, *extra)

    ghh0, ghl0, gout0, *gb0, pqb = grads((0,), True, xa, xb, hid_b0, "grads_b0", 4e9)
    w = weights_of(0, (2, 3), (80, 80, 96, 96), ghh0, ghl0, gout0, hid_b0, (gb0[1], gb0[3]))
    up = shift(w[2], "z", 4, 1)
    w3 = shift(w[3], "z", 4, 3)
    ghh1, ghl1, gout1, *gb1 = grads((1,), False, xa, xb, hid_b1, "grads_b1", 4e9, gone)
    v = weights_of(
        1,
        (1, 2),
        (88, 104, 104, 88, 32),
        ghh1,
        ghl1,
        gout1,
        hid_b1,
        (gb1[1], gb1[3], x0a, x0b0, x0b1, pqa, pqb, gb0[2], gb1[2]),
    )
    down = shift(v[2], "z", 4, 3)
    v1 = shift(v[1], "z", 4, 1)
    g2 = shift(v[4], "z", 4, 2)
    up, w3 = lax.optimization_barrier((up, w3))
    down, v1 = lax.optimization_barrier((down, v1))
    w1 = shift(w[1] + up[0:80], "z", 4, 1)
    v3 = shift(v[3] + down[0:88], "z", 4, 3)
    new_tables, new_accumulator = call(
        update_kernel, [f32(2, 64, 512), f32(2, 512)], [SMEM_SPEC] + vmem(15), name="update", flops=5e9
    )(idx, ga[0], *gone, gb0[0], gb1[0], up, w3, v1, down, g2, counts_near, counts_far, decayed, accumulator[:, 0])
    first, second, lift_out, press_out = call(
        sum_kernel,
        [f32(1024, 128), f32(256, 128), f32(32, rank), f32(32, rank)],
        vmem(7),
        name="sum",
        flops=1e6,
    )(column, w[0], w1, w3, v[0], v1, v3)
    return (
        jnp.transpose(new_tables, (0, 2, 1))[:, None],
        new_accumulator[:, None],
        first.reshape(64, 8, 2, 128).transpose(0, 2, 1, 3).reshape(64, 2, 1024),
        second.reshape(64, 2, 2, 128).transpose(0, 2, 1, 3).reshape(64, 2, 256),
        lift_out,
        press_out,
        logits,
    )


def solution(mesh):
    split = Mesh(mesh.devices.reshape(4, 2, 4, 2, 2), ("y", "xl", "z", "xh", "core"))
    member = ("z", "xh", "core")
    placed = (
        P(TOWER, member, None, None),
        P(TOWER, member, None),
        P(TOWER, member, None),
        P(TOWER, member, None, None),
        P(TOWER, member, None),
        P(None, TOWER, None),
        P(None, TOWER, None),
        P(),
        P(),
        P(),
        P(member, None),
    )
    return jax.shard_map(
        per_device,
        mesh=split,
        in_specs=placed,
        out_specs=(
            P(TOWER, member, None, None),
            P(TOWER, member, None),
            P(member, TOWER, None),
            P(member, TOWER, None),
            P(TOWER + member, None),
            P(TOWER + member, None),
            P(member, TOWER),
        ),
        check_vma=False,
    )
```
